32 devices in a mesh: brick: 8 (over z, x), group: 4 (over y, core).
Axes of the slice: x: 2, y: 2, z: 4, core: 2. Of those that a mesh axis runs over, the one named last changes fastest.
Arguments:
- features: bfloat16 [32768, 96], P(('brick', 'group')), may hold values from -6 to 6
- order: int32 [32768], P(('brick', 'group')), may hold values from 0 to 1023, as said below
- face_list: int32 [8192], P(('brick', 'group')), may hold values from 0 to 1023, as said below
- face_count: int32 [64], P(('brick', 'group')), may hold values from 32 to 128, as said below
- kernel_map: int32 [27, 32768], P(None, ('brick', 'group')), may hold values from 0 to 1280, as said below
- weight: bfloat16 [27, 96, 256], replicated, may hold values from -0.15625 to 0.15625
- bias: float32 [256], replicated, may hold values from -3 to 3
- cotangent: bfloat16 [32768, 256], P(('brick', 'group')), may hold values from -6 to 6
Outputs:
- output: bfloat16 [32768, 256], P(('brick', 'group'))
- grad_in: bfloat16 [32768, 96], P(('brick', 'group'))
- weight_grad: float32 [27, 96, 256], replicated
The draws below stay inside these ranges and needn't reach their ends.
Inputs may be any that keep to these rules, and one draw needn't show every extreme that they name: `order`: each device's 1024 entries are a permutation of 0 .. 1023. `face_list`: rows of the device's own brick. `face_count`: some list is full in every draw. `kernel_map`: the value 1024 + 2 * 128 names the zero row; offset 27 // 2 maps every voxel i to row i.
All inputs are finite; a program needn't handle non-finite values.
Results may differ from the reference program's by a relative error of at most 0.012.
Values may be sent and summed in bfloat16 or wider, within the bound.
No kernel may reach another device: no remote copies, remote signals or barrier semaphores. Data moves between devices by JAX's collectives and lax.ppermute only.
A program may use at most 64 MiB of HBM per device.

```python
import math
import jax
import jax.numpy as jnp
from jax import lax

C_IN = 96
C_OUT = 256
K = 27
VOX_DEV = 1024
FACE = 128
VOXELS = 32768
FACE_ALL = 8192
COUNT_ALL = 64
N_BRICK = 8
N_GROUP = 4


def draw_order(key, part):
    blocks = VOXELS // VOX_DEV
    subkeys = jax.random.split(key, blocks)
    perms = jax.vmap(lambda sub: jax.random.permutation(sub, VOX_DEV))(subkeys)
    return perms.reshape(VOXELS).astype(jnp.int32)


def draw_face_list(key, part):
    return jax.random.randint(key, (FACE_ALL,), 0, VOX_DEV).astype(jnp.int32)


def draw_face_count(key, part):
    counts = jax.random.randint(key, (COUNT_ALL,), FACE // 4, FACE + 1)
    where_full = jax.random.randint(jax.random.fold_in(key, 7), (), 0, COUNT_ALL)
    counts = counts.at[where_full].set(FACE)
    return counts.astype(jnp.int32)


def draw_kernel_map(key, part):
    target = jax.random.randint(jax.random.fold_in(key, 1), (K, VOXELS), 0, VOX_DEV + 2 * FACE)
    present = jax.random.randint(jax.random.fold_in(key, 2), (K, VOXELS), 0, 5) < 3
    mapped = jnp.where(present, target, VOX_DEV + 2 * FACE)
    center = jnp.arange(VOXELS) % VOX_DEV
    mapped = mapped.at[K // 2].set(center)
    return mapped.astype(jnp.int32)


def block_scale(rng, shape, cuts, least, largest):
    factor_of = 1.0
    for position, parts in cuts:
        steps = jax.random.uniform(jax.random.fold_in(jax.random.fold_in(rng, 6), position), (parts,), jnp.float32, least / len(cuts), largest / len(cuts))
        factor_of = factor_of * jnp.repeat(jnp.exp(steps), shape[position] // parts).reshape((-1,) + (1,) * (len(shape) - 1 - position))
    return factor_of


def gaussian(own_key, dims, scale, limit, shards=(), held_as=jnp.bfloat16):
    result = scale * jax.random.normal(own_key, dims, jnp.float32)
    if shards:
        result = result * block_scale(own_key, dims, shards, -0.22, 0.18)
    return jnp.clip(result, -limit, limit).astype(held_as)


def setup_inputs(seed: int = 0) -> dict:
    key_list = jax.random.split(jax.random.key(seed), 9)
    return {
        "features": gaussian(key_list[0], (VOXELS, C_IN), 1.0, 6.0, ((0, 32),)),
        "order": draw_order(jax.random.fold_in(key_list[8], 71), 0),
        "face_list": draw_face_list(jax.random.fold_in(key_list[8], 71), 0),
        "face_count": draw_face_count(jax.random.fold_in(key_list[8], 71), 0),
        "kernel_map": draw_kernel_map(jax.random.fold_in(key_list[8], 71), 0),
        "weight": gaussian(key_list[5], (K, C_IN, C_OUT), (K * C_IN // 2) ** -0.5, 0.15625),
        "bias": gaussian(key_list[6], (C_OUT,), 0.5, 3.0, (), jnp.float32),
        "cotangent": gaussian(key_list[7], (VOXELS, C_OUT), 1.0, 6.0, ((0, 32),)),
    }


def regroup(blocks):
    channels = blocks.shape[-1]
    pieces = blocks.reshape(N_BRICK, N_GROUP, N_BRICK, VOX_DEV // N_BRICK, channels)
    return pieces.transpose(2, 1, 0, 3, 4).reshape(N_BRICK, N_GROUP, VOX_DEV, channels)

def block_pass(extended, offset_maps, out_grad, weight, bias):

    def forward(summed, operands):
        map_row, kernel = operands
        return (summed + jnp.dot(extended[map_row], kernel, preferred_element_type=jnp.float32), None)
    start = jnp.zeros((VOX_DEV, C_OUT), jnp.float32)
    pre, _ = lax.scan(forward, start, (offset_maps, weight))
    pre = pre + bias
    output = jnp.maximum(pre, 0.0).astype(jnp.bfloat16)
    pre_grad = jnp.where(pre > 0, out_grad, jnp.zeros_like(out_grad))

    def backward(ext_grad, operands):
        map_row, kernel = operands
        kernel_grad = lax.dot_general(extended[map_row], pre_grad, (((0,), (0,)), ((), ())), preferred_element_type=jnp.float32)
        contrib = lax.dot_general(pre_grad, kernel, (((1,), (1,)), ((), ())), preferred_element_type=jnp.float32)
        return (ext_grad.at[map_row].add(contrib), kernel_grad)
    zeros_grad = jnp.zeros((extended.shape[0], C_IN), jnp.float32)
    ext_grad, kernel_grads = lax.scan(backward, zeros_grad, (offset_maps, weight))
    return (output, ext_grad, kernel_grads)

def reference(features, order, face_list, face_count, kernel_map, weight, bias, cotangent):
    devices_all = N_BRICK * N_GROUP
    scan_rows = features.reshape(N_BRICK, N_GROUP, VOX_DEV, C_IN)
    orders = order.reshape(N_BRICK, N_GROUP, VOX_DEV)
    sent_rows = jnp.take_along_axis(scan_rows, orders[..., None], axis=2)
    local_rows = regroup(sent_rows)
    face_lists = face_list.reshape(N_BRICK, N_GROUP, 2 * FACE)
    counts = face_count.reshape(N_BRICK, N_GROUP, 2)
    slots = jnp.arange(FACE).astype(jnp.int32)
    lower_keep = (slots[None, None, :] < counts[..., 0:1])[..., None]
    upper_keep = (slots[None, None, :] < counts[..., 1:2])[..., None]
    lower_list = face_lists[..., :FACE]
    upper_list = face_lists[..., FACE:]
    lower_rows = jnp.where(lower_keep, jnp.take_along_axis(local_rows, lower_list[..., None], axis=2), jnp.zeros((), jnp.bfloat16))
    upper_rows = jnp.where(upper_keep, jnp.take_along_axis(local_rows, upper_list[..., None], axis=2), jnp.zeros((), jnp.bfloat16))
    empty_rows = jnp.zeros((1, N_GROUP, FACE, C_IN), jnp.bfloat16)
    prev_upper = jnp.concatenate([empty_rows, upper_rows[:-1]], 0)
    next_lower = jnp.concatenate([lower_rows[1:], empty_rows], 0)
    zero_row = jnp.zeros((N_BRICK, N_GROUP, 1, C_IN), jnp.bfloat16)
    extended = jnp.concatenate([local_rows, prev_upper, next_lower, zero_row], 2)
    extended = extended.reshape(devices_all, VOX_DEV + 2 * FACE + 1, C_IN)
    offset_maps = kernel_map.reshape(K, devices_all, VOX_DEV).transpose(1, 0, 2)
    out_grads = cotangent.reshape(devices_all, VOX_DEV, C_OUT)

    def device_step(running, operands):
        ext_rows, dev_maps, grad_rows = operands
        output, ext_grad, kernel_grads = block_pass(ext_rows, dev_maps, grad_rows, weight, bias)
        return (running + kernel_grads, (output, ext_grad))
    start = jnp.zeros((K, C_IN, C_OUT), jnp.float32)
    weight_sum, (results, ext_grads) = lax.scan(device_step, start, (extended, offset_maps, out_grads))
    ext_grads = ext_grads.reshape(N_BRICK, N_GROUP, VOX_DEV + 2 * FACE + 1, C_IN)
    to_prev = ext_grads[:, :, VOX_DEV:VOX_DEV + FACE]
    to_next = ext_grads[:, :, VOX_DEV + FACE:VOX_DEV + 2 * FACE]
    zero_grad = jnp.zeros((1, N_GROUP, FACE, C_IN), jnp.float32)
    from_prev = jnp.concatenate([zero_grad, to_next[:-1]], 0)
    from_next = jnp.concatenate([to_prev[1:], zero_grad], 0)
    from_prev = jnp.where(lower_keep, from_prev, jnp.zeros((), jnp.float32))
    from_next = jnp.where(upper_keep, from_next, jnp.zeros((), jnp.float32))

    def add_faces(base, low_idx, low_vals, up_idx, up_vals):
        return base.at[low_idx].add(low_vals).at[up_idx].add(up_vals)
    local_grad = jax.vmap(add_faces)(ext_grads[:, :, :VOX_DEV].reshape(devices_all, VOX_DEV, C_IN), lower_list.reshape(devices_all, FACE), from_prev.reshape(devices_all, FACE, C_IN), upper_list.reshape(devices_all, FACE), from_next.reshape(devices_all, FACE, C_IN))
    brick_grad = local_grad.astype(jnp.bfloat16).reshape(N_BRICK, N_GROUP, VOX_DEV, C_IN)
    returned = regroup(brick_grad).reshape(devices_all, VOX_DEV, C_IN)

    def place_back(order_row, values):
        return jnp.zeros((VOX_DEV, C_IN), jnp.bfloat16).at[order_row].set(values)
    grad_in = jax.vmap(place_back)(orders.reshape(devices_all, VOX_DEV), returned)
    weight_grad = weight_sum * jnp.float32(1.0 / math.sqrt(VOXELS))
    return (results.reshape(VOXELS, C_OUT), grad_in.reshape(VOXELS, C_IN), weight_grad)
```

```python
import functools
import math

import jax
import jax.numpy as jnp
from jax import lax
from jax.experimental import pallas as pl
from jax.experimental.pallas import tpu as pltpu
from jax.sharding import PartitionSpec as P

BF = jnp.bfloat16
F32 = jnp.float32
LOW = 256
SHIFT = 8
VMEM_LIMIT = 48 << 20
AXES = ("brick", "group")


def dot(a, b, a_dim, b_dim):
    dims = (((a_dim,), (b_dim,)), ((), ()))
    return lax.dot_general(a, b, dims, preferred_element_type=F32)


def one_hot_rows(index, width):
    columns = jnp.arange(width, dtype=jnp.int32)
    return (index[:, None] == columns[None, :]).astype(BF)


def forward_kernel(x_ref, map_ref, wt_ref, bias_ref, cot_ref, out_ref, pg_ref, wg_ref, g_ref):
    offsets, voxels = map_ref.shape
    depth = wt_ref.shape[1]
    channels = depth // offsets
    blocks = x_ref.shape[0] // channels
    lanes = min(256, voxels)
    iota = lax.broadcasted_iota(jnp.int32, (LOW, lanes), 0).astype(BF)

    def offset(k, carry):
        row = map_ref[pl.ds(k, 1), :]
        low = (row & (LOW - 1)).astype(F32).astype(BF)
        high = lax.shift_right_logical(row, SHIFT)
        at = pl.ds(pl.multiple_of(k * channels, channels), channels)
        for n in range(voxels // lanes):
            sl = slice(n * lanes, (n + 1) * lanes)
            hit = iota == jnp.broadcast_to(low[:, sl], (LOW, lanes))
            hot = jnp.where(hit, jnp.ones((), BF), jnp.zeros((), BF))
            block = jnp.broadcast_to(high[:, sl], (channels, lanes))
            picked = jnp.zeros((channels, lanes), F32)
            for a in range(blocks):
                term = dot(x_ref[a * channels : (a + 1) * channels, :], hot, 1, 0)
                picked = jnp.where(block == a, term, picked)
            g_ref[at, sl] = picked.astype(BF)
        return carry

    lax.fori_loop(0, offsets, offset, 0)
    for n in range(voxels // lanes):
        sl = slice(n * lanes, (n + 1) * lanes)
        pre = dot(wt_ref[...], g_ref[:, sl], 1, 0).T + bias_ref[...]
        out_ref[sl, :] = jnp.maximum(pre, 0.0).astype(BF)
        pg_ref[sl, :] = jnp.where(pre > 0, cot_ref[sl, :].astype(F32), 0.0).astype(BF)
    step = depth // 9
    for m in range(9):
        sl = slice(m * step, (m + 1) * step)
        wg_ref[sl, :] = dot(g_ref[sl, :], pg_ref[...], 1, 0).astype(BF)
    wg_ref[depth:, :] = jnp.zeros((wg_ref.shape[0] - depth, wg_ref.shape[1]), BF)


def backward_kernel(pg_ref, map_ref, w_ref, acc_ref, c_ref):
    offsets, voxels = map_ref.shape
    depth = w_ref.shape[0]
    channels = depth // offsets
    blocks = acc_ref.shape[0] // channels
    step = depth // 9
    for m in range(9):
        sl = slice(m * step, (m + 1) * step)
        c_ref[sl, :] = dot(w_ref[sl, :], pg_ref[...], 1, 1).astype(BF)
    acc_ref[...] = jnp.zeros_like(acc_ref)
    iota = lax.broadcasted_iota(jnp.int32, (LOW, voxels), 0).astype(BF)

    def offset(k, carry):
        row = map_ref[pl.ds(k, 1), :]
        low = (row & (LOW - 1)).astype(F32).astype(BF)
        high = lax.shift_right_logical(row, SHIFT).astype(F32).astype(BF)
        hit = iota == jnp.broadcast_to(low, (LOW, voxels))
        hot = jnp.where(hit, jnp.ones((), BF), jnp.zeros((), BF))
        contrib = c_ref[pl.ds(pl.multiple_of(k * channels, channels), channels), :]
        block = jnp.broadcast_to(high, (channels, voxels))
        for a in range(blocks):
            part = jnp.where(block == jnp.array(a, BF), contrib, jnp.zeros((), BF))
            acc_ref[a * channels : (a + 1) * channels, :] += dot(part, hot, 1, 1)
        return carry

    lax.fori_loop(0, offsets, offset, 0)


def whole(count):
    return [pl.BlockSpec(memory_space=pltpu.VMEM)] * count


def forward(x, maps, wt, bias, cot, padded):
    offsets, voxels = maps.shape
    c_out, depth = wt.shape
    macs = voxels * depth * c_out * 2 + offsets * voxels * LOW * x.shape[0]
    return pl.pallas_call(
        forward_kernel,
        out_shape=(
            jax.ShapeDtypeStruct((voxels, c_out), BF),
            jax.ShapeDtypeStruct((voxels, c_out), BF),
            jax.ShapeDtypeStruct((padded, c_out), BF),
        ),
        in_specs=whole(5),
        out_specs=tuple(whole(3)),
        scratch_shapes=[pltpu.VMEM((depth, voxels), BF)],
        compiler_params=pltpu.CompilerParams(vmem_limit_bytes=VMEM_LIMIT),
        cost_estimate=pl.CostEstimate(flops=2 * macs, bytes_accessed=5 << 20, transcendentals=0),
    )(x, maps, wt, bias, cot)


def backward(pg, maps, w, rows):
    offsets, voxels = maps.shape
    depth, c_out = w.shape
    macs = voxels * depth * c_out + offsets * voxels * LOW * rows
    return pl.pallas_call(
        backward_kernel,
        out_shape=jax.ShapeDtypeStruct((rows, LOW), F32),
        in_specs=whole(3),
        out_specs=whole(1)[0],
        scratch_shapes=[pltpu.VMEM((depth, voxels), BF)],
        compiler_params=pltpu.CompilerParams(vmem_limit_bytes=VMEM_LIMIT),
        cost_estimate=pl.CostEstimate(flops=2 * macs, bytes_accessed=4 << 20, transcendentals=0),
    )(pg, maps, w)


def stages(count):
    plan, stride = [], 1
    while stride < count:
        left = count // stride
        radix = 4 if stride > 1 and left % 4 == 0 else 2
        if left % radix:
            radix = left
        plan.append((stride, radix))
        stride *= radix
    return plan


def swapped(array, count, stride, radix, delta):
    def partner(i):
        digit = i // stride % radix
        other = (digit ^ delta) if radix in (2, 4) else (delta - digit) % radix
        return i + (other - digit) * stride

    return lax.ppermute(array, AXES, [(i, partner(i)) for i in range(count)])


def other_digit(digit, delta, radix):
    return (digit ^ delta) if radix in (2, 4) else (delta - digit) % radix


def sum_over_all(x, count):
    flat = lax.axis_index("brick") * lax.axis_size("group") + lax.axis_index("group")
    plan = stages(count)
    for stride, radix in plan:
        digit = flat // stride % radix
        pieces = x.reshape((radix, x.shape[0] // radix) + x.shape[1:])
        got = []
        for delta in range(radix):
            other = other_digit(digit, delta, radix)
            piece = lax.dynamic_index_in_dim(pieces, other, 0, keepdims=False)
            if radix in (2, 4) and delta == 0:
                total = piece.astype(F32)
            else:
                got.append(swapped(piece, count, stride, radix, delta))
        if radix not in (2, 4):
            total = jnp.zeros(got[0].shape, F32)
        for piece in got:
            total = total + piece.astype(F32)
        x = total.astype(BF)
    for stride, radix in reversed(plan):
        digit = flat // stride % radix
        got = [x if radix in (2, 4) and d == 0 else swapped(x, count, stride, radix, d) for d in range(radix)]
        parts = []
        for place in range(radix):
            part = got[other_digit(place, 0, radix)]
            for d in range(1, radix):
                part = jnp.where(digit == d, got[other_digit(place, d, radix) if radix in (2, 4) else (place + d) % radix], part)
            parts.append(part)
        x = jnp.concatenate(parts, 0)
    return x


def meet(array_up, array_down):
    size = lax.axis_size("brick")
    odd = lax.axis_index("brick") % 2 == 1
    got = []
    for start in (0, 1):
        pairs = []
        for i in range(start, size - 1, 2):
            pairs += [(i, i + 1), (i + 1, i)]
        goes_up = ~odd if start == 0 else odd
        got.append(lax.ppermute(jnp.where(goes_up, array_up, array_down), "brick", pairs))
    return jnp.where(odd, got[0], got[1]), jnp.where(odd, got[1], got[0])


def on_device(features, order, face_list, face_count, kernel_map, weight, bias, cotangent):
    offsets, channels, c_out = weight.shape
    rows = features.shape[0]
    face = face_list.shape[0] // 2
    bricks = lax.axis_size("brick")
    count = bricks * lax.axis_size("group")
    per = rows // bricks
    depth = offsets * channels
    unit = 8 * count
    padded = -(-depth // unit) * unit
    blocks = rows // LOW

    w = weight.reshape(depth, c_out)
    wt = w.T
    order_pick = one_hot_rows(order, rows)
    sent = dot(order_pick, features, 1, 0).astype(BF)
    local = lax.all_to_all(sent, "brick", split_axis=0, concat_axis=0, tiled=True)

    slots = jnp.arange(face, dtype=jnp.int32)
    lower_pick = one_hot_rows(face_list[:face], rows) * (slots < face_count[0]).astype(BF)[:, None]
    upper_pick = one_hot_rows(face_list[face:], rows) * (slots < face_count[1]).astype(BF)[:, None]
    lower = dot(local, lower_pick, 0, 1).astype(BF)
    upper = dot(local, upper_pick, 0, 1).astype(BF)
    prev_upper, next_lower = meet(upper, lower)

    x_local = local.reshape(blocks, LOW, channels).transpose(0, 2, 1).reshape(blocks * channels, LOW)
    x = jnp.concatenate([x_local, jnp.concatenate([prev_upper, next_lower], 1)], 0)
    output, pre_grad, kernel_grads = forward(x, kernel_map, wt, bias[None], cotangent, padded)

    weight_sum = sum_over_all(kernel_grads, count)
    scale = jnp.float32(1.0 / math.sqrt(count * rows))
    weight_grad = (weight_sum[:depth].astype(F32) * scale).reshape(offsets, channels, c_out)

    acc = backward(pre_grad, kernel_map, w, x.shape[0])
    faces = acc[blocks * channels :].astype(BF)
    from_prev, from_next = meet(faces[:, face:], faces[:, :face])
    here = acc[: blocks * channels].reshape(blocks, channels, LOW).transpose(0, 2, 1).reshape(rows, channels)
    local_grad = here + dot(lower_pick, from_prev, 0, 1) + dot(upper_pick, from_next, 0, 1)
    returned = lax.all_to_all(local_grad.astype(BF), "brick", split_axis=0, concat_axis=0, tiled=True)
    grad_in = dot(order_pick, returned, 0, 0).astype(BF)
    return output, grad_in, weight_grad


def solution(mesh):
    return jax.shard_map(
        on_device,
        mesh=mesh,
        in_specs=(
            P(AXES, None),
            P(AXES),
            P(AXES),
            P(AXES),
            P(None, AXES),
            P(),
            P(),
            P(AXES, None),
        ),
        out_specs=(P(AXES, None), P(AXES, None), P()),
        check_vma=False,
    )
```

```python
import functools
import math

import jax
import jax.numpy as jnp
from jax import lax
from jax.experimental import pallas as pl
from jax.experimental.pallas import tpu as pltpu
from jax.sharding import PartitionSpec as P

BF = jnp.bfloat16
F32 = jnp.float32
LOW = 256
SHIFT = 8
VMEM_LIMIT = 32 << 20
AXES = ("brick", "group")


def dot(a, b, a_dim, b_dim):
    dims = (((a_dim,), (b_dim,)), ((), ()))
    return lax.dot_general(a, b, dims, preferred_element_type=F32)


def one_hot_rows(index, width):
    columns = jnp.arange(width, dtype=jnp.int32)
    return (index[:, None] == columns[None, :]).astype(BF)


def one_hot_low(row, lanes):
    low = (row & (LOW - 1)).astype(F32).astype(BF)
    iota = lax.broadcasted_iota(jnp.int32, (LOW, lanes), 0).astype(BF)
    hit = iota == jnp.broadcast_to(low, (LOW, lanes))
    return jnp.where(hit, jnp.ones((), BF), jnp.zeros((), BF))


def forward_kernel(local_ref, prev_ref, next_ref, map_ref, w_ref, bias_ref, cot_ref, out_ref, pg_ref, wg_ref, g_ref, x_ref, wt_ref):
    offsets, voxels = map_ref.shape
    depth, c_out = w_ref.shape
    channels = depth // offsets
    here = voxels // LOW
    blocks = x_ref.shape[0] // channels
    center = offsets // 2
    for a in range(here):
        x_ref[a * channels : (a + 1) * channels, :] = local_ref[a * LOW : (a + 1) * LOW, :].T
    half = prev_ref.shape[1]
    x_ref[here * channels :, :half] = prev_ref[...]
    x_ref[here * channels :, half:] = next_ref[...]
    for k in range(offsets):
        wt_ref[:, k * channels : (k + 1) * channels] = w_ref[k * channels : (k + 1) * channels, :].T
        at = slice(k * channels, (k + 1) * channels)
        if k == center:
            for a in range(here):
                g_ref[at, a * LOW : (a + 1) * LOW] = x_ref[a * channels : (a + 1) * channels, :]
            continue
        row = map_ref[k : k + 1, :]
        high = lax.shift_right_logical(row, SHIFT)
        for n in range(here):
            sl = slice(n * LOW, (n + 1) * LOW)
            terms = dot(x_ref[...], one_hot_low(row[:, sl], LOW), 1, 0)
            block = jnp.broadcast_to(high[:, sl], (channels, LOW))
            picked = jnp.zeros((channels, LOW), F32)
            for a in range(blocks):
                picked = jnp.where(block == a, terms[a * channels : (a + 1) * channels], picked)
            g_ref[at, sl] = picked.astype(BF)
    for n in range(here):
        sl = slice(n * LOW, (n + 1) * LOW)
        pre = dot(wt_ref[...], g_ref[:, sl], 1, 0).T + bias_ref[...]
        out_ref[sl, :] = jnp.maximum(pre, 0.0).astype(BF)
        pg_ref[sl, :] = jnp.where(pre > 0, cot_ref[sl, :].astype(F32), 0.0).astype(BF)
    step = depth // 9
    for m in range(9):
        sl = slice(m * step, (m + 1) * step)
        wg_ref[sl, :] = dot(g_ref[sl, :], pg_ref[...], 1, 0).astype(BF)
    wg_ref[depth:, :] = jnp.zeros((wg_ref.shape[0] - depth, c_out), BF)


def backward_kernel(first, last, pg_ref, map_ref, w_ref, *refs):
    in_ref, acc_ref = refs if len(refs) == 2 else (None, refs[0])
    offsets, voxels = map_ref.shape
    channels = w_ref.shape[0] // offsets
    here = voxels // LOW
    blocks = acc_ref.shape[0] // channels
    acc_ref[...] = jnp.zeros_like(acc_ref) if in_ref is None else in_ref[...]
    for k in range(first, last):
        contrib = dot(w_ref[k * channels : (k + 1) * channels, :], pg_ref[...], 1, 1)
        if k == offsets // 2:
            for a in range(here):
                acc_ref[a * channels : (a + 1) * channels, :] += contrib[:, a * LOW : (a + 1) * LOW]
            continue
        contrib = contrib.astype(BF)
        row = map_ref[k : k + 1, :]
        high = lax.shift_right_logical(row, SHIFT).astype(F32).astype(BF)
        block = jnp.broadcast_to(high, (channels, voxels))
        parts = [jnp.where(block == jnp.array(a, BF), contrib, jnp.zeros((), BF)) for a in range(blocks)]
        acc_ref[...] += dot(jnp.concatenate(parts, 0), one_hot_low(row, voxels), 1, 1)


def whole(count):
    return [pl.BlockSpec(memory_space=pltpu.VMEM)] * count


def forward(local, prev_upper, next_lower, maps, w, bias, cot, padded):
    offsets, voxels = maps.shape
    depth, c_out = w.shape
    rows = depth // offsets * (voxels // LOW + 1)
    macs = voxels * depth * c_out * 2 + offsets * voxels * LOW * rows
    return pl.pallas_call(
        forward_kernel,
        out_shape=(
            jax.ShapeDtypeStruct((voxels, c_out), BF),
            jax.ShapeDtypeStruct((voxels, c_out), BF),
            jax.ShapeDtypeStruct((padded, c_out), BF),
        ),
        in_specs=whole(7),
        out_specs=tuple(whole(3)),
        scratch_shapes=[pltpu.VMEM((depth, voxels), BF), pltpu.VMEM((rows, LOW), BF), pltpu.VMEM((c_out, depth), BF)],
        compiler_params=pltpu.CompilerParams(vmem_limit_bytes=VMEM_LIMIT),
        cost_estimate=pl.CostEstimate(flops=2 * macs, bytes_accessed=5 << 20, transcendentals=0),
    )(local, prev_upper, next_lower, maps, w, bias, cot)


def backward(first, last, pg, maps, w, acc, rows):
    offsets, voxels = maps.shape
    depth, c_out = w.shape
    macs = (voxels * depth * c_out + offsets * voxels * LOW * rows) * (last - first) // offsets
    args = (pg, maps, w) if acc is None else (pg, maps, w, acc)
    return pl.pallas_call(
        functools.partial(backward_kernel, first, last),
        out_shape=jax.ShapeDtypeStruct((rows, LOW), F32),
        in_specs=whole(len(args)),
        out_specs=whole(1)[0],
        compiler_params=pltpu.CompilerParams(vmem_limit_bytes=VMEM_LIMIT),
        cost_estimate=pl.CostEstimate(flops=2 * macs, bytes_accessed=3 << 20, transcendentals=0),
    )(*args)


def stages(count):
    plan, stride = [], 1
    while stride < count:
        left = count // stride
        radix = 4 if stride > 1 and left % 4 == 0 else 2
        if left % radix:
            radix = left
        plan.append((stride, radix))
        stride *= radix
    return plan


def swapped(array, count, stride, radix, delta):
    def partner(i):
        digit = i // stride % radix
        other = (digit ^ delta) if radix in (2, 4) else (delta - digit) % radix
        return i + (other - digit) * stride

    return lax.ppermute(array, AXES, [(i, partner(i)) for i in range(count)])


def other_digit(digit, delta, radix):
    return (digit ^ delta) if radix in (2, 4) else (delta - digit) % radix


def sum_over_all(x, count):
    flat = lax.axis_index("brick") * lax.axis_size("group") + lax.axis_index("group")
    plan = stages(count)
    for stride, radix in plan:
        digit = flat // stride % radix
        pieces = x.reshape((radix, x.shape[0] // radix) + x.shape[1:])
        got = []
        for delta in range(radix):
            other = other_digit(digit, delta, radix)
            piece = lax.dynamic_index_in_dim(pieces, other, 0, keepdims=False)
            if radix in (2, 4) and delta == 0:
                total = piece.astype(F32)
            else:
                got.append(swapped(piece, count, stride, radix, delta))
        if radix not in (2, 4):
            total = jnp.zeros(got[0].shape, F32)
        for piece in got:
            total = total + piece.astype(F32)
        x = total.astype(BF)
    for stride, radix in reversed(plan):
        digit = flat // stride % radix
        got = [x if radix in (2, 4) and d == 0 else swapped(x, count, stride, radix, d) for d in range(radix)]
        parts = []
        for place in range(radix):
            part = got[other_digit(place, 0, radix)]
            for d in range(1, radix):
                part = jnp.where(digit == d, got[other_digit(place, d, radix) if radix in (2, 4) else (place + d) % radix], part)
            parts.append(part)
        x = jnp.concatenate(parts, 0)
    return x


def meet(array_up, array_down):
    size = lax.axis_size("brick")
    odd = lax.axis_index("brick") % 2 == 1
    got = []
    for start in (0, 1):
        pairs = []
        for i in range(start, size - 1, 2):
            pairs += [(i, i + 1), (i + 1, i)]
        goes_up = ~odd if start == 0 else odd
        got.append(lax.ppermute(jnp.where(goes_up, array_up, array_down), "brick", pairs))
    return jnp.where(odd, got[0], got[1]), jnp.where(odd, got[1], got[0])


def on_device(features, order, face_list, face_count, kernel_map, weight, bias, cotangent):
    offsets, channels, c_out = weight.shape
    rows = features.shape[0]
    face = face_list.shape[0] // 2
    bricks = lax.axis_size("brick")
    count = bricks * lax.axis_size("group")
    per = rows // bricks
    depth = offsets * channels
    unit = 8 * count
    padded = -(-depth // unit) * unit
    blocks = rows // LOW

    w = weight.reshape(depth, c_out)
    order_pick = one_hot_rows(order, rows)
    sent = dot(order_pick, features, 1, 0).astype(BF)
    local = lax.all_to_all(sent, "brick", split_axis=0, concat_axis=0, tiled=True)

    slots = jnp.arange(face, dtype=jnp.int32)
    lower_pick = one_hot_rows(face_list[:face], rows) * (slots < face_count[0]).astype(BF)[:, None]
    upper_pick = one_hot_rows(face_list[face:], rows) * (slots < face_count[1]).astype(BF)[:, None]
    lower = dot(local, lower_pick, 0, 1).astype(BF)
    upper = dot(local, upper_pick, 0, 1).astype(BF)
    prev_upper, next_lower = meet(upper, lower)

    output, pre_grad, kernel_grads = forward(
        local, prev_upper, next_lower, kernel_map, w, bias[None], cotangent, padded
    )

    weight_sum = sum_over_all(kernel_grads, count)
    scale = jnp.float32(1.0 / math.sqrt(count * rows))
    weight_grad = (weight_sum[:depth].astype(F32) * scale).reshape(offsets, channels, c_out)

    acc = None
    for first, last in ((0, offsets // 3), (offsets // 3, 2 * offsets // 3), (2 * offsets // 3, offsets)):
        acc = backward(first, last, pre_grad, kernel_map, w, acc, (blocks + 1) * channels)
    faces = acc[blocks * channels :].astype(BF)
    from_prev, from_next = meet(faces[:, face:], faces[:, :face])
    here = acc[: blocks * channels].reshape(blocks, channels, LOW).transpose(0, 2, 1).reshape(rows, channels)
    local_grad = here + dot(lower_pick, from_prev, 0, 1) + dot(upper_pick, from_next, 0, 1)
    returned = lax.all_to_all(local_grad.astype(BF), "brick", split_axis=0, concat_axis=0, tiled=True)
    grad_in = dot(order_pick, returned, 0, 0).astype(BF)
    return output, grad_in, weight_grad


def solution(mesh):
    return jax.shard_map(
        on_device,
        mesh=mesh,
        in_specs=(
            P(AXES, None),
            P(AXES),
            P(AXES),
            P(AXES),
            P(None, AXES),
            P(),
            P(),
            P(AXES, None),
        ),
        out_specs=(P(AXES, None), P(AXES, None), P()),
        check_vma=False,
    )
```

```python
import functools
import math

import jax
import jax.numpy as jnp
from jax import lax
from jax.experimental import pallas as pl
from jax.experimental.pallas import tpu as pltpu
from jax.sharding import PartitionSpec as P

BF = jnp.bfloat16
F32 = jnp.float32
LOW = 256
SHIFT = 8
VMEM_LIMIT = 20 << 20
AXES = ("brick", "group")


def dot(a, b, a_dim, b_dim):
    dims = (((a_dim,), (b_dim,)), ((), ()))
    return lax.dot_general(a, b, dims, preferred_element_type=F32)


def one_hot_rows(index, width):
    columns = jnp.arange(width, dtype=jnp.int32)
    return (index[:, None] == columns[None, :]).astype(BF)


def one_hot_low(row, lanes):
    low = (row & (LOW - 1)).astype(F32).astype(BF)
    iota = lax.broadcasted_iota(jnp.int32, (LOW, lanes), 0).astype(BF)
    hit = iota == jnp.broadcast_to(low, (LOW, lanes))
    return jnp.where(hit, jnp.ones((), BF), jnp.zeros((), BF))


def send_kernel(feat_ref, order_ref, out_ref):
    channels, rows = feat_ref.shape
    per = out_ref.shape[2]
    for n in range(rows // LOW):
        row = order_ref[:, n * LOW : (n + 1) * LOW]
        hot = one_hot_low(row, LOW)
        block = jnp.broadcast_to(lax.shift_right_logical(row, SHIFT), (channels, LOW))
        picked = jnp.zeros((channels, LOW), F32)
        for a in range(rows // LOW):
            picked = jnp.where(block == a, dot(feat_ref[:, a * LOW : (a + 1) * LOW], hot, 1, 0), picked)
        picked = picked.astype(BF)
        for p in range(LOW // per):
            out_ref[n * (LOW // per) + p] = picked[:, p * per : (p + 1) * per]


def forward_kernel(
    half_ref, got_ref, prev_ref, next_ref, map_ref, w_ref, bias_ref, cot_hbm, out_hbm, pg_hbm, send_ref, keep_ref,
    g_ref, x_ref, wt_ref, cot_ref, out_ref, pg_ref, cot_sem, out_sem, pg_sem,
):
    fetch = pltpu.make_async_copy(cot_hbm, cot_ref, cot_sem)
    fetch.start()
    offsets, voxels = map_ref.shape
    depth, c_out = w_ref.shape
    channels = depth // offsets
    here = voxels // LOW
    blocks = x_ref.shape[0] // channels
    center = offsets // 2
    per = got_ref.shape[2]
    for a in range(here):
        for p in range(LOW // per):
            x_ref[a * channels : (a + 1) * channels, p * per : (p + 1) * per] = got_ref[a * (LOW // per) + p]
    face = prev_ref.shape[1]
    x_ref[here * channels :, :face] = prev_ref[...]
    x_ref[here * channels :, face:] = next_ref[...]
    for k in range(offsets):
        wt_ref[:, k * channels : (k + 1) * channels] = w_ref[k * channels : (k + 1) * channels, :].T
        at = slice(k * channels, (k + 1) * channels)
        if k == center:
            for a in range(here):
                g_ref[at, a * LOW : (a + 1) * LOW] = x_ref[a * channels : (a + 1) * channels, :]
            continue
        row = map_ref[k : k + 1, :]
        high = lax.shift_right_logical(row, SHIFT)
        for n in range(here):
            sl = slice(n * LOW, (n + 1) * LOW)
            terms = dot(x_ref[...], one_hot_low(row[:, sl], LOW), 1, 0)
            block = jnp.broadcast_to(high[:, sl], (channels, LOW))
            picked = jnp.zeros((channels, LOW), F32)
            for a in range(blocks):
                picked = jnp.where(block == a, terms[a * channels : (a + 1) * channels], picked)
            g_ref[at, sl] = picked.astype(BF)
    fetch.wait()
    copies = []
    for n in range(here):
        sl = slice(n * LOW, (n + 1) * LOW)
        pre = dot(wt_ref[...], g_ref[:, sl], 1, 0).T + bias_ref[...]
        out_ref[sl, :] = jnp.maximum(pre, 0.0).astype(BF)
        pg_ref[sl, :] = jnp.where(pre > 0, cot_ref[sl, :].astype(F32), 0.0).astype(BF)
    copies.append(pltpu.make_async_copy(out_ref, out_hbm, out_sem))
    copies.append(pltpu.make_async_copy(pg_ref, pg_hbm, pg_sem))
    for copy in copies:
        copy.start()
    half = half_ref[0]
    count = depth // 2
    step = count // 9
    for ref, which in ((send_ref, 1 - half), (keep_ref, half)):
        for m in range(9):
            at = pl.ds(pl.multiple_of(which * count + m * step, 16), step)
            ref[m * step : (m + 1) * step, :] = dot(g_ref[at, :], pg_ref[...], 1, 0).astype(ref.dtype)
        ref[count:, :] = jnp.zeros((ref.shape[0] - count, c_out), ref.dtype)
    for copy in copies:
        copy.wait()


def backward_kernel(pg_ref, map_ref, w_ref, here_ref, faces_ref, c_ref, acc_ref):
    offsets, voxels = map_ref.shape
    depth = w_ref.shape[0]
    channels = depth // offsets
    here = voxels // LOW
    blocks = acc_ref.shape[0] // channels
    step = depth // 9
    for m in range(9):
        sl = slice(m * step, (m + 1) * step)
        c_ref[sl, :] = dot(w_ref[sl, :], pg_ref[...], 1, 1).astype(BF)
    center = offsets // 2
    for a in range(here):
        at = slice(a * channels, (a + 1) * channels)
        acc_ref[at, :] = c_ref[center * channels : (center + 1) * channels, a * LOW : (a + 1) * LOW].astype(F32)
    acc_ref[here * channels :, :] = jnp.zeros((channels * (blocks - here), LOW), F32)
    for k in range(offsets):
        if k == center:
            continue
        contrib = c_ref[k * channels : (k + 1) * channels, :]
        row = map_ref[k : k + 1, :]
        high = lax.shift_right_logical(row, SHIFT).astype(F32).astype(BF)
        block = jnp.broadcast_to(high, (channels, voxels))
        parts = [jnp.where(block == jnp.array(a, BF), contrib, jnp.zeros((), BF)) for a in range(blocks)]
        acc_ref[...] += dot(jnp.concatenate(parts, 0), one_hot_low(row, voxels), 1, 1)
    per = here_ref.shape[2]
    for a in range(here):
        for p in range(LOW // per):
            here_ref[a * (LOW // per) + p] = acc_ref[a * channels : (a + 1) * channels, p * per : (p + 1) * per]
    faces_ref[...] = acc_ref[here * channels :, :].astype(BF)


def whole(count):
    return [pl.BlockSpec(memory_space=pltpu.VMEM)] * count


def send_blocks(features, order, bricks):
    channels, rows = features.shape
    return pl.pallas_call(
        send_kernel,
        out_shape=jax.ShapeDtypeStruct((bricks, channels, rows // bricks), BF),
        in_specs=whole(2),
        out_specs=whole(1)[0],
        cost_estimate=pl.CostEstimate(flops=2 * rows * rows * channels, bytes_accessed=1 << 19, transcendentals=0),
    )(features, order)


def forward(half, got, prev_upper, next_lower, maps, w, bias, cot, padded):
    offsets, voxels = maps.shape
    depth, c_out = w.shape
    rows = depth // offsets * (voxels // LOW + 1)
    macs = voxels * depth * c_out * 2 + offsets * voxels * LOW * rows
    hbm = pl.BlockSpec(memory_space=pltpu.HBM)
    return pl.pallas_call(
        forward_kernel,
        out_shape=(
            jax.ShapeDtypeStruct((voxels, c_out), BF),
            jax.ShapeDtypeStruct((voxels, c_out), BF),
            jax.ShapeDtypeStruct((padded // 2, c_out), BF),
            jax.ShapeDtypeStruct((padded // 2, c_out), F32),
        ),
        in_specs=[pl.BlockSpec(memory_space=pltpu.SMEM)] + whole(6) + [hbm],
        out_specs=(hbm, hbm) + tuple(whole(2)),
        scratch_shapes=[
            pltpu.VMEM((depth, voxels), BF),
            pltpu.VMEM((rows, LOW), BF),
            pltpu.VMEM((c_out, depth), BF),
            pltpu.VMEM((voxels, c_out), BF),
            pltpu.VMEM((voxels, c_out), BF),
            pltpu.VMEM((voxels, c_out), BF),
            pltpu.SemaphoreType.DMA,
            pltpu.SemaphoreType.DMA,
            pltpu.SemaphoreType.DMA,
        ],
        compiler_params=pltpu.CompilerParams(vmem_limit_bytes=VMEM_LIMIT),
        cost_estimate=pl.CostEstimate(flops=2 * macs, bytes_accessed=5 << 20, transcendentals=0),
    )(half, got, prev_upper, next_lower, maps, w, bias, cot)


def backward(pg, maps, w, bricks):
    offsets, voxels = maps.shape
    depth, c_out = w.shape
    channels = depth // offsets
    rows = channels * (voxels // LOW + 1)
    macs = voxels * depth * c_out + offsets * voxels * LOW * rows
    return pl.pallas_call(
        backward_kernel,
        out_shape=(
            jax.ShapeDtypeStruct((bricks, channels, voxels // bricks), F32),
            jax.ShapeDtypeStruct((channels, LOW), BF),
        ),
        in_specs=whole(3),
        out_specs=tuple(whole(2)),
        scratch_shapes=[pltpu.VMEM((depth, voxels), BF), pltpu.VMEM((rows, LOW), F32)],
        compiler_params=pltpu.CompilerParams(vmem_limit_bytes=VMEM_LIMIT),
        cost_estimate=pl.CostEstimate(flops=2 * macs, bytes_accessed=3 << 20, transcendentals=0),
    )(pg, maps, w)


def stages(count):
    plan, stride = [], 1
    while stride < count:
        left = count // stride
        radix = 4 if stride > 1 and left % 4 == 0 else 2
        if left % radix:
            radix = left
        plan.append((stride, radix))
        stride *= radix
    return plan


def swapped(array, count, stride, radix, delta):
    def partner(i):
        digit = i // stride % radix
        other = (digit ^ delta) if radix in (2, 4) else (delta - digit) % radix
        return i + (other - digit) * stride

    return lax.ppermute(array, AXES, [(i, partner(i)) for i in range(count)])


def other_digit(digit, delta, radix):
    return (digit ^ delta) if radix in (2, 4) else (delta - digit) % radix


def reduce_stage(x, flat, count, stride, radix):
    digit = flat // stride % radix
    pieces = x.reshape((radix, x.shape[0] // radix) + x.shape[1:])
    total = None
    for delta in range(radix):
        piece = lax.dynamic_index_in_dim(pieces, other_digit(digit, delta, radix), 0, keepdims=False)
        if radix not in (2, 4) or delta:
            piece = swapped(piece, count, stride, radix, delta)
        total = piece.astype(F32) if total is None else total + piece.astype(F32)
    return total.astype(BF)


def gather_stage(x, flat, count, stride, radix):
    digit = flat // stride % radix
    got = [x if radix in (2, 4) and d == 0 else swapped(x, count, stride, radix, d) for d in range(radix)]
    parts = []
    for place in range(radix):
        part = got[0]
        for d in range(radix):
            where = (place ^ d) if radix in (2, 4) else (place + d) % radix
            part = jnp.where(digit == d, got[where], part)
        parts.append(part)
    return jnp.concatenate(parts, 0)


def meet(array_up, array_down):
    size = lax.axis_size("brick")
    odd = lax.axis_index("brick") % 2 == 1
    got = []
    for start in (0, 1):
        pairs = []
        for i in range(start, size - 1, 2):
            pairs += [(i, i + 1), (i + 1, i)]
        goes_up = ~odd if start == 0 else odd
        got.append(lax.ppermute(jnp.where(goes_up, array_up, array_down), "brick", pairs))
    return jnp.where(odd, got[0], got[1]), jnp.where(odd, got[1], got[0])


def on_device(features, order, face_list, face_count, kernel_map, weight, bias, cotangent):
    offsets, channels, c_out = weight.shape
    rows = features.shape[0]
    face = face_list.shape[0] // 2
    bricks = lax.axis_size("brick")
    count = bricks * lax.axis_size("group")
    per = rows // bricks
    depth = offsets * channels
    unit = 8 * count
    padded = -(-depth // unit) * unit

    w = weight.reshape(depth, c_out)
    flat = lax.axis_index("brick") * lax.axis_size("group") + lax.axis_index("group")
    send = send_blocks(features.T, order[None], bricks)
    got = lax.all_to_all(send, "brick", split_axis=0, concat_axis=0)
    local = got.transpose(1, 0, 2).reshape(channels, rows)

    slots = jnp.arange(face, dtype=jnp.int32)
    lower_pick = one_hot_rows(face_list[:face], rows) * (slots < face_count[0]).astype(BF)[:, None]
    upper_pick = one_hot_rows(face_list[face:], rows) * (slots < face_count[1]).astype(BF)[:, None]
    lower = dot(local, lower_pick, 1, 1).astype(BF)
    upper = dot(local, upper_pick, 1, 1).astype(BF)
    prev_upper, next_lower = meet(upper, lower)

    half = (flat % 2).astype(jnp.int32)[None]
    output, pre_grad, give, keep = forward(
        half, got, prev_upper, next_lower, kernel_map, w, bias[None], cotangent, padded
    )
    plan = stages(count)[1:]
    total = (keep + swapped(give, count, 1, 2, 1).astype(F32)).astype(BF)
    total = reduce_stage(total, flat, count, *plan[0])
    here, faces = backward(pre_grad, kernel_map, w, bricks)
    total, faces = lax.optimization_barrier((total, faces))
    from_prev, from_next = meet(faces[:, face:], faces[:, :face])
    for stride, radix in plan[1:]:
        total = reduce_stage(total, flat, count, stride, radix)

    added = dot(from_prev, lower_pick, 1, 0) + dot(from_next, upper_pick, 1, 0)
    local_grad = (here + added.reshape(channels, bricks, per).transpose(1, 0, 2)).astype(BF)
    total, local_grad = lax.optimization_barrier((total, local_grad))
    returned = lax.all_to_all(local_grad, "brick", split_axis=0, concat_axis=0)
    returned = returned.transpose(1, 0, 2).reshape(channels, rows)
    order_pick = one_hot_rows(order, rows)

    for stride, radix in reversed(plan):
        total = gather_stage(total, flat, count, stride, radix)
    total, returned = lax.optimization_barrier((total, returned))
    grad_in = dot(returned, order_pick, 1, 0).astype(BF).T
    other = swapped(total, count, 1, 2, 1)
    low = jnp.where(flat % 2 == 0, total, other)[: depth // 2]
    high = jnp.where(flat % 2 == 0, other, total)[: depth // 2]
    scale = jnp.float32(1.0 / math.sqrt(count * rows))
    weight_grad = (jnp.concatenate([low, high], 0).astype(F32) * scale).reshape(offsets, channels, c_out)
    return output, grad_in, weight_grad


def solution(mesh):
    return jax.shard_map(
        on_device,
        mesh=mesh,
        in_specs=(
            P(AXES, None),
            P(AXES),
            P(AXES),
            P(AXES),
            P(None, AXES),
            P(),
            P(),
            P(AXES, None),
        ),
        out_specs=(P(AXES, None), P(AXES, None), P()),
        check_vma=False,
    )
```

```python
import functools
import math

import jax
import jax.numpy as jnp
from jax import lax
from jax.experimental import pallas as pl
from jax.experimental.pallas import tpu as pltpu
from jax.sharding import PartitionSpec as P

BF = jnp.bfloat16
F32 = jnp.float32
LOW = 256
SHIFT = 8
VMEM_LIMIT = 20 << 20
SMALL_LIMIT = 6 << 20
FULL_LIMIT = 58 << 20
AXES = ("brick", "group")


def dot(a, b, a_dim, b_dim):
    dims = (((a_dim,), (b_dim,)), ((), ()))
    return lax.dot_general(a, b, dims, preferred_element_type=F32)


def one_hot_rows(index, width):
    columns = jnp.arange(width, dtype=jnp.int32)
    return (index[:, None] == columns[None, :]).astype(BF)


def one_hot_low(low, lanes):
    iota = lax.broadcasted_iota(jnp.int32, (LOW, lanes), 0).astype(BF)
    hit = iota == jnp.broadcast_to(low.astype(BF), (LOW, lanes))
    return jnp.where(hit, jnp.ones((), BF), jnp.zeros((), BF))


def send_kernel(feat_ref, order_ref, out_ref, x_ref):
    channels, rows = feat_ref.shape
    per = out_ref.shape[2]
    for a in range(rows // LOW):
        x_ref[a * channels : (a + 1) * channels, :] = feat_ref[:, a * LOW : (a + 1) * LOW]
    for n in range(rows // LOW):
        row = order_ref[:, n * LOW : (n + 1) * LOW]
        terms = dot(x_ref[...], one_hot_low((row & (LOW - 1)).astype(F32), LOW), 1, 0)
        block = jnp.broadcast_to(lax.shift_right_logical(row, SHIFT), (channels, LOW))
        picked = terms[:channels]
        for a in range(1, rows // LOW):
            picked = jnp.where(block == a, terms[a * channels : (a + 1) * channels], picked)
        picked = picked.astype(BF)
        for p in range(LOW // per):
            out_ref[n * (LOW // per) + p] = picked[:, p * per : (p + 1) * per]


def forward_kernel(
    half_ref, got_ref, prev_ref, next_ref, low_ref, high_ref, w_hbm, bias_ref, cot_hbm, out_hbm, send_ref, keep_ref,
    g_ref, x_ref, wt_ref, w_ref, cot_ref, out_ref, pg_ref, w_sem, cot_sem, out_sem,
):
    fetch_w = pltpu.make_async_copy(w_hbm, w_ref, w_sem)
    fetch_w.start()
    fetch_cot = pltpu.make_async_copy(cot_hbm, cot_ref, cot_sem)
    fetch_cot.start()
    offsets, voxels = low_ref.shape
    depth, c_out = w_ref.shape
    channels = depth // offsets
    here = voxels // LOW
    blocks = x_ref.shape[0] // channels
    center = offsets // 2
    per = got_ref.shape[2]
    for a in range(here):
        for p in range(LOW // per):
            x_ref[a * channels : (a + 1) * channels, p * per : (p + 1) * per] = got_ref[a * (LOW // per) + p]
    face = prev_ref.shape[1]
    x_ref[here * channels :, :face] = prev_ref[...]
    x_ref[here * channels :, face:] = next_ref[...]
    ready = offsets // 3
    for k in range(offsets):
        if k == ready:
            fetch_w.wait()
            fetch_cot.wait()
        for j in range(2 * (k - ready), min(2 * (k - ready + 1), offsets)) if k >= ready else ():
            wt_ref[:, j * channels : (j + 1) * channels] = w_ref[j * channels : (j + 1) * channels, :].T
        at = slice(k * channels, (k + 1) * channels)
        if k == center:
            for a in range(here):
                g_ref[at, a * LOW : (a + 1) * LOW] = x_ref[a * channels : (a + 1) * channels, :]
            continue
        low, high = low_ref[k : k + 1, :], high_ref[k : k + 1, :]
        for n in range(here):
            sl = slice(n * LOW, (n + 1) * LOW)
            terms = dot(x_ref[...], one_hot_low(low[:, sl], LOW), 1, 0)
            block = jnp.broadcast_to(high[:, sl], (channels, LOW))
            picked = jnp.zeros((channels, LOW), F32)
            for a in range(blocks):
                picked = jnp.where(block == a, terms[a * channels : (a + 1) * channels], picked)
            g_ref[at, sl] = picked.astype(BF)
    for n in range(here):
        sl = slice(n * LOW, (n + 1) * LOW)
        pre = dot(wt_ref[...], g_ref[:, sl], 1, 0).T + bias_ref[0:1, :]
        out_ref[sl, :] = jnp.maximum(pre, 0.0).astype(BF)
        pg_ref[sl, :] = jnp.where(pre > 0, cot_ref[sl, :].astype(F32), 0.0).astype(BF)
    store = pltpu.make_async_copy(out_ref, out_hbm, out_sem)
    store.start()
    half = half_ref[0]
    count = depth // 2
    step = count // 3
    for ref, which in ((send_ref, 1 - half), (keep_ref, half)):
        for m in range(3):
            at = pl.ds(pl.multiple_of(which * count + m * step, 16), step)
            ref[m * step : (m + 1) * step, :] = dot(g_ref[at, :], pg_ref[...], 1, 0).astype(ref.dtype)
        ref[count:, :] = jnp.zeros((ref.shape[0] - count, c_out), ref.dtype)
    store.wait()


def backward_kernel(
    packed, out_hbm, cot_hbm, low_ref, high_ref, w_ref, here_ref, faces_ref,
    c_ref, acc_ref, pg_ref, out_ref, cot_ref, out_sem, cot_sem,
):
    fetch_out = pltpu.make_async_copy(out_hbm, out_ref, out_sem)
    fetch_out.start()
    fetch_cot = pltpu.make_async_copy(cot_hbm, cot_ref, cot_sem)
    fetch_cot.start()
    offsets, voxels = low_ref.shape
    depth = w_ref.shape[0]
    channels = depth // offsets
    here = voxels // LOW
    blocks = acc_ref.shape[0] // channels
    fetch_out.wait()
    fetch_cot.wait()
    pg_ref[...] = jnp.where(out_ref[...] > 0, cot_ref[...], jnp.zeros((), BF))
    step = depth // 3
    for m in range(3):
        sl = slice(m * step, (m + 1) * step)
        c_ref[sl, :] = dot(w_ref[sl, :], pg_ref[...], 1, 1).astype(BF)
    center = offsets // 2
    for a in range(here):
        at = slice(a * channels, (a + 1) * channels)
        acc_ref[at, :] = c_ref[center * channels : (center + 1) * channels, a * LOW : (a + 1) * LOW].astype(F32)
    acc_ref[here * channels :, :] = jnp.zeros((channels * (blocks - here), LOW), F32)
    for k in range(offsets):
        if k == center:
            continue
        contrib = c_ref[k * channels : (k + 1) * channels, :]
        low, high = low_ref[k : k + 1, :], high_ref[k : k + 1, :]
        block = jnp.broadcast_to(high.astype(BF), (channels, voxels))
        parts = [jnp.where(block == jnp.array(a, BF), contrib, jnp.zeros((), BF)) for a in range(blocks)]
        acc_ref[...] += dot(jnp.concatenate(parts, 0), one_hot_low(low, voxels), 1, 1)
    if packed:
        part, per = channels // 2, LOW // 2
        for a in range(here):
            for p in range(2):
                for h in range(2):
                    at = slice(a * channels + h * part, a * channels + (h + 1) * part)
                    to = slice((2 * a + p) * part, (2 * a + p + 1) * part)
                    here_ref[to, h * per : (h + 1) * per] = acc_ref[at, p * per : (p + 1) * per]
    else:
        here_ref[...] = acc_ref[: here * channels, :]
    faces_ref[...] = acc_ref[here * channels :, :].astype(BF)


def finish_kernel(packed, here_ref, prev_ref, next_ref, pick_ref, out_ref, from_ref):
    channels, face = prev_ref.shape
    blocks = here_ref.shape[0] // channels
    from_ref[:, :face] = prev_ref[...]
    from_ref[:, face:] = next_ref[...]
    part, per = channels // 2, LOW // 2
    for a in range(blocks):
        added = dot(from_ref[...], pick_ref[:, a * LOW : (a + 1) * LOW], 1, 0)
        if not packed:
            at = slice(a * channels, (a + 1) * channels)
            out_ref[at, :] = (here_ref[at, :] + added).astype(BF)
            continue
        for p in range(2):
            at = slice((2 * a + p) * part, (2 * a + p + 1) * part)
            for h in range(2):
                lanes = slice(h * per, (h + 1) * per)
                term = added[h * part : (h + 1) * part, p * per : (p + 1) * per]
                out_ref[at, lanes] = (here_ref[at, lanes] + term).astype(BF)


def place_kernel(side_ref, keep_ref, came_ref, order_ref, out_ref, back_ref):
    channels, rows = out_ref.shape
    part, per = channels // 2, LOW // 2
    side = side_ref[0]
    for z in range(rows // LOW):
        at = slice(z * part, (z + 1) * part)
        for p in range(2):
            block = jnp.where(side == p, keep_ref[at, :].astype(F32), came_ref[at, :].astype(F32)).astype(BF)
            lanes = slice((2 * z + p) * per, (2 * z + p + 1) * per)
            for h in range(2):
                back_ref[h * part : (h + 1) * part, lanes] = block[:, h * per : (h + 1) * per]
    row = order_ref[...]
    block = jnp.broadcast_to(lax.shift_right_logical(row, SHIFT).astype(F32).astype(BF), (channels, rows))
    back = back_ref[...]
    parts = [jnp.where(block == jnp.array(a, BF), back, jnp.zeros((), BF)) for a in range(rows // LOW)]
    placed = dot(jnp.concatenate(parts, 0), one_hot_low((row & (LOW - 1)).astype(F32), rows), 1, 1)
    for a in range(rows // LOW):
        out_ref[:, a * LOW : (a + 1) * LOW] = placed[a * channels : (a + 1) * channels].astype(BF)


def whole(count):
    return [pl.BlockSpec(memory_space=pltpu.VMEM)] * count


def send_blocks(features, order, bricks):
    channels, rows = features.shape
    return pl.pallas_call(
        send_kernel,
        out_shape=jax.ShapeDtypeStruct((bricks, channels, rows // bricks), BF),
        in_specs=whole(2),
        out_specs=whole(1)[0],
        scratch_shapes=[pltpu.VMEM((channels * rows // LOW, LOW), BF)],
        compiler_params=pltpu.CompilerParams(vmem_limit_bytes=SMALL_LIMIT),
        cost_estimate=pl.CostEstimate(flops=2 * rows * rows * channels, bytes_accessed=1 << 19, transcendentals=0),
    )(features, order)


def forward(half, got, prev_upper, next_lower, low, high, w, bias, cot, padded):
    offsets, voxels = low.shape
    depth, c_out = w.shape
    rows = depth // offsets * (voxels // LOW + 1)
    macs = voxels * depth * c_out * 2 + offsets * voxels * LOW * rows
    hbm = pl.BlockSpec(memory_space=pltpu.HBM)
    return pl.pallas_call(
        forward_kernel,
        out_shape=(
            jax.ShapeDtypeStruct((voxels, c_out), BF),
            jax.ShapeDtypeStruct((padded // 2, c_out), BF),
            jax.ShapeDtypeStruct((padded // 2, c_out), F32),
        ),
        in_specs=[pl.BlockSpec(memory_space=pltpu.SMEM)] + whole(5) + [hbm] + whole(1) + [hbm],
        out_specs=(hbm,) + tuple(whole(2)),
        scratch_shapes=[
            pltpu.VMEM((depth, voxels), BF),
            pltpu.VMEM((rows, LOW), BF),
            pltpu.VMEM((c_out, depth), BF),
            pltpu.VMEM((depth, c_out), BF),
            pltpu.VMEM((voxels, c_out), BF),
            pltpu.VMEM((voxels, c_out), BF),
            pltpu.VMEM((voxels, c_out), BF),
            pltpu.SemaphoreType.DMA,
            pltpu.SemaphoreType.DMA,
            pltpu.SemaphoreType.DMA,
        ],
        compiler_params=pltpu.CompilerParams(vmem_limit_bytes=FULL_LIMIT),
        cost_estimate=pl.CostEstimate(flops=2 * macs, bytes_accessed=5 << 20, transcendentals=0),
    )(half, got, prev_upper, next_lower, low, high, w, bias, cot)


def backward(packed, out, cot, low, high, w):
    hbm = pl.BlockSpec(memory_space=pltpu.HBM)
    offsets, voxels = low.shape
    depth, c_out = w.shape
    channels = depth // offsets
    rows = channels * (voxels // LOW + 1)
    macs = voxels * depth * c_out + offsets * voxels * LOW * rows
    return pl.pallas_call(
        functools.partial(backward_kernel, packed),
        out_shape=(
            jax.ShapeDtypeStruct((voxels // LOW * channels, LOW), F32),
            jax.ShapeDtypeStruct((channels, LOW), BF),
        ),
        in_specs=[hbm, hbm] + whole(3),
        out_specs=tuple(whole(2)),
        scratch_shapes=[
            pltpu.VMEM((depth, voxels), BF),
            pltpu.VMEM((rows, LOW), F32),
            pltpu.VMEM((voxels, c_out), BF),
            pltpu.VMEM((voxels, c_out), BF),
            pltpu.VMEM((voxels, c_out), BF),
            pltpu.SemaphoreType.DMA,
            pltpu.SemaphoreType.DMA,
        ],
        compiler_params=pltpu.CompilerParams(vmem_limit_bytes=VMEM_LIMIT),
        cost_estimate=pl.CostEstimate(flops=2 * macs, bytes_accessed=3 << 20, transcendentals=0),
    )(out, cot, low, high, w)


def finish(packed, here, from_prev, from_next, pick):
    rows, _ = here.shape
    channels, face = from_prev.shape
    return pl.pallas_call(
        functools.partial(finish_kernel, packed),
        out_shape=jax.ShapeDtypeStruct((rows, LOW), BF),
        in_specs=whole(4),
        out_specs=whole(1)[0],
        scratch_shapes=[pltpu.VMEM((channels, 2 * face), BF)],
        compiler_params=pltpu.CompilerParams(vmem_limit_bytes=SMALL_LIMIT),
        cost_estimate=pl.CostEstimate(flops=4 * rows * LOW * face, bytes_accessed=1 << 20, transcendentals=0),
    )(here, from_prev, from_next, pick)


def place(side, keep, came, order, channels):
    rows = order.shape[1]
    return pl.pallas_call(
        place_kernel,
        out_shape=jax.ShapeDtypeStruct((channels, rows), BF),
        in_specs=[pl.BlockSpec(memory_space=pltpu.SMEM)] + whole(3),
        out_specs=whole(1)[0],
        scratch_shapes=[pltpu.VMEM((channels, rows), BF)],
        compiler_params=pltpu.CompilerParams(vmem_limit_bytes=SMALL_LIMIT),
        cost_estimate=pl.CostEstimate(flops=2 * rows * rows * channels, bytes_accessed=1 << 20, transcendentals=0),
    )(side, keep, came, order)


def stages(count):
    plan, stride = [], 1
    while stride < count:
        left = count // stride
        radix = 4 if stride > 1 and left % 4 == 0 else 2
        if left % radix:
            radix = left
        plan.append((stride, radix))
        stride *= radix
    return plan


def swapped(array, count, stride, radix, delta):
    def partner(i):
        digit = i // stride % radix
        other = (digit ^ delta) if radix in (2, 4) else (delta - digit) % radix
        return i + (other - digit) * stride

    return lax.ppermute(array, AXES, [(i, partner(i)) for i in range(count)])


def other_digit(digit, delta, radix):
    return (digit ^ delta) if radix in (2, 4) else (delta - digit) % radix


def reduce_stage(x, flat, count, stride, radix):
    digit = flat // stride % radix
    pieces = x.reshape((radix, x.shape[0] // radix) + x.shape[1:])
    total = None
    for delta in range(radix):
        piece = lax.dynamic_index_in_dim(pieces, other_digit(digit, delta, radix), 0, keepdims=False)
        if radix not in (2, 4) or delta:
            piece = swapped(piece, count, stride, radix, delta)
        total = piece.astype(F32) if total is None else total + piece.astype(F32)
    return total.astype(BF)


def by_digit(got, digit, radix):
    parts = []
    for place in range(radix):
        part = got[0]
        for d in range(radix):
            where = (place ^ d) if radix in (2, 4) else (place + d) % radix
            part = jnp.where(digit == d, got[where], part)
        parts.append(part)
    return parts


def joined(parts):
    return parts[0] if len(parts) == 1 else jnp.concatenate(parts, 0)


def gather_stage(parts, flat, count, stride, radix, cargo=lambda delta: None):
    digit = flat // stride % radix
    rows = sum(part.shape[0] for part in parts)
    got, brought = [], {}
    for d in range(radix):
        if radix in (2, 4) and d == 0:
            got.append(joined(parts))
            continue
        extra = cargo(d)
        piece = swapped(joined(parts if extra is None else parts + [extra]), count, stride, radix, d)
        got.append(piece[:rows])
        brought[d] = piece[rows:]
    return by_digit(got, digit, radix), brought


def meet(array_up, array_down):
    size = lax.axis_size("brick")
    odd = lax.axis_index("brick") % 2 == 1
    got = []
    for start in (0, 1):
        pairs = []
        for i in range(start, size - 1, 2):
            pairs += [(i, i + 1), (i + 1, i)]
        goes_up = ~odd if start == 0 else odd
        got.append(lax.ppermute(jnp.where(goes_up, array_up, array_down), "brick", pairs))
    return jnp.where(odd, got[0], got[1]), jnp.where(odd, got[1], got[0])


def on_device(features, order, face_list, face_count, kernel_map, weight, bias, cotangent):
    offsets, channels, c_out = weight.shape
    rows = features.shape[0]
    face = face_list.shape[0] // 2
    bricks = lax.axis_size("brick")
    count = bricks * lax.axis_size("group")
    per = rows // bricks
    depth = offsets * channels
    unit = 8 * count
    padded = -(-depth // unit) * unit

    w = weight.reshape(depth, c_out)
    flat = lax.axis_index("brick") * lax.axis_size("group") + lax.axis_index("group")
    send = send_blocks(features.T, order[None], bricks)
    got = lax.all_to_all(send, "brick", split_axis=0, concat_axis=0)

    slots = jnp.arange(2 * face, dtype=jnp.int32)
    live = jnp.where(slots < face, slots < face_count[0], slots - face < face_count[1])
    pick = one_hot_rows(jnp.where(live, face_list, -1), rows)
    pick, got = lax.optimization_barrier((pick, got))
    local = got.transpose(1, 0, 2).reshape(channels, rows)
    shown = dot(local, pick, 1, 1).astype(BF)
    prev_upper, next_lower = meet(shown[:, face:], shown[:, :face])

    half = (flat % 2).astype(jnp.int32)[None]
    low = (kernel_map & (LOW - 1)).astype(F32)
    high = lax.shift_right_logical(kernel_map, SHIFT).astype(F32)
    tall_bias = jnp.broadcast_to(bias, (8, c_out))
    output, give, keep = forward(half, got, prev_upper, next_lower, low, high, w, tall_bias, cotangent, padded)
    packed = (bricks, count) == (8, 32) and per * 2 == LOW and channels % 16 == 0
    plan = stages(count)[1:]
    total = (keep + swapped(give, count, 1, 2, 1).astype(F32)).astype(BF)
    total = reduce_stage(total, flat, count, *plan[0])
    here, faces = backward(packed, output, cotangent, low, high, w)
    total, faces = lax.optimization_barrier((total, faces))
    from_prev, from_next = meet(faces[:, face:], faces[:, :face])
    for stride, radix in plan[1:]:
        total = reduce_stage(total, flat, count, stride, radix)

    local_grad = finish(packed, here, from_prev, from_next, pick)
    if packed:
        part = channels // 2
        total, local_grad = lax.optimization_barrier((total, local_grad))
        local_grad = local_grad.reshape(bricks // 2, channels, LOW)
        z, x = flat // 8, flat // 4 % 2
        cargo = lambda d: lax.dynamic_index_in_dim(local_grad, z ^ d, 0, keepdims=False)
        parts, brought = gather_stage([total], flat, count, 8, 4, cargo)
        mine = jnp.stack(by_digit([cargo(0)] + [brought[d] for d in (1, 2, 3)], z, 4))
        mine = mine.reshape(bricks // 2, 2, part, LOW)
        give = jnp.where(x == 0, mine[:, 1], mine[:, 0]).reshape(-1, LOW)
        keep = jnp.where(x == 0, mine[:, 0], mine[:, 1]).reshape(-1, LOW)
        parts, brought = gather_stage(parts, flat, count, 2, 4, lambda d: give if d == 2 else None)
        came = brought[2]
    else:
        blocks = rows // LOW
        send = local_grad.reshape(blocks, channels, LOW // per, per).transpose(0, 2, 1, 3)
        came = lax.all_to_all(send.reshape(bricks, channels, per), "brick", split_axis=0, concat_axis=0)
        parts = [total]
        for stride, radix in reversed(plan):
            parts, _ = gather_stage(parts, flat, count, stride, radix)
    total = joined(parts)
    total, came = lax.optimization_barrier((total, came))
    if packed:
        grad_in = place(x.astype(jnp.int32)[None], keep, came, order[None], channels).T
    else:
        returned = came.transpose(1, 0, 2).reshape(channels, rows)
        grad_in = dot(returned, one_hot_rows(order, rows), 1, 0).astype(BF).T
    other = swapped(total, count, 1, 2, 1)
    low = jnp.where(flat % 2 == 0, total, other)[: depth // 2]
    high = jnp.where(flat % 2 == 0, other, total)[: depth // 2]
    scale = jnp.float32(1.0 / math.sqrt(count * rows))
    weight_grad = (jnp.concatenate([low, high], 0).astype(F32) * scale).reshape(offsets, channels, c_out)
    return output, grad_in, weight_grad


def solution(mesh):
    return jax.shard_map(
        on_device,
        mesh=mesh,
        in_specs=(
            P(AXES, None),
            P(AXES),
            P(AXES),
            P(AXES),
            P(None, AXES),
            P(),
            P(),
            P(AXES, None),
        ),
        out_specs=(P(AXES, None), P(AXES, None), P()),
        check_vma=False,
    )
```

```python
import functools
import math

import jax
import jax.numpy as jnp
from jax import lax
from jax.experimental import pallas as pl
from jax.experimental.pallas import tpu as pltpu
from jax.sharding import PartitionSpec as P

BF = jnp.bfloat16
F32 = jnp.float32
LOW = 256
SHIFT = 8
VMEM_LIMIT = 20 << 20
SMALL_LIMIT = 6 << 20
FULL_LIMIT = 52 << 20
ALL_LIMIT = 60 << 20
AXES = ("brick", "group")


def dot(a, b, a_dim, b_dim):
    dims = (((a_dim,), (b_dim,)), ((), ()))
    return lax.dot_general(a, b, dims, preferred_element_type=F32)


def one_hot_rows(index, width):
    columns = jnp.arange(width, dtype=jnp.int32)
    return (index[:, None] == columns[None, :]).astype(BF)


def one_hot_low(low, lanes):
    iota = lax.broadcasted_iota(jnp.int32, (LOW, lanes), 0).astype(BF)
    hit = iota == jnp.broadcast_to(low.astype(BF), (LOW, lanes))
    return jnp.where(hit, jnp.ones((), BF), jnp.zeros((), BF))


def send_kernel(feat_hbm, order_hbm, out_ref, feat_ref, order_ref, x_ref, feat_sem, order_sem):
    fetch_feat = pltpu.make_async_copy(feat_hbm, feat_ref, feat_sem)
    fetch_feat.start()
    fetch_order = pltpu.make_async_copy(order_hbm, order_ref, order_sem)
    fetch_order.start()
    channels, rows = feat_ref.shape
    per = out_ref.shape[2]
    fetch_feat.wait()
    fetch_order.wait()
    for a in range(rows // LOW):
        x_ref[a * channels : (a + 1) * channels, :] = feat_ref[:, a * LOW : (a + 1) * LOW]
    for n in range(rows // LOW):
        row = order_ref[:, n * LOW : (n + 1) * LOW]
        terms = dot(x_ref[...], one_hot_low((row & (LOW - 1)).astype(F32), LOW), 1, 0)
        block = jnp.broadcast_to(lax.shift_right_logical(row, SHIFT), (channels, LOW))
        picked = terms[:channels]
        for a in range(1, rows // LOW):
            picked = jnp.where(block == a, terms[a * channels : (a + 1) * channels], picked)
        picked = picked.astype(BF)
        for p in range(LOW // per):
            out_ref[n * (LOW // per) + p] = picked[:, p * per : (p + 1) * per]


def sides(odd, first_ref, second_ref):
    first, second = first_ref[...].astype(F32), second_ref[...].astype(F32)
    low = jnp.where(odd == 1, first, second)
    high = jnp.where(odd == 1, second, first)
    return low.astype(BF), high.astype(BF)


def forward_kernel(
    flag_ref, got_ref, even_ref, odd_ref, low_ref, high_ref, w_hbm, bias_ref, cot_hbm, out_hbm, send_ref, keep_ref,
    g_ref, x_ref, wt_ref, w_ref, cot_ref, out_ref, pg_ref, w_sem, cot_sem, out_sem,
):
    fetch_w = pltpu.make_async_copy(w_hbm, w_ref, w_sem)
    fetch_w.start()
    fetch_cot = pltpu.make_async_copy(cot_hbm, cot_ref, cot_sem)
    fetch_cot.start()
    offsets, voxels = low_ref.shape
    depth, c_out = w_ref.shape
    channels = depth // offsets
    here = voxels // LOW
    blocks = x_ref.shape[0] // channels
    center = offsets // 2
    per = got_ref.shape[2]
    for a in range(here):
        for p in range(LOW // per):
            x_ref[a * channels : (a + 1) * channels, p * per : (p + 1) * per] = got_ref[a * (LOW // per) + p]
    face = even_ref.shape[1]
    prev, after = sides(flag_ref[1], even_ref, odd_ref)
    x_ref[here * channels :, :face] = prev
    x_ref[here * channels :, face:] = after
    ready = offsets // 3
    for k in range(offsets):
        if k == ready:
            fetch_w.wait()
            fetch_cot.wait()
        for j in range(2 * (k - ready), min(2 * (k - ready + 1), offsets)) if k >= ready else ():
            wt_ref[:, j * channels : (j + 1) * channels] = w_ref[j * channels : (j + 1) * channels, :].T
        at = slice(k * channels, (k + 1) * channels)
        if k == center:
            for a in range(here):
                g_ref[at, a * LOW : (a + 1) * LOW] = x_ref[a * channels : (a + 1) * channels, :]
            continue
        low, high = low_ref[k : k + 1, :], high_ref[k : k + 1, :]
        for n in range(here):
            sl = slice(n * LOW, (n + 1) * LOW)
            terms = dot(x_ref[...], one_hot_low(low[:, sl], LOW), 1, 0)
            block = jnp.broadcast_to(high[:, sl], (channels, LOW))
            picked = jnp.zeros((channels, LOW), F32)
            for a in range(blocks):
                picked = jnp.where(block == a, terms[a * channels : (a + 1) * channels], picked)
            g_ref[at, sl] = picked.astype(BF)
    for n in range(here):
        sl = slice(n * LOW, (n + 1) * LOW)
        pre = dot(wt_ref[...], g_ref[:, sl], 1, 0).T + bias_ref[...]
        out_ref[sl, :] = jnp.maximum(pre, 0.0).astype(BF)
        pg_ref[sl, :] = jnp.where(pre > 0, cot_ref[sl, :].astype(F32), 0.0).astype(BF)
    store = pltpu.make_async_copy(out_ref, out_hbm, out_sem)
    store.start()
    half = flag_ref[0]
    count = depth // 2
    for ref, which in ((send_ref, 1 - half), (keep_ref, half)):
        for m in range(0, count, 288):
            step = min(288, count - m)
            at = pl.ds(pl.multiple_of(which * count + m, 16), step)
            ref[m : m + step, :] = dot(g_ref[at, :], pg_ref[...], 1, 0).astype(ref.dtype)
        ref[count:, :] = jnp.zeros((ref.shape[0] - count, c_out), ref.dtype)
    store.wait()


def backward_kernel(
    packed, flag_ref, out_hbm, cot_hbm, low_ref, high_ref, w_ref, here_ref, first_ref, second_ref,
    c_ref, acc_ref, pg_ref, out_ref, cot_ref, out_sem, cot_sem,
):
    fetch_out = pltpu.make_async_copy(out_hbm, out_ref, out_sem)
    fetch_out.start()
    fetch_cot = pltpu.make_async_copy(cot_hbm, cot_ref, cot_sem)
    fetch_cot.start()
    offsets, voxels = low_ref.shape
    depth = w_ref.shape[0]
    channels = depth // offsets
    here = voxels // LOW
    blocks = acc_ref.shape[0] // channels
    fetch_out.wait()
    fetch_cot.wait()
    pg_ref[...] = jnp.where(out_ref[...] > 0, cot_ref[...], jnp.zeros((), BF))
    step = depth // 9
    for m in range(9):
        sl = slice(m * step, (m + 1) * step)
        c_ref[sl, :] = dot(w_ref[sl, :], pg_ref[...], 1, 1).astype(BF)
    center = offsets // 2
    for a in range(here):
        at = slice(a * channels, (a + 1) * channels)
        acc_ref[at, :] = c_ref[center * channels : (center + 1) * channels, a * LOW : (a + 1) * LOW].astype(F32)
    acc_ref[here * channels :, :] = jnp.zeros((channels * (blocks - here), LOW), F32)
    for k in range(offsets):
        if k == center:
            continue
        contrib = c_ref[k * channels : (k + 1) * channels, :]
        low, high = low_ref[k : k + 1, :], high_ref[k : k + 1, :]
        block = jnp.broadcast_to(high.astype(BF), (channels, voxels))
        parts = [jnp.where(block == jnp.array(a, BF), contrib, jnp.zeros((), BF)) for a in range(blocks)]
        acc_ref[...] += dot(jnp.concatenate(parts, 0), one_hot_low(low, voxels), 1, 1)
    if packed:
        part, per = channels // 2, LOW // 2
        for a in range(here):
            for p in range(2):
                for h in range(2):
                    at = slice(a * channels + h * part, a * channels + (h + 1) * part)
                    to = slice((2 * a + p) * part, (2 * a + p + 1) * part)
                    here_ref[to, h * per : (h + 1) * per] = acc_ref[at, p * per : (p + 1) * per]
    else:
        here_ref[...] = acc_ref[: here * channels, :]
    face = first_ref.shape[1]
    down, up = acc_ref[here * channels :, :face], acc_ref[here * channels :, face:]
    odd = flag_ref[1]
    first_ref[...] = jnp.where(odd == 1, down, up).astype(BF)
    second_ref[...] = jnp.where(odd == 1, up, down).astype(BF)


def finish_kernel(packed, flag_ref, here_ref, first_ref, second_ref, pick_ref, out_ref, from_ref):
    channels, face = first_ref.shape
    blocks = here_ref.shape[0] // channels
    prev, after = sides(flag_ref[1], first_ref, second_ref)
    from_ref[:, :face] = prev
    from_ref[:, face:] = after
    part, per = channels // 2, LOW // 2
    for a in range(blocks):
        added = dot(from_ref[...], pick_ref[:, a * LOW : (a + 1) * LOW], 1, 0)
        if not packed:
            at = slice(a * channels, (a + 1) * channels)
            out_ref[at, :] = (here_ref[at, :] + added).astype(BF)
            continue
        for p in range(2):
            at = slice((2 * a + p) * part, (2 * a + p + 1) * part)
            for h in range(2):
                lanes = slice(h * per, (h + 1) * per)
                term = added[h * part : (h + 1) * part, p * per : (p + 1) * per]
                out_ref[at, lanes] = (here_ref[at, lanes] + term).astype(BF)


def place_kernel(side_ref, keep_ref, came_ref, order_ref, out_ref, back_ref):
    channels, rows = out_ref.shape
    part, per = channels // 2, LOW // 2
    side = side_ref[0]
    for z in range(rows // LOW):
        at = slice(z * part, (z + 1) * part)
        for p in range(2):
            block = jnp.where(side == p, keep_ref[at, :].astype(F32), came_ref[at, :].astype(F32)).astype(BF)
            lanes = slice((2 * z + p) * per, (2 * z + p + 1) * per)
            for h in range(2):
                back_ref[h * part : (h + 1) * part, lanes] = block[:, h * per : (h + 1) * per]
    row = order_ref[...]
    block = jnp.broadcast_to(lax.shift_right_logical(row, SHIFT).astype(F32).astype(BF), (channels, rows))
    back = back_ref[...]
    parts = [jnp.where(block == jnp.array(a, BF), back, jnp.zeros((), BF)) for a in range(rows // LOW)]
    placed = dot(jnp.concatenate(parts, 0), one_hot_low((row & (LOW - 1)).astype(F32), rows), 1, 1)
    for a in range(rows // LOW):
        out_ref[:, a * LOW : (a + 1) * LOW] = placed[a * channels : (a + 1) * channels].astype(BF)


def whole(count):
    return [pl.BlockSpec(memory_space=pltpu.VMEM)] * count


def send_blocks(features, order, bricks):
    channels, rows = features.shape
    hbm = pl.BlockSpec(memory_space=pltpu.HBM)
    return pl.pallas_call(
        send_kernel,
        out_shape=jax.ShapeDtypeStruct((bricks, channels, rows // bricks), BF),
        in_specs=[hbm, hbm],
        out_specs=whole(1)[0],
        scratch_shapes=[
            pltpu.VMEM((channels, rows), BF),
            pltpu.VMEM((1, rows), jnp.int32),
            pltpu.VMEM((channels * rows // LOW, LOW), BF),
            pltpu.SemaphoreType.DMA,
            pltpu.SemaphoreType.DMA,
        ],
        compiler_params=pltpu.CompilerParams(vmem_limit_bytes=ALL_LIMIT),
        cost_estimate=pl.CostEstimate(flops=2 * rows * rows * channels, bytes_accessed=1 << 19, transcendentals=0),
    )(features, order)


def forward(flags, got, first, second, low, high, w, bias, cot, padded):
    offsets, voxels = low.shape
    depth, c_out = w.shape
    rows = depth // offsets * (voxels // LOW + 1)
    macs = voxels * depth * c_out * 2 + offsets * voxels * LOW * rows
    hbm = pl.BlockSpec(memory_space=pltpu.HBM)
    return pl.pallas_call(
        forward_kernel,
        out_shape=(
            jax.ShapeDtypeStruct((voxels, c_out), BF),
            jax.ShapeDtypeStruct((padded // 2, c_out), BF),
            jax.ShapeDtypeStruct((padded // 2, c_out), F32),
        ),
        in_specs=[pl.BlockSpec(memory_space=pltpu.SMEM)] + whole(5) + [hbm] + whole(1) + [hbm],
        out_specs=(hbm,) + tuple(whole(2)),
        scratch_shapes=[
            pltpu.VMEM((depth, voxels), BF),
            pltpu.VMEM((rows, LOW), BF),
            pltpu.VMEM((c_out, depth), BF),
            pltpu.VMEM((depth, c_out), BF),
            pltpu.VMEM((voxels, c_out), BF),
            pltpu.VMEM((voxels, c_out), BF),
            pltpu.VMEM((voxels, c_out), BF),
            pltpu.SemaphoreType.DMA,
            pltpu.SemaphoreType.DMA,
            pltpu.SemaphoreType.DMA,
        ],
        compiler_params=pltpu.CompilerParams(vmem_limit_bytes=FULL_LIMIT),
        cost_estimate=pl.CostEstimate(flops=2 * macs, bytes_accessed=5 << 20, transcendentals=0),
    )(flags, got, first, second, low, high, w, bias, cot)


def backward(packed, flags, out, cot, low, high, w, face):
    hbm = pl.BlockSpec(memory_space=pltpu.HBM)
    offsets, voxels = low.shape
    depth, c_out = w.shape
    channels = depth // offsets
    rows = channels * (voxels // LOW + 1)
    macs = voxels * depth * c_out + offsets * voxels * LOW * rows
    return pl.pallas_call(
        functools.partial(backward_kernel, packed),
        out_shape=(
            jax.ShapeDtypeStruct((voxels // LOW * channels, LOW), F32),
            jax.ShapeDtypeStruct((channels, face), BF),
            jax.ShapeDtypeStruct((channels, face), BF),
        ),
        in_specs=[pl.BlockSpec(memory_space=pltpu.SMEM), hbm, hbm] + whole(3),
        out_specs=tuple(whole(3)),
        scratch_shapes=[
            pltpu.VMEM((depth, voxels), BF),
            pltpu.VMEM((rows, LOW), F32),
            pltpu.VMEM((voxels, c_out), BF),
            pltpu.VMEM((voxels, c_out), BF),
            pltpu.VMEM((voxels, c_out), BF),
            pltpu.SemaphoreType.DMA,
            pltpu.SemaphoreType.DMA,
        ],
        compiler_params=pltpu.CompilerParams(vmem_limit_bytes=VMEM_LIMIT),
        cost_estimate=pl.CostEstimate(flops=2 * macs, bytes_accessed=3 << 20, transcendentals=0),
    )(flags, out, cot, low, high, w)


def finish(packed, flags, here, first, second, pick):
    rows, _ = here.shape
    channels, face = first.shape
    return pl.pallas_call(
        functools.partial(finish_kernel, packed),
        out_shape=jax.ShapeDtypeStruct((rows, LOW), BF),
        in_specs=[pl.BlockSpec(memory_space=pltpu.SMEM)] + whole(4),
        out_specs=whole(1)[0],
        scratch_shapes=[pltpu.VMEM((channels, 2 * face), BF)],
        compiler_params=pltpu.CompilerParams(vmem_limit_bytes=SMALL_LIMIT),
        cost_estimate=pl.CostEstimate(flops=4 * rows * LOW * face, bytes_accessed=1 << 20, transcendentals=0),
    )(flags, here, first, second, pick)


def place(side, keep, came, order, channels):
    rows = order.shape[1]
    return pl.pallas_call(
        place_kernel,
        out_shape=jax.ShapeDtypeStruct((channels, rows), BF),
        in_specs=[pl.BlockSpec(memory_space=pltpu.SMEM)] + whole(3),
        out_specs=whole(1)[0],
        scratch_shapes=[pltpu.VMEM((channels, rows), BF)],
        compiler_params=pltpu.CompilerParams(vmem_limit_bytes=SMALL_LIMIT),
        cost_estimate=pl.CostEstimate(flops=2 * rows * rows * channels, bytes_accessed=1 << 20, transcendentals=0),
    )(side, keep, came, order)


def stages(count):
    plan, stride = [], 1
    while stride < count:
        left = count // stride
        radix = 4 if stride > 1 and left % 4 == 0 else 2
        if left % radix:
            radix = left
        plan.append((stride, radix))
        stride *= radix
    return plan


def swapped(array, count, stride, radix, delta):
    def partner(i):
        digit = i // stride % radix
        other = (digit ^ delta) if radix in (2, 4) else (delta - digit) % radix
        return i + (other - digit) * stride

    return lax.ppermute(array, AXES, [(i, partner(i)) for i in range(count)])


def other_digit(digit, delta, radix):
    return (digit ^ delta) if radix in (2, 4) else (delta - digit) % radix


def reduce_stage(x, flat, count, stride, radix):
    digit = flat // stride % radix
    pieces = x.reshape((radix, x.shape[0] // radix) + x.shape[1:])
    total = None
    for delta in range(radix):
        piece = lax.dynamic_index_in_dim(pieces, other_digit(digit, delta, radix), 0, keepdims=False)
        if radix not in (2, 4) or delta:
            piece = swapped(piece, count, stride, radix, delta)
        total = piece.astype(F32) if total is None else total + piece.astype(F32)
    return total.astype(BF)


def by_digit(got, digit, radix):
    parts = []
    for place in range(radix):
        part = got[0]
        for d in range(radix):
            where = (place ^ d) if radix in (2, 4) else (place + d) % radix
            part = jnp.where(digit == d, got[where], part)
        parts.append(part)
    return parts


def joined(parts):
    return parts[0] if len(parts) == 1 else jnp.concatenate(parts, 0)


def gather_stage(parts, flat, count, stride, radix, cargo=lambda delta: None):
    digit = flat // stride % radix
    rows = sum(part.shape[0] for part in parts)
    got, brought = [], {}
    for d in range(radix):
        if radix in (2, 4) and d == 0:
            got.append(joined(parts))
            continue
        extra = cargo(d)
        piece = swapped(joined(parts if extra is None else parts + [extra]), count, stride, radix, d)
        got.append(piece[:rows])
        brought[d] = piece[rows:]
    return by_digit(got, digit, radix), brought


def meet(first, second):
    size = lax.axis_size("brick")
    got = []
    for start, array in ((0, first), (1, second)):
        pairs = []
        for i in range(start, size - 1, 2):
            pairs += [(i, i + 1), (i + 1, i)]
        got.append(lax.ppermute(array, "brick", pairs))
    return got


def on_device(features, order, face_list, face_count, kernel_map, weight, bias, cotangent):
    offsets, channels, c_out = weight.shape
    rows = features.shape[0]
    face = face_list.shape[0] // 2
    bricks = lax.axis_size("brick")
    count = bricks * lax.axis_size("group")
    per = rows // bricks
    depth = offsets * channels
    unit = 8 * count
    padded = -(-depth // unit) * unit

    w = weight.reshape(depth, c_out)
    flat = lax.axis_index("brick") * lax.axis_size("group") + lax.axis_index("group")
    send = send_blocks(features.T, order[None], bricks)
    got = lax.all_to_all(send, "brick", split_axis=0, concat_axis=0)

    slots = jnp.arange(2 * face, dtype=jnp.int32)
    live = jnp.where(slots < face, slots < face_count[0], slots - face < face_count[1])
    pick = one_hot_rows(jnp.where(live, face_list, -1), rows)
    pick, got = lax.optimization_barrier((pick, got))
    local = got.transpose(1, 0, 2).reshape(channels, rows)
    shown = dot(local, pick, 1, 1).astype(BF)
    odd = lax.axis_index("brick") % 2
    down, up = shown[:, :face], shown[:, face:]
    first, second = meet(jnp.where(odd == 1, down, up), jnp.where(odd == 1, up, down))

    flags = jnp.stack([flat % 2, odd]).astype(jnp.int32)
    low = (kernel_map & (LOW - 1)).astype(F32)
    high = lax.shift_right_logical(kernel_map, SHIFT).astype(F32)
    output, give, keep = forward(flags, got, first, second, low, high, w, bias[None], cotangent, padded)
    packed = (bricks, count) == (8, 32) and per * 2 == LOW and channels % 16 == 0
    plan = stages(count)[1:]
    total = (keep + swapped(give, count, 1, 2, 1).astype(F32)).astype(BF)
    total = reduce_stage(total, flat, count, *plan[0])
    here, first, second = backward(packed, flags, output, cotangent, low, high, w, face)
    total, first, second = lax.optimization_barrier((total, first, second))
    first, second = meet(first, second)
    for stride, radix in plan[1:]:
        total = reduce_stage(total, flat, count, stride, radix)

    local_grad = finish(packed, flags, here, first, second, pick)
    if packed:
        part = channels // 2
        total, local_grad = lax.optimization_barrier((total, local_grad))
        local_grad = local_grad.reshape(bricks // 2, channels, LOW)
        z, x = flat // 8, flat // 4 % 2
        cargo = lambda d: lax.dynamic_index_in_dim(local_grad, z ^ d, 0, keepdims=False)
        parts, brought = gather_stage([total], flat, count, 8, 4, cargo)
        mine = jnp.stack(by_digit([cargo(0)] + [brought[d] for d in (1, 2, 3)], z, 4))
        mine = mine.reshape(bricks // 2, 2, part, LOW)
        give = jnp.where(x == 0, mine[:, 1], mine[:, 0]).reshape(-1, LOW)
        keep = jnp.where(x == 0, mine[:, 0], mine[:, 1]).reshape(-1, LOW)
        parts, brought = gather_stage(parts, flat, count, 2, 4, lambda d: give if d == 2 else None)
        came = brought[2]
    else:
        blocks = rows // LOW
        send = local_grad.reshape(blocks, channels, LOW // per, per).transpose(0, 2, 1, 3)
        came = lax.all_to_all(send.reshape(bricks, channels, per), "brick", split_axis=0, concat_axis=0)
        parts = [total]
        for stride, radix in reversed(plan):
            parts, _ = gather_stage(parts, flat, count, stride, radix)
    total = joined(parts)
    total, came = lax.optimization_barrier((total, came))
    if packed:
        grad_in = place(x.astype(jnp.int32)[None], keep, came, order[None], channels).T
    else:
        returned = came.transpose(1, 0, 2).reshape(channels, rows)
        grad_in = dot(returned, one_hot_rows(order, rows), 1, 0).astype(BF).T
    other = swapped(total, count, 1, 2, 1)
    low = jnp.where(flat % 2 == 0, total, other)[: depth // 2]
    high = jnp.where(flat % 2 == 0, other, total)[: depth // 2]
    scale = jnp.float32(1.0 / math.sqrt(count * rows))
    weight_grad = (jnp.concatenate([low, high], 0).astype(F32) * scale).reshape(offsets, channels, c_out)
    return output, grad_in, weight_grad


def solution(mesh):
    return jax.shard_map(
        on_device,
        mesh=mesh,
        in_specs=(
            P(AXES, None),
            P(AXES),
            P(AXES),
            P(AXES),
            P(None, AXES),
            P(),
            P(),
            P(AXES, None),
        ),
        out_specs=(P(AXES, None), P(AXES, None), P()),
        check_vma=False,
    )
```

```python
import functools
import math

import jax
import jax.numpy as jnp
from jax import lax
from jax.experimental import pallas as pl
from jax.experimental.pallas import tpu as pltpu
from jax.sharding import PartitionSpec as P

BF = jnp.bfloat16
F32 = jnp.float32
LOW = 256
SHIFT = 8
VMEM_LIMIT = 20 << 20
SMALL_LIMIT = 6 << 20
FULL_LIMIT = 52 << 20
ALL_LIMIT = 60 << 20
AXES = ("brick", "group")


def dot(a, b, a_dim, b_dim):
    dims = (((a_dim,), (b_dim,)), ((), ()))
    return lax.dot_general(a, b, dims, preferred_element_type=F32)


def one_hot_rows(index, width):
    columns = jnp.arange(width, dtype=jnp.int32)
    return (index[:, None] == columns[None, :]).astype(BF)


def one_hot_low(low, lanes):
    iota = lax.broadcasted_iota(jnp.int32, (LOW, lanes), 0).astype(BF)
    hit = iota == jnp.broadcast_to(low.astype(BF), (LOW, lanes))
    return jnp.where(hit, jnp.ones((), BF), jnp.zeros((), BF))


def send_kernel(feat_hbm, order_hbm, out_ref, feat_ref, order_ref, x_ref, feat_sem, order_sem):
    fetch_feat = pltpu.make_async_copy(feat_hbm, feat_ref, feat_sem)
    fetch_feat.start()
    fetch_order = pltpu.make_async_copy(order_hbm, order_ref, order_sem)
    fetch_order.start()
    channels, rows = feat_ref.shape
    per = out_ref.shape[2]
    fetch_feat.wait()
    fetch_order.wait()
    for a in range(rows // LOW):
        x_ref[a * channels : (a + 1) * channels, :] = feat_ref[:, a * LOW : (a + 1) * LOW]
    for n in range(rows // LOW):
        row = order_ref[:, n * LOW : (n + 1) * LOW]
        terms = dot(x_ref[...], one_hot_low((row & (LOW - 1)).astype(F32), LOW), 1, 0)
        block = jnp.broadcast_to(lax.shift_right_logical(row, SHIFT), (channels, LOW))
        picked = terms[:channels]
        for a in range(1, rows // LOW):
            picked = jnp.where(block == a, terms[a * channels : (a + 1) * channels], picked)
        picked = picked.astype(BF)
        for p in range(LOW // per):
            out_ref[n * (LOW // per) + p] = picked[:, p * per : (p + 1) * per]


def sides(odd, first_ref, second_ref):
    first, second = first_ref[...].astype(F32), second_ref[...].astype(F32)
    low = jnp.where(odd == 1, first, second)
    high = jnp.where(odd == 1, second, first)
    return low.astype(BF), high.astype(BF)


def forward_kernel(
    flag_ref, got_ref, even_ref, odd_ref, low_ref, high_ref, w_hbm, bias_ref, cot_hbm, out_hbm, send_hbm, keep_hbm,
    g_ref, x_ref, wt_ref, w_ref, cot_ref, out_ref, pg_ref, send_ref, keep_ref, w_sem, cot_sem, out_sem, grad_sems,
):
    fetch_w = pltpu.make_async_copy(w_hbm, w_ref, w_sem)
    fetch_w.start()
    fetch_cot = pltpu.make_async_copy(cot_hbm, cot_ref, cot_sem)
    fetch_cot.start()
    offsets, voxels = low_ref.shape
    depth, c_out = w_ref.shape
    channels = depth // offsets
    here = voxels // LOW
    blocks = x_ref.shape[0] // channels
    center = offsets // 2
    per = got_ref.shape[2]
    for a in range(here):
        for p in range(LOW // per):
            x_ref[a * channels : (a + 1) * channels, p * per : (p + 1) * per] = got_ref[a * (LOW // per) + p]
    face = even_ref.shape[1]
    prev, after = sides(flag_ref[1], even_ref, odd_ref)
    x_ref[here * channels :, :face] = prev
    x_ref[here * channels :, face:] = after
    ready = offsets // 3
    for k in range(offsets):
        if k == ready:
            fetch_w.wait()
            fetch_cot.wait()
        for j in range(2 * (k - ready), min(2 * (k - ready + 1), offsets)) if k >= ready else ():
            wt_ref[:, j * channels : (j + 1) * channels] = w_ref[j * channels : (j + 1) * channels, :].T
        at = slice(k * channels, (k + 1) * channels)
        if k == center:
            for a in range(here):
                g_ref[at, a * LOW : (a + 1) * LOW] = x_ref[a * channels : (a + 1) * channels, :]
            continue
        low, high = low_ref[k : k + 1, :], high_ref[k : k + 1, :]
        for n in range(here):
            sl = slice(n * LOW, (n + 1) * LOW)
            terms = dot(x_ref[...], one_hot_low(low[:, sl], LOW), 1, 0)
            block = jnp.broadcast_to(high[:, sl], (channels, LOW))
            picked = jnp.zeros((channels, LOW), F32)
            for a in range(blocks):
                picked = jnp.where(block == a, terms[a * channels : (a + 1) * channels], picked)
            g_ref[at, sl] = picked.astype(BF)
    for n in range(here):
        sl = slice(n * LOW, (n + 1) * LOW)
        pre = dot(wt_ref[...], g_ref[:, sl], 1, 0).T + bias_ref[...]
        out_ref[sl, :] = jnp.maximum(pre, 0.0).astype(BF)
        pg_ref[sl, :] = jnp.where(pre > 0, cot_ref[sl, :].astype(F32), 0.0).astype(BF)
    store = pltpu.make_async_copy(out_ref, out_hbm, out_sem)
    store.start()
    half = flag_ref[0]
    count = depth // 2
    stores = [store]
    for ref, to, which in ((send_ref, send_hbm, 1 - half), (keep_ref, keep_hbm, half)):
        ref[count:, :] = jnp.zeros((ref.shape[0] - count, c_out), ref.dtype)
        for m in range(0, count, 288):
            step = min(288, count - m)
            at = pl.ds(pl.multiple_of(which * count + m, 16), step)
            ref[m : m + step, :] = dot(g_ref[at, :], pg_ref[...], 1, 0).astype(ref.dtype)
            end = ref.shape[0] if m + step == count else m + step
            store = pltpu.make_async_copy(ref.at[m:end, :], to.at[m:end, :], grad_sems.at[len(stores) - 1])
            store.start()
            stores.append(store)
    for store in stores:
        store.wait()


def backward_kernel(
    packed, flag_ref, out_ref, cot_ref, low_ref, high_ref, w_ref, here_ref, first_ref, second_ref, c_ref, acc_ref, pg_ref
):
    offsets, voxels = low_ref.shape
    depth = w_ref.shape[0]
    channels = depth // offsets
    here = voxels // LOW
    blocks = acc_ref.shape[0] // channels
    pg_ref[...] = jnp.where(out_ref[...] > 0, cot_ref[...], jnp.zeros((), BF))
    step = depth // 9
    for m in range(9):
        sl = slice(m * step, (m + 1) * step)
        c_ref[sl, :] = dot(w_ref[sl, :], pg_ref[...], 1, 1).astype(BF)
    center = offsets // 2
    for a in range(here):
        at = slice(a * channels, (a + 1) * channels)
        acc_ref[at, :] = c_ref[center * channels : (center + 1) * channels, a * LOW : (a + 1) * LOW].astype(F32)
    acc_ref[here * channels :, :] = jnp.zeros((channels * (blocks - here), LOW), F32)
    for k in range(offsets):
        if k == center:
            continue
        contrib = c_ref[k * channels : (k + 1) * channels, :]
        low, high = low_ref[k : k + 1, :], high_ref[k : k + 1, :]
        block = jnp.broadcast_to(high.astype(BF), (channels, voxels))
        parts = [jnp.where(block == jnp.array(a, BF), contrib, jnp.zeros((), BF)) for a in range(blocks)]
        acc_ref[...] += dot(jnp.concatenate(parts, 0), one_hot_low(low, voxels), 1, 1)
    if packed:
        part, per = channels // 2, LOW // 2
        for a in range(here):
            for p in range(2):
                for h in range(2):
                    at = slice(a * channels + h * part, a * channels + (h + 1) * part)
                    to = slice((2 * a + p) * part, (2 * a + p + 1) * part)
                    here_ref[to, h * per : (h + 1) * per] = acc_ref[at, p * per : (p + 1) * per]
    else:
        here_ref[...] = acc_ref[: here * channels, :]
    face = first_ref.shape[1]
    down, up = acc_ref[here * channels :, :face], acc_ref[here * channels :, face:]
    odd = flag_ref[1]
    first_ref[...] = jnp.where(odd == 1, down, up).astype(BF)
    second_ref[...] = jnp.where(odd == 1, up, down).astype(BF)


def finish_kernel(packed, flag_ref, here_ref, first_ref, second_ref, pick_ref, out_ref, from_ref):
    channels, face = first_ref.shape
    blocks = here_ref.shape[0] // channels
    prev, after = sides(flag_ref[1], first_ref, second_ref)
    from_ref[:, :face] = prev
    from_ref[:, face:] = after
    part, per = channels // 2, LOW // 2
    for a in range(blocks):
        added = dot(from_ref[...], pick_ref[:, a * LOW : (a + 1) * LOW], 1, 0)
        if not packed:
            at = slice(a * channels, (a + 1) * channels)
            out_ref[at, :] = (here_ref[at, :] + added).astype(BF)
            continue
        for p in range(2):
            at = slice((2 * a + p) * part, (2 * a + p + 1) * part)
            for h in range(2):
                lanes = slice(h * per, (h + 1) * per)
                term = added[h * part : (h + 1) * part, p * per : (p + 1) * per]
                out_ref[at, lanes] = (here_ref[at, lanes] + term).astype(BF)


def place_kernel(z_ref, *refs):
    came_refs, (order_ref, out_ref, back_ref) = refs[:-3], refs[-3:]
    channels, rows = out_ref.shape
    part, per = channels // 2, LOW // 2
    for d, came_ref in enumerate(came_refs):
        base = (z_ref[0] ^ d) * LOW
        for p in range(2):
            lanes = pl.ds(pl.multiple_of(base + p * per, per), per)
            for h in range(2):
                back_ref[h * part : (h + 1) * part, lanes] = came_ref[p * part : (p + 1) * part, h * per : (h + 1) * per]
    row = order_ref[...]
    block = jnp.broadcast_to(lax.shift_right_logical(row, SHIFT).astype(F32).astype(BF), (channels, rows))
    back = back_ref[...]
    parts = [jnp.where(block == jnp.array(a, BF), back, jnp.zeros((), BF)) for a in range(rows // LOW)]
    placed = dot(jnp.concatenate(parts, 0), one_hot_low((row & (LOW - 1)).astype(F32), rows), 1, 1)
    for a in range(rows // LOW):
        out_ref[:, a * LOW : (a + 1) * LOW] = placed[a * channels : (a + 1) * channels].astype(BF)


def whole(count):
    return [pl.BlockSpec(memory_space=pltpu.VMEM)] * count


def send_blocks(features, order, bricks):
    channels, rows = features.shape
    hbm = pl.BlockSpec(memory_space=pltpu.HBM)
    return pl.pallas_call(
        send_kernel,
        out_shape=jax.ShapeDtypeStruct((bricks, channels, rows // bricks), BF),
        in_specs=[hbm, hbm],
        out_specs=whole(1)[0],
        scratch_shapes=[
            pltpu.VMEM((channels, rows), BF),
            pltpu.VMEM((1, rows), jnp.int32),
            pltpu.VMEM((channels * rows // LOW, LOW), BF),
            pltpu.SemaphoreType.DMA,
            pltpu.SemaphoreType.DMA,
        ],
        compiler_params=pltpu.CompilerParams(vmem_limit_bytes=ALL_LIMIT),
        cost_estimate=pl.CostEstimate(flops=2 * rows * rows * channels, bytes_accessed=1 << 19, transcendentals=0),
    )(features, order)


def forward(flags, got, first, second, low, high, w, bias, cot, padded):
    offsets, voxels = low.shape
    depth, c_out = w.shape
    rows = depth // offsets * (voxels // LOW + 1)
    macs = voxels * depth * c_out * 2 + offsets * voxels * LOW * rows
    hbm = pl.BlockSpec(memory_space=pltpu.HBM)
    return pl.pallas_call(
        forward_kernel,
        out_shape=(
            jax.ShapeDtypeStruct((voxels, c_out), BF),
            jax.ShapeDtypeStruct((padded // 2, c_out), BF),
            jax.ShapeDtypeStruct((padded // 2, c_out), F32),
        ),
        in_specs=[pl.BlockSpec(memory_space=pltpu.SMEM)] + whole(5) + [hbm] + whole(1) + [hbm],
        out_specs=(hbm, hbm, hbm),
        scratch_shapes=[
            pltpu.VMEM((depth, voxels), BF),
            pltpu.VMEM((rows, LOW), BF),
            pltpu.VMEM((c_out, depth), BF),
            pltpu.VMEM((depth, c_out), BF),
            pltpu.VMEM((voxels, c_out), BF),
            pltpu.VMEM((voxels, c_out), BF),
            pltpu.VMEM((voxels, c_out), BF),
            pltpu.VMEM((padded // 2, c_out), BF),
            pltpu.VMEM((padded // 2, c_out), F32),
            pltpu.SemaphoreType.DMA,
            pltpu.SemaphoreType.DMA,
            pltpu.SemaphoreType.DMA,
            pltpu.SemaphoreType.DMA((2 * pl.cdiv(depth // 2, 288),)),
        ],
        compiler_params=pltpu.CompilerParams(vmem_limit_bytes=FULL_LIMIT),
        cost_estimate=pl.CostEstimate(flops=2 * macs, bytes_accessed=5 << 20, transcendentals=0),
    )(flags, got, first, second, low, high, w, bias, cot)


def backward(packed, flags, out, cot, low, high, w, face):
    offsets, voxels = low.shape
    depth, c_out = w.shape
    channels = depth // offsets
    rows = channels * (voxels // LOW + 1)
    macs = voxels * depth * c_out + offsets * voxels * LOW * rows
    return pl.pallas_call(
        functools.partial(backward_kernel, packed),
        out_shape=(
            jax.ShapeDtypeStruct((voxels // LOW * channels, LOW), F32),
            jax.ShapeDtypeStruct((channels, face), BF),
            jax.ShapeDtypeStruct((channels, face), BF),
        ),
        in_specs=[pl.BlockSpec(memory_space=pltpu.SMEM)] + whole(5),
        out_specs=tuple(whole(3)),
        scratch_shapes=[
            pltpu.VMEM((depth, voxels), BF),
            pltpu.VMEM((rows, LOW), F32),
            pltpu.VMEM((voxels, c_out), BF),
        ],
        compiler_params=pltpu.CompilerParams(vmem_limit_bytes=VMEM_LIMIT),
        cost_estimate=pl.CostEstimate(flops=2 * macs, bytes_accessed=3 << 20, transcendentals=0),
    )(flags, out, cot, low, high, w)


def finish(packed, flags, here, first, second, pick):
    rows, _ = here.shape
    channels, face = first.shape
    return pl.pallas_call(
        functools.partial(finish_kernel, packed),
        out_shape=jax.ShapeDtypeStruct((rows, LOW), BF),
        in_specs=[pl.BlockSpec(memory_space=pltpu.SMEM)] + whole(4),
        out_specs=whole(1)[0],
        scratch_shapes=[pltpu.VMEM((channels, 2 * face), BF)],
        compiler_params=pltpu.CompilerParams(vmem_limit_bytes=SMALL_LIMIT),
        cost_estimate=pl.CostEstimate(flops=4 * rows * LOW * face, bytes_accessed=1 << 20, transcendentals=0),
    )(flags, here, first, second, pick)


def place(z, came, order, channels):
    rows = order.shape[1]
    return pl.pallas_call(
        place_kernel,
        out_shape=jax.ShapeDtypeStruct((channels, rows), BF),
        in_specs=[pl.BlockSpec(memory_space=pltpu.SMEM)] + whole(len(came) + 1),
        out_specs=whole(1)[0],
        scratch_shapes=[pltpu.VMEM((channels, rows), BF)],
        compiler_params=pltpu.CompilerParams(vmem_limit_bytes=SMALL_LIMIT),
        cost_estimate=pl.CostEstimate(flops=2 * rows * rows * channels, bytes_accessed=1 << 20, transcendentals=0),
    )(z, *came, order)


def stages(count):
    plan, stride = [], 1
    while stride < count:
        left = count // stride
        radix = 4 if stride > 1 and left % 4 == 0 else 2
        if left % radix:
            radix = left
        plan.append((stride, radix))
        stride *= radix
    return plan


def swapped(array, count, stride, radix, delta):
    def partner(i):
        digit = i // stride % radix
        other = (digit ^ delta) if radix in (2, 4) else (delta - digit) % radix
        return i + (other - digit) * stride

    return lax.ppermute(array, AXES, [(i, partner(i)) for i in range(count)])


def other_digit(digit, delta, radix):
    return (digit ^ delta) if radix in (2, 4) else (delta - digit) % radix


def reduce_stage(x, flat, count, stride, radix):
    digit = flat // stride % radix
    pieces = x.reshape((radix, x.shape[0] // radix) + x.shape[1:])
    total = None
    for delta in range(radix):
        piece = lax.dynamic_index_in_dim(pieces, other_digit(digit, delta, radix), 0, keepdims=False)
        if radix not in (2, 4) or delta:
            piece = swapped(piece, count, stride, radix, delta)
        total = piece.astype(F32) if total is None else total + piece.astype(F32)
    return total.astype(BF)


def by_digit(got, digit, radix):
    parts = []
    for place in range(radix):
        part = got[0]
        for d in range(radix):
            where = (place ^ d) if radix in (2, 4) else (place + d) % radix
            part = jnp.where(digit == d, got[where], part)
        parts.append(part)
    return parts


def joined(parts):
    return parts[0] if len(parts) == 1 else jnp.concatenate(parts, 0)


def gather_stage(x, flat, count, stride, radix):
    digit = flat // stride % radix
    got = [x if radix in (2, 4) and d == 0 else swapped(x, count, stride, radix, d) for d in range(radix)]
    return by_digit(got, digit, radix)


def meet(first, second):
    size = lax.axis_size("brick")
    got = []
    for start, array in ((0, first), (1, second)):
        pairs = []
        for i in range(start, size - 1, 2):
            pairs += [(i, i + 1), (i + 1, i)]
        got.append(lax.ppermute(array, "brick", pairs))
    return got


def on_device(features, order, face_list, face_count, kernel_map, weight, bias, cotangent):
    offsets, channels, c_out = weight.shape
    rows = features.shape[0]
    face = face_list.shape[0] // 2
    bricks = lax.axis_size("brick")
    count = bricks * lax.axis_size("group")
    per = rows // bricks
    depth = offsets * channels
    unit = 8 * count
    padded = -(-depth // unit) * unit

    w = weight.reshape(depth, c_out)
    flat = lax.axis_index("brick") * lax.axis_size("group") + lax.axis_index("group")
    send = send_blocks(features.T, order[None], bricks)
    got = lax.all_to_all(send, "brick", split_axis=0, concat_axis=0)

    slots = jnp.arange(2 * face, dtype=jnp.int32)
    live = jnp.where(slots < face, slots < face_count[0], slots - face < face_count[1])
    pick = one_hot_rows(jnp.where(live, face_list, -1), rows)
    pick, got = lax.optimization_barrier((pick, got))
    local = got.transpose(1, 0, 2).reshape(channels, rows)
    shown = dot(local, pick, 1, 1).astype(BF)
    odd = lax.axis_index("brick") % 2
    down, up = shown[:, :face], shown[:, face:]
    first, second = meet(jnp.where(odd == 1, down, up), jnp.where(odd == 1, up, down))

    flags = jnp.stack([flat % 2, odd]).astype(jnp.int32)
    low = (kernel_map & (LOW - 1)).astype(F32)
    high = lax.shift_right_logical(kernel_map, SHIFT).astype(F32)
    output, give, keep = forward(flags, got, first, second, low, high, w, bias[None], cotangent, padded)
    packed = (bricks, count) == (8, 32) and per * 2 == LOW and channels % 16 == 0
    plan = stages(count)[1:]
    total = (keep + swapped(give, count, 1, 2, 1).astype(F32)).astype(BF)
    total = reduce_stage(total, flat, count, *plan[0])
    here, first, second = backward(packed, flags, output, cotangent, low, high, w, face)
    total, first, second = lax.optimization_barrier((total, first, second))
    first, second = meet(first, second)
    for stride, radix in plan[1:]:
        total = reduce_stage(total, flat, count, stride, radix)

    local_grad = finish(packed, flags, here, first, second, pick)
    if packed:
        part = channels // 2
        total, local_grad = lax.optimization_barrier((total, local_grad))
        z, x = flat // 8, flat // 4 % 2
        cargo = local_grad.reshape(bricks // 2, 2, part, LOW)
        keep = jnp.where(x == 0, cargo[:, 0], cargo[:, 1])
        give = jnp.where(x == 0, cargo[:, 1], cargo[:, 0])
        came = swapped(give.reshape(-1, LOW), count, 4, 2, 1).reshape(keep.shape)
        cargo = jnp.stack([jnp.where(x == 0, keep, came), jnp.where(x == 0, came, keep)], 1)
        cargo = cargo.reshape(bricks // 2, channels, LOW)
        parts = gather_stage(total, flat, count, 8, 4)
        total, cargo = lax.optimization_barrier((joined(parts), cargo))
        came = [lax.dynamic_index_in_dim(cargo, z ^ d, 0, keepdims=False) for d in range(4)]
        came = came[:1] + [swapped(came[d], count, 8, 4, d) for d in (1, 2, 3)]
        parts = gather_stage(total, flat, count, 2, 4)
    else:
        blocks = rows // LOW
        send = local_grad.reshape(blocks, channels, LOW // per, per).transpose(0, 2, 1, 3)
        came = lax.all_to_all(send.reshape(bricks, channels, per), "brick", split_axis=0, concat_axis=0)
        parts = [total]
        for stride, radix in reversed(plan):
            parts = gather_stage(joined(parts), flat, count, stride, radix)
    total = joined(parts)
    total, came = lax.optimization_barrier((total, came))
    if packed:
        grad_in = place(z.astype(jnp.int32)[None], came, order[None], channels).T
    else:
        returned = came.transpose(1, 0, 2).reshape(channels, rows)
        grad_in = dot(returned, one_hot_rows(order, rows), 1, 0).astype(BF).T
    other = swapped(total, count, 1, 2, 1)
    low = jnp.where(flat % 2 == 0, total, other)[: depth // 2]
    high = jnp.where(flat % 2 == 0, other, total)[: depth // 2]
    scale = jnp.float32(1.0 / math.sqrt(count * rows))
    weight_grad = (jnp.concatenate([low, high], 0).astype(F32) * scale).reshape(offsets, channels, c_out)
    return output, grad_in, weight_grad


def solution(mesh):
    return jax.shard_map(
        on_device,
        mesh=mesh,
        in_specs=(
            P(AXES, None),
            P(AXES),
            P(AXES),
            P(AXES),
            P(None, AXES),
            P(),
            P(),
            P(AXES, None),
        ),
        out_specs=(P(AXES, None), P(AXES, None), P()),
        check_vma=False,
    )
```

```python
import functools
import math

import jax
import jax.numpy as jnp
from jax import lax
from jax.experimental import pallas as pl
from jax.experimental.pallas import tpu as pltpu
from jax.sharding import PartitionSpec as P

BF = jnp.bfloat16
F32 = jnp.float32
LOW = 256
SHIFT = 8
VMEM_LIMIT = 53 << 20
SMALL_LIMIT = 6 << 20
FULL_LIMIT = 51 << 20
ALL_LIMIT = 60 << 20
AXES = ("brick", "group")


def dot(a, b, a_dim, b_dim):
    dims = (((a_dim,), (b_dim,)), ((), ()))
    return lax.dot_general(a, b, dims, preferred_element_type=F32)


def one_hot_rows(index, width):
    columns = jnp.arange(width, dtype=jnp.int32)
    return (index[:, None] == columns[None, :]).astype(BF)


def one_hot_low(low, lanes):
    iota = lax.broadcasted_iota(jnp.int32, (LOW, lanes), 0).astype(BF)
    hit = iota == jnp.broadcast_to(low.astype(BF), (LOW, lanes))
    return jnp.where(hit, jnp.ones((), BF), jnp.zeros((), BF))


def send_kernel(feat_hbm, order_hbm, out_ref, feat_ref, order_ref, x_ref, feat_sem, order_sem):
    fetch_feat = pltpu.make_async_copy(feat_hbm, feat_ref, feat_sem)
    fetch_feat.start()
    fetch_order = pltpu.make_async_copy(order_hbm, order_ref, order_sem)
    fetch_order.start()
    channels, rows = feat_ref.shape
    per = out_ref.shape[2]
    fetch_feat.wait()
    fetch_order.wait()
    for a in range(rows // LOW):
        x_ref[a * channels : (a + 1) * channels, :] = feat_ref[:, a * LOW : (a + 1) * LOW]
    for n in range(rows // LOW):
        row = order_ref[:, n * LOW : (n + 1) * LOW]
        terms = dot(x_ref[...], one_hot_low((row & (LOW - 1)).astype(F32), LOW), 1, 0)
        block = jnp.broadcast_to(lax.shift_right_logical(row, SHIFT), (channels, LOW))
        picked = terms[:channels]
        for a in range(1, rows // LOW):
            picked = jnp.where(block == a, terms[a * channels : (a + 1) * channels], picked)
        picked = picked.astype(BF)
        for p in range(LOW // per):
            out_ref[n * (LOW // per) + p] = picked[:, p * per : (p + 1) * per]


def sides(odd, first_ref, second_ref):
    first, second = first_ref[...].astype(F32), second_ref[...].astype(F32)
    low = jnp.where(odd == 1, first, second)
    high = jnp.where(odd == 1, second, first)
    return low.astype(BF), high.astype(BF)


def forward_kernel(
    flag_ref, got_ref, even_ref, odd_ref, low_ref, high_ref, w_hbm, bias_ref, cot_hbm, out_hbm, send_ref, keep_ref,
    g_ref, x_ref, wt_ref, w_ref, cot_ref, out_ref, pg_ref, w_sem, cot_sem, out_sem,
):
    fetch_w = pltpu.make_async_copy(w_hbm, w_ref, w_sem)
    fetch_w.start()
    fetch_cot = pltpu.make_async_copy(cot_hbm, cot_ref, cot_sem)
    fetch_cot.start()
    offsets, voxels = low_ref.shape
    depth, c_out = w_ref.shape
    channels = depth // offsets
    here = voxels // LOW
    blocks = x_ref.shape[0] // channels
    center = offsets // 2
    per = got_ref.shape[2]
    for a in range(here):
        for p in range(LOW // per):
            x_ref[a * channels : (a + 1) * channels, p * per : (p + 1) * per] = got_ref[a * (LOW // per) + p]
    face = even_ref.shape[1]
    prev, after = sides(flag_ref[1], even_ref, odd_ref)
    x_ref[here * channels :, :face] = prev
    x_ref[here * channels :, face:] = after
    ready = offsets // 3
    for k in range(offsets):
        if k == ready:
            fetch_w.wait()
            fetch_cot.wait()
        for j in range(2 * (k - ready), min(2 * (k - ready + 1), offsets)) if k >= ready else ():
            wt_ref[:, j * channels : (j + 1) * channels] = w_ref[j * channels : (j + 1) * channels, :].T
        at = slice(k * channels, (k + 1) * channels)
        if k == center:
            for a in range(here):
                g_ref[at, a * LOW : (a + 1) * LOW] = x_ref[a * channels : (a + 1) * channels, :]
            continue
        low, high = low_ref[k : k + 1, :], high_ref[k : k + 1, :]
        for n in range(here):
            sl = slice(n * LOW, (n + 1) * LOW)
            terms = dot(x_ref[...], one_hot_low(low[:, sl], LOW), 1, 0)
            block = jnp.broadcast_to(high[:, sl], (channels, LOW))
            picked = jnp.zeros((channels, LOW), F32)
            for a in range(blocks):
                picked = jnp.where(block == a, terms[a * channels : (a + 1) * channels], picked)
            g_ref[at, sl] = picked.astype(BF)
    for n in range(here):
        sl = slice(n * LOW, (n + 1) * LOW)
        pre = dot(wt_ref[...], g_ref[:, sl], 1, 0).T + bias_ref[...]
        out_ref[sl, :] = jnp.maximum(pre, 0.0).astype(BF)
        pg_ref[sl, :] = jnp.where(pre > 0, cot_ref[sl, :].astype(F32), 0.0).astype(BF)
    store = pltpu.make_async_copy(out_ref, out_hbm, out_sem)
    store.start()
    half = flag_ref[0]
    count = depth // 2
    for ref, which in ((send_ref, 1 - half), (keep_ref, half)):
        for m in range(0, count, 288):
            step = min(288, count - m)
            at = pl.ds(pl.multiple_of(which * count + m, 16), step)
            ref[m : m + step, :] = dot(g_ref[at, :], pg_ref[...], 1, 0).astype(ref.dtype)
        ref[count:, :] = jnp.zeros((ref.shape[0] - count, c_out), ref.dtype)
    store.wait()


def backward_kernel(
    packed, flag_ref, out_hbm, cot_hbm, low_ref, high_ref, w_ref, here_ref, first_ref, second_ref,
    c_ref, acc_ref, pg_ref, out_ref, cot_ref, out_sem, cot_sem,
):
    fetch_out = pltpu.make_async_copy(out_hbm, out_ref, out_sem)
    fetch_out.start()
    fetch_cot = pltpu.make_async_copy(cot_hbm, cot_ref, cot_sem)
    fetch_cot.start()
    offsets, voxels = low_ref.shape
    depth = w_ref.shape[0]
    channels = depth // offsets
    here = voxels // LOW
    blocks = acc_ref.shape[0] // channels
    fetch_out.wait()
    fetch_cot.wait()
    pg_ref[...] = jnp.where(out_ref[...] > 0, cot_ref[...], jnp.zeros((), BF))
    step = depth // 9
    for m in range(9):
        sl = slice(m * step, (m + 1) * step)
        c_ref[sl, :] = dot(w_ref[sl, :], pg_ref[...], 1, 1).astype(BF)
    center = offsets // 2
    for a in range(here):
        at = slice(a * channels, (a + 1) * channels)
        acc_ref[at, :] = c_ref[center * channels : (center + 1) * channels, a * LOW : (a + 1) * LOW].astype(F32)
    acc_ref[here * channels :, :] = jnp.zeros((channels * (blocks - here), LOW), F32)
    for k in range(offsets):
        if k == center:
            continue
        contrib = c_ref[k * channels : (k + 1) * channels, :]
        low, high = low_ref[k : k + 1, :], high_ref[k : k + 1, :]
        block = jnp.broadcast_to(high.astype(BF), (channels, voxels))
        parts = [jnp.where(block == jnp.array(a, BF), contrib, jnp.zeros((), BF)) for a in range(blocks)]
        acc_ref[...] += dot(jnp.concatenate(parts, 0), one_hot_low(low, voxels), 1, 1)
    if packed:
        part, per = channels // 2, LOW // 2
        for a in range(here):
            for p in range(2):
                for h in range(2):
                    at = slice(a * channels + h * part, a * channels + (h + 1) * part)
                    to = slice((2 * a + p) * part, (2 * a + p + 1) * part)
                    here_ref[to, h * per : (h + 1) * per] = acc_ref[at, p * per : (p + 1) * per]
    else:
        here_ref[...] = acc_ref[: here * channels, :]
    face = first_ref.shape[1]
    down, up = acc_ref[here * channels :, :face], acc_ref[here * channels :, face:]
    odd = flag_ref[1]
    first_ref[...] = jnp.where(odd == 1, down, up).astype(BF)
    second_ref[...] = jnp.where(odd == 1, up, down).astype(BF)


def finish_kernel(packed, flag_ref, here_ref, first_ref, second_ref, pick_ref, out_ref, from_ref):
    channels, face = first_ref.shape
    blocks = here_ref.shape[0] // channels
    prev, after = sides(flag_ref[1], first_ref, second_ref)
    from_ref[:, :face] = prev
    from_ref[:, face:] = after
    part, per = channels // 2, LOW // 2
    for a in range(blocks):
        added = dot(from_ref[...], pick_ref[:, a * LOW : (a + 1) * LOW], 1, 0)
        if not packed:
            at = slice(a * channels, (a + 1) * channels)
            out_ref[at, :] = (here_ref[at, :] + added).astype(BF)
            continue
        for p in range(2):
            at = slice((2 * a + p) * part, (2 * a + p + 1) * part)
            for h in range(2):
                lanes = slice(h * per, (h + 1) * per)
                term = added[h * part : (h + 1) * part, p * per : (p + 1) * per]
                out_ref[at, lanes] = (here_ref[at, lanes] + term).astype(BF)


def place_kernel(side_ref, keep_ref, came_ref, order_ref, out_ref, back_ref):
    channels, rows = out_ref.shape
    part, per = channels // 2, LOW // 2
    side = side_ref[0]
    for z in range(rows // LOW):
        at = slice(z * part, (z + 1) * part)
        for p in range(2):
            block = jnp.where(side == p, keep_ref[at, :].astype(F32), came_ref[at, :].astype(F32)).astype(BF)
            lanes = slice((2 * z + p) * per, (2 * z + p + 1) * per)
            for h in range(2):
                back_ref[h * part : (h + 1) * part, lanes] = block[:, h * per : (h + 1) * per]
    row = order_ref[...]
    block = jnp.broadcast_to(lax.shift_right_logical(row, SHIFT).astype(F32).astype(BF), (channels, rows))
    back = back_ref[...]
    parts = [jnp.where(block == jnp.array(a, BF), back, jnp.zeros((), BF)) for a in range(rows // LOW)]
    placed = dot(jnp.concatenate(parts, 0), one_hot_low((row & (LOW - 1)).astype(F32), rows), 1, 1)
    for a in range(rows // LOW):
        out_ref[:, a * LOW : (a + 1) * LOW] = placed[a * channels : (a + 1) * channels].astype(BF)


def halve_kernel(digit_ref, keep_ref, got_ref, *out_refs):
    rows = out_refs[0].shape[0]
    for d, out_ref in enumerate(out_refs):
        at = pl.ds(pl.multiple_of((digit_ref[0] ^ d) * rows, 16), rows)
        out_ref[...] = (keep_ref[at, :].astype(F32) + got_ref[at, :].astype(F32)).astype(out_ref.dtype)


def whole(count):
    return [pl.BlockSpec(memory_space=pltpu.VMEM)] * count


def send_blocks(features, order, bricks):
    channels, rows = features.shape
    hbm = pl.BlockSpec(memory_space=pltpu.HBM)
    return pl.pallas_call(
        send_kernel,
        out_shape=jax.ShapeDtypeStruct((bricks, channels, rows // bricks), BF),
        in_specs=[hbm, hbm],
        out_specs=whole(1)[0],
        scratch_shapes=[
            pltpu.VMEM((channels, rows), BF),
            pltpu.VMEM((1, rows), jnp.int32),
            pltpu.VMEM((channels * rows // LOW, LOW), BF),
            pltpu.SemaphoreType.DMA,
            pltpu.SemaphoreType.DMA,
        ],
        compiler_params=pltpu.CompilerParams(vmem_limit_bytes=ALL_LIMIT),
        cost_estimate=pl.CostEstimate(flops=2 * rows * rows * channels, bytes_accessed=1 << 19, transcendentals=0),
    )(features, order)


def forward(flags, got, first, second, low, high, w, bias, cot, padded):
    offsets, voxels = low.shape
    depth, c_out = w.shape
    rows = depth // offsets * (voxels // LOW + 1)
    macs = voxels * depth * c_out * 2 + offsets * voxels * LOW * rows
    hbm = pl.BlockSpec(memory_space=pltpu.HBM)
    return pl.pallas_call(
        forward_kernel,
        out_shape=(
            jax.ShapeDtypeStruct((voxels, c_out), BF),
            jax.ShapeDtypeStruct((padded // 2, c_out), BF),
            jax.ShapeDtypeStruct((padded // 2, c_out), BF),
        ),
        in_specs=[pl.BlockSpec(memory_space=pltpu.SMEM)] + whole(5) + [hbm] + whole(1) + [hbm],
        out_specs=(hbm,) + tuple(whole(2)),
        scratch_shapes=[
            pltpu.VMEM((depth, voxels), BF),
            pltpu.VMEM((rows, LOW), BF),
            pltpu.VMEM((c_out, depth), BF),
            pltpu.VMEM((depth, c_out), BF),
            pltpu.VMEM((voxels, c_out), BF),
            pltpu.VMEM((voxels, c_out), BF),
            pltpu.VMEM((voxels, c_out), BF),
            pltpu.SemaphoreType.DMA,
            pltpu.SemaphoreType.DMA,
            pltpu.SemaphoreType.DMA,
        ],
        compiler_params=pltpu.CompilerParams(vmem_limit_bytes=FULL_LIMIT),
        cost_estimate=pl.CostEstimate(flops=2 * macs, bytes_accessed=5 << 20, transcendentals=0),
    )(flags, got, first, second, low, high, w, bias, cot)


def backward(packed, flags, out, cot, low, high, w, face):
    hbm = pl.BlockSpec(memory_space=pltpu.HBM)
    offsets, voxels = low.shape
    depth, c_out = w.shape
    channels = depth // offsets
    rows = channels * (voxels // LOW + 1)
    macs = voxels * depth * c_out + offsets * voxels * LOW * rows
    return pl.pallas_call(
        functools.partial(backward_kernel, packed),
        out_shape=(
            jax.ShapeDtypeStruct((voxels // LOW * channels, LOW), F32),
            jax.ShapeDtypeStruct((channels, face), BF),
            jax.ShapeDtypeStruct((channels, face), BF),
        ),
        in_specs=[pl.BlockSpec(memory_space=pltpu.SMEM), hbm, hbm] + whole(3),
        out_specs=tuple(whole(3)),
        scratch_shapes=[
            pltpu.VMEM((depth, voxels), BF),
            pltpu.VMEM((rows, LOW), F32),
            pltpu.VMEM((voxels, c_out), BF),
            pltpu.VMEM((voxels, c_out), BF),
            pltpu.VMEM((voxels, c_out), BF),
            pltpu.SemaphoreType.DMA,
            pltpu.SemaphoreType.DMA,
        ],
        compiler_params=pltpu.CompilerParams(vmem_limit_bytes=VMEM_LIMIT),
        cost_estimate=pl.CostEstimate(flops=2 * macs, bytes_accessed=3 << 20, transcendentals=0),
    )(flags, out, cot, low, high, w)


def finish(packed, flags, here, first, second, pick):
    rows, _ = here.shape
    channels, face = first.shape
    return pl.pallas_call(
        functools.partial(finish_kernel, packed),
        out_shape=jax.ShapeDtypeStruct((rows, LOW), BF),
        in_specs=[pl.BlockSpec(memory_space=pltpu.SMEM)] + whole(4),
        out_specs=whole(1)[0],
        scratch_shapes=[pltpu.VMEM((channels, 2 * face), BF)],
        compiler_params=pltpu.CompilerParams(vmem_limit_bytes=SMALL_LIMIT),
        cost_estimate=pl.CostEstimate(flops=4 * rows * LOW * face, bytes_accessed=1 << 20, transcendentals=0),
    )(flags, here, first, second, pick)


def place(side, keep, came, order, channels):
    rows = order.shape[1]
    return pl.pallas_call(
        place_kernel,
        out_shape=jax.ShapeDtypeStruct((channels, rows), BF),
        in_specs=[pl.BlockSpec(memory_space=pltpu.SMEM)] + whole(3),
        out_specs=whole(1)[0],
        scratch_shapes=[pltpu.VMEM((channels, rows), BF)],
        compiler_params=pltpu.CompilerParams(vmem_limit_bytes=SMALL_LIMIT),
        cost_estimate=pl.CostEstimate(flops=2 * rows * rows * channels, bytes_accessed=1 << 20, transcendentals=0),
    )(side, keep, came, order)


def halve(digit, keep, got, radix):
    rows, width = keep.shape
    shapes = [jax.ShapeDtypeStruct((rows // radix, width), F32 if d == 0 else BF) for d in range(radix)]
    return pl.pallas_call(
        halve_kernel,
        out_shape=tuple(shapes),
        in_specs=[pl.BlockSpec(memory_space=pltpu.SMEM)] + whole(2),
        out_specs=tuple(whole(radix)),
        compiler_params=pltpu.CompilerParams(vmem_limit_bytes=SMALL_LIMIT),
        cost_estimate=pl.CostEstimate(flops=rows * width, bytes_accessed=7 * rows * width, transcendentals=0),
    )(digit, keep, got)


def stages(count):
    plan, stride = [], 1
    while stride < count:
        left = count // stride
        radix = 4 if stride > 1 and left % 4 == 0 else 2
        if left % radix:
            radix = left
        plan.append((stride, radix))
        stride *= radix
    return plan


def swapped(array, count, stride, radix, delta):
    def partner(i):
        digit = i // stride % radix
        other = (digit ^ delta) if radix in (2, 4) else (delta - digit) % radix
        return i + (other - digit) * stride

    return lax.ppermute(array, AXES, [(i, partner(i)) for i in range(count)])


def other_digit(digit, delta, radix):
    return (digit ^ delta) if radix in (2, 4) else (delta - digit) % radix


def reduce_stage(x, flat, count, stride, radix):
    digit = flat // stride % radix
    pieces = x.reshape((radix, x.shape[0] // radix) + x.shape[1:])
    total = None
    for delta in range(radix):
        piece = lax.dynamic_index_in_dim(pieces, other_digit(digit, delta, radix), 0, keepdims=False)
        if radix not in (2, 4) or delta:
            piece = swapped(piece, count, stride, radix, delta)
        total = piece.astype(F32) if total is None else total + piece.astype(F32)
    return total.astype(BF)


def by_digit(got, digit, radix):
    parts = []
    for place in range(radix):
        part = got[0]
        for d in range(radix):
            where = (place ^ d) if radix in (2, 4) else (place + d) % radix
            part = jnp.where(digit == d, got[where], part)
        parts.append(part)
    return parts


def joined(parts):
    return parts[0] if len(parts) == 1 else jnp.concatenate(parts, 0)


def gather_stage(parts, flat, count, stride, radix, cargo=lambda delta: None):
    digit = flat // stride % radix
    rows = sum(part.shape[0] for part in parts)
    got, brought = [], {}
    for d in range(radix):
        if radix in (2, 4) and d == 0:
            got.append(joined(parts))
            continue
        extra = cargo(d)
        piece = swapped(joined(parts if extra is None else parts + [extra]), count, stride, radix, d)
        got.append(piece[:rows])
        brought[d] = piece[rows:]
    return by_digit(got, digit, radix), brought


def meet(first, second):
    size = lax.axis_size("brick")
    got = []
    for start, array in ((0, first), (1, second)):
        pairs = []
        for i in range(start, size - 1, 2):
            pairs += [(i, i + 1), (i + 1, i)]
        got.append(lax.ppermute(array, "brick", pairs))
    return got


def on_device(features, order, face_list, face_count, kernel_map, weight, bias, cotangent):
    offsets, channels, c_out = weight.shape
    rows = features.shape[0]
    face = face_list.shape[0] // 2
    bricks = lax.axis_size("brick")
    count = bricks * lax.axis_size("group")
    per = rows // bricks
    depth = offsets * channels
    unit = 8 * count
    padded = -(-depth // unit) * unit

    w = weight.reshape(depth, c_out)
    flat = lax.axis_index("brick") * lax.axis_size("group") + lax.axis_index("group")
    send = send_blocks(features.T, order[None], bricks)
    got = lax.all_to_all(send, "brick", split_axis=0, concat_axis=0)

    slots = jnp.arange(2 * face, dtype=jnp.int32)
    live = jnp.where(slots < face, slots < face_count[0], slots - face < face_count[1])
    pick = one_hot_rows(jnp.where(live, face_list, -1), rows)
    pick, got = lax.optimization_barrier((pick, got))
    local = got.transpose(1, 0, 2).reshape(channels, rows)
    shown = dot(local, pick, 1, 1).astype(BF)
    odd = lax.axis_index("brick") % 2
    down, up = shown[:, :face], shown[:, face:]
    first, second = meet(jnp.where(odd == 1, down, up), jnp.where(odd == 1, up, down))

    flags = jnp.stack([flat % 2, odd]).astype(jnp.int32)
    low = (kernel_map & (LOW - 1)).astype(F32)
    high = lax.shift_right_logical(kernel_map, SHIFT).astype(F32)
    output, give, keep = forward(flags, got, first, second, low, high, w, bias[None], cotangent, padded)
    packed = (bricks, count) == (8, 32) and per * 2 == LOW and channels % 16 == 0
    plan = stages(count)[1:]
    taken = swapped(give, count, 1, 2, 1)
    if plan[0][1] == 4 and padded % 128 == 0:
        stride, radix = plan[0]
        pieces = halve((flat // stride % radix).astype(jnp.int32)[None], keep, taken, radix)
        total = pieces[0]
        for d in range(1, radix):
            total = total + swapped(pieces[d], count, stride, radix, d).astype(F32)
        total = total.astype(BF)
    else:
        total = (keep.astype(F32) + taken.astype(F32)).astype(BF)
        total = reduce_stage(total, flat, count, *plan[0])
    here, first, second = backward(packed, flags, output, cotangent, low, high, w, face)
    total, first, second = lax.optimization_barrier((total, first, second))
    first, second = meet(first, second)
    for stride, radix in plan[1:]:
        total = reduce_stage(total, flat, count, stride, radix)

    local_grad = finish(packed, flags, here, first, second, pick)
    if packed:
        part = channels // 2
        total, local_grad = lax.optimization_barrier((total, local_grad))
        local_grad = local_grad.reshape(bricks // 2, channels, LOW)
        z, x = flat // 8, flat // 4 % 2
        cargo = lambda d: lax.dynamic_index_in_dim(local_grad, z ^ d, 0, keepdims=False)
        parts, brought = gather_stage([total], flat, count, 8, 4, cargo)
        mine = jnp.stack(by_digit([cargo(0)] + [brought[d] for d in (1, 2, 3)], z, 4))
        mine = mine.reshape(bricks // 2, 2, part, LOW)
        give = jnp.where(x == 0, mine[:, 1], mine[:, 0]).reshape(-1, LOW)
        keep = jnp.where(x == 0, mine[:, 0], mine[:, 1]).reshape(-1, LOW)
        parts, brought = gather_stage(parts, flat, count, 2, 4, lambda d: give if d == 2 else None)
        came = brought[2]
    else:
        blocks = rows // LOW
        send = local_grad.reshape(blocks, channels, LOW // per, per).transpose(0, 2, 1, 3)
        came = lax.all_to_all(send.reshape(bricks, channels, per), "brick", split_axis=0, concat_axis=0)
        parts = [total]
        for stride, radix in reversed(plan):
            parts, _ = gather_stage(parts, flat, count, stride, radix)
    total = joined(parts)
    total, came = lax.optimization_barrier((total, came))
    if packed:
        grad_in = place(x.astype(jnp.int32)[None], keep, came, order[None], channels).T
    else:
        returned = came.transpose(1, 0, 2).reshape(channels, rows)
        grad_in = dot(returned, one_hot_rows(order, rows), 1, 0).astype(BF).T
    other = swapped(total, count, 1, 2, 1)
    low = jnp.where(flat % 2 == 0, total, other)[: depth // 2]
    high = jnp.where(flat % 2 == 0, other, total)[: depth // 2]
    scale = jnp.float32(1.0 / math.sqrt(count * rows))
    weight_grad = (jnp.concatenate([low, high], 0).astype(F32) * scale).reshape(offsets, channels, c_out)
    return output, grad_in, weight_grad


def solution(mesh):
    return jax.shard_map(
        on_device,
        mesh=mesh,
        in_specs=(
            P(AXES, None),
            P(AXES),
            P(AXES),
            P(AXES),
            P(None, AXES),
            P(),
            P(),
            P(AXES, None),
        ),
        out_specs=(P(AXES, None), P(AXES, None), P()),
        check_vma=False,
    )
```

```python
import functools
import math

import jax
import jax.numpy as jnp
from jax import lax
from jax.experimental import pallas as pl
from jax.experimental.pallas import tpu as pltpu
from jax.sharding import PartitionSpec as P

BF = jnp.bfloat16
F32 = jnp.float32
LOW = 256
SHIFT = 8
VMEM_LIMIT = 53 << 20
SMALL_LIMIT = 6 << 20
FULL_LIMIT = 51 << 20
ALL_LIMIT = 60 << 20
AXES = ("brick", "group")


def dot(a, b, a_dim, b_dim):
    dims = (((a_dim,), (b_dim,)), ((), ()))
    return lax.dot_general(a, b, dims, preferred_element_type=F32)


def one_hot_rows(index, width):
    columns = jnp.arange(width, dtype=jnp.int32)
    return (index[:, None] == columns[None, :]).astype(BF)


def one_hot_low(low, lanes):
    iota = lax.broadcasted_iota(jnp.int32, (LOW, lanes), 0).astype(BF)
    hit = iota == jnp.broadcast_to(low.astype(BF), (LOW, lanes))
    return jnp.where(hit, jnp.ones((), BF), jnp.zeros((), BF))


def send_kernel(feat_hbm, order_hbm, out_ref, feat_ref, order_ref, x_ref, feat_sem, order_sem):
    fetch_feat = pltpu.make_async_copy(feat_hbm, feat_ref, feat_sem)
    fetch_feat.start()
    fetch_order = pltpu.make_async_copy(order_hbm, order_ref, order_sem)
    fetch_order.start()
    channels, rows = feat_ref.shape
    per = out_ref.shape[2]
    fetch_feat.wait()
    fetch_order.wait()
    for a in range(rows // LOW):
        x_ref[a * channels : (a + 1) * channels, :] = feat_ref[:, a * LOW : (a + 1) * LOW]
    for n in range(rows // LOW):
        row = order_ref[:, n * LOW : (n + 1) * LOW]
        terms = dot(x_ref[...], one_hot_low((row & (LOW - 1)).astype(F32), LOW), 1, 0)
        block = jnp.broadcast_to(lax.shift_right_logical(row, SHIFT), (channels, LOW))
        picked = terms[:channels]
        for a in range(1, rows // LOW):
            picked = jnp.where(block == a, terms[a * channels : (a + 1) * channels], picked)
        picked = picked.astype(BF)
        for p in range(LOW // per):
            out_ref[n * (LOW // per) + p] = picked[:, p * per : (p + 1) * per]


def sides(odd, first_ref, second_ref):
    first, second = first_ref[...].astype(F32), second_ref[...].astype(F32)
    low = jnp.where(odd == 1, first, second)
    high = jnp.where(odd == 1, second, first)
    return low.astype(BF), high.astype(BF)


def forward_kernel(
    flag_ref, got_ref, even_ref, odd_ref, low_ref, high_ref, w_hbm, bias_ref, cot_hbm, out_hbm, send_ref, keep_ref,
    g_ref, x_ref, wt_ref, w_ref, cot_ref, out_ref, pg_ref, w_sem, cot_sem, out_sem,
):
    fetch_w = pltpu.make_async_copy(w_hbm, w_ref, w_sem)
    fetch_w.start()
    fetch_cot = pltpu.make_async_copy(cot_hbm, cot_ref, cot_sem)
    fetch_cot.start()
    offsets, voxels = low_ref.shape
    depth, c_out = w_ref.shape
    channels = depth // offsets
    here = voxels // LOW
    blocks = x_ref.shape[0] // channels
    center = offsets // 2
    per = got_ref.shape[2]
    for a in range(here):
        for p in range(LOW // per):
            x_ref[a * channels : (a + 1) * channels, p * per : (p + 1) * per] = got_ref[a * (LOW // per) + p]
    face = even_ref.shape[1]
    prev, after = sides(flag_ref[1], even_ref, odd_ref)
    x_ref[here * channels :, :face] = prev
    x_ref[here * channels :, face:] = after
    ready = offsets // 3
    for k in range(offsets):
        if k == ready:
            fetch_w.wait()
            fetch_cot.wait()
        for j in range(2 * (k - ready), min(2 * (k - ready + 1), offsets)) if k >= ready else ():
            wt_ref[:, j * channels : (j + 1) * channels] = w_ref[j * channels : (j + 1) * channels, :].T
        at = slice(k * channels, (k + 1) * channels)
        if k == center:
            for a in range(here):
                g_ref[at, a * LOW : (a + 1) * LOW] = x_ref[a * channels : (a + 1) * channels, :]
            continue
        low, high = low_ref[k : k + 1, :], high_ref[k : k + 1, :]
        for n in range(here):
            sl = slice(n * LOW, (n + 1) * LOW)
            terms = dot(x_ref[...], one_hot_low(low[:, sl], LOW), 1, 0)
            block = jnp.broadcast_to(high[:, sl], (channels, LOW))
            picked = jnp.zeros((channels, LOW), F32)
            for a in range(blocks):
                picked = jnp.where(block == a, terms[a * channels : (a + 1) * channels], picked)
            g_ref[at, sl] = picked.astype(BF)
    for n in range(here):
        sl = slice(n * LOW, (n + 1) * LOW)
        pre = dot(wt_ref[...], g_ref[:, sl], 1, 0).T + bias_ref[...]
        out_ref[sl, :] = jnp.maximum(pre, 0.0).astype(BF)
        pg_ref[sl, :] = jnp.where(pre > 0, cot_ref[sl, :].astype(F32), 0.0).astype(BF)
    store = pltpu.make_async_copy(out_ref, out_hbm, out_sem)
    store.start()
    half = flag_ref[0]
    count = depth // 2
    for ref, which in ((send_ref, 1 - half), (keep_ref, half)):
        for m in range(0, count, 288):
            step = min(288, count - m)
            at = pl.ds(pl.multiple_of(which * count + m, 16), step)
            ref[m : m + step, :] = dot(g_ref[at, :], pg_ref[...], 1, 0).astype(ref.dtype)
        ref[count:, :] = jnp.zeros((ref.shape[0] - count, c_out), ref.dtype)
    store.wait()


def backward_kernel(
    packed, flag_ref, out_hbm, cot_hbm, low_ref, high_ref, w_hbm, here_ref, first_ref, second_ref,
    c_ref, acc_ref, pg_ref, out_ref, cot_ref, w_ref, out_sem, cot_sem, w_sems,
):
    fetch_out = pltpu.make_async_copy(out_hbm, out_ref, out_sem)
    fetch_out.start()
    fetch_cot = pltpu.make_async_copy(cot_hbm, cot_ref, cot_sem)
    fetch_cot.start()
    offsets, voxels = low_ref.shape
    depth = w_ref.shape[0]
    step = depth // 9
    fetch_w = []
    for m in range(9):
        sl = slice(m * step, (m + 1) * step)
        fetch_w.append(pltpu.make_async_copy(w_hbm.at[sl, :], w_ref.at[sl, :], w_sems.at[m]))
        fetch_w[m].start()
    channels = depth // offsets
    here = voxels // LOW
    blocks = acc_ref.shape[0] // channels
    fetch_out.wait()
    fetch_cot.wait()
    pg_ref[...] = jnp.where(out_ref[...] > 0, cot_ref[...], jnp.zeros((), BF))
    for m in range(9):
        sl = slice(m * step, (m + 1) * step)
        fetch_w[m].wait()
        c_ref[sl, :] = dot(w_ref[sl, :], pg_ref[...], 1, 1).astype(BF)
    center = offsets // 2
    for a in range(here):
        at = slice(a * channels, (a + 1) * channels)
        acc_ref[at, :] = c_ref[center * channels : (center + 1) * channels, a * LOW : (a + 1) * LOW].astype(F32)
    acc_ref[here * channels :, :] = jnp.zeros((channels * (blocks - here), LOW), F32)
    for k in range(offsets):
        if k == center:
            continue
        contrib = c_ref[k * channels : (k + 1) * channels, :]
        low, high = low_ref[k : k + 1, :], high_ref[k : k + 1, :]
        block = jnp.broadcast_to(high.astype(BF), (channels, voxels))
        parts = [jnp.where(block == jnp.array(a, BF), contrib, jnp.zeros((), BF)) for a in range(blocks)]
        acc_ref[...] += dot(jnp.concatenate(parts, 0), one_hot_low(low, voxels), 1, 1)
    if packed:
        part, per = channels // 2, LOW // 2
        for a in range(here):
            for p in range(2):
                for h in range(2):
                    at = slice(a * channels + h * part, a * channels + (h + 1) * part)
                    to = slice((2 * a + p) * part, (2 * a + p + 1) * part)
                    here_ref[to, h * per : (h + 1) * per] = acc_ref[at, p * per : (p + 1) * per]
    else:
        here_ref[...] = acc_ref[: here * channels, :]
    face = first_ref.shape[1]
    down, up = acc_ref[here * channels :, :face], acc_ref[here * channels :, face:]
    odd = flag_ref[1]
    first_ref[...] = jnp.where(odd == 1, down, up).astype(BF)
    second_ref[...] = jnp.where(odd == 1, up, down).astype(BF)


def finish_kernel(packed, flag_ref, here_ref, first_ref, second_ref, pick_ref, out_ref, from_ref):
    channels, face = first_ref.shape
    blocks = here_ref.shape[0] // channels
    prev, after = sides(flag_ref[1], first_ref, second_ref)
    from_ref[:, :face] = prev
    from_ref[:, face:] = after
    part, per = channels // 2, LOW // 2
    for a in range(blocks):
        added = dot(from_ref[...], pick_ref[:, a * LOW : (a + 1) * LOW], 1, 0)
        if not packed:
            at = slice(a * channels, (a + 1) * channels)
            out_ref[at, :] = (here_ref[at, :] + added).astype(BF)
            continue
        for p in range(2):
            at = slice((2 * a + p) * part, (2 * a + p + 1) * part)
            for h in range(2):
                lanes = slice(h * per, (h + 1) * per)
                term = added[h * part : (h + 1) * part, p * per : (p + 1) * per]
                out_ref[at, lanes] = (here_ref[at, lanes] + term).astype(BF)


def place_kernel(side_ref, keep_ref, came_ref, order_ref, out_ref, back_ref):
    channels, rows = out_ref.shape
    part, per = channels // 2, LOW // 2
    side = side_ref[0]
    for z in range(rows // LOW):
        at = slice(z * part, (z + 1) * part)
        for p in range(2):
            block = jnp.where(side == p, keep_ref[at, :].astype(F32), came_ref[at, :].astype(F32)).astype(BF)
            lanes = slice((2 * z + p) * per, (2 * z + p + 1) * per)
            for h in range(2):
                back_ref[h * part : (h + 1) * part, lanes] = block[:, h * per : (h + 1) * per]
    row = order_ref[...]
    block = jnp.broadcast_to(lax.shift_right_logical(row, SHIFT).astype(F32).astype(BF), (channels, rows))
    back = back_ref[...]
    parts = [jnp.where(block == jnp.array(a, BF), back, jnp.zeros((), BF)) for a in range(rows // LOW)]
    placed = dot(jnp.concatenate(parts, 0), one_hot_low((row & (LOW - 1)).astype(F32), rows), 1, 1)
    for a in range(rows // LOW):
        out_ref[:, a * LOW : (a + 1) * LOW] = placed[a * channels : (a + 1) * channels].astype(BF)


def halve_kernel(digit_ref, keep_ref, got_ref, *out_refs):
    rows = out_refs[0].shape[0]
    for d, out_ref in enumerate(out_refs):
        at = pl.ds(pl.multiple_of((digit_ref[0] ^ d) * rows, 16), rows)
        out_ref[...] = (keep_ref[at, :].astype(F32) + got_ref[at, :].astype(F32)).astype(out_ref.dtype)


def whole(count):
    return [pl.BlockSpec(memory_space=pltpu.VMEM)] * count


def send_blocks(features, order, bricks):
    channels, rows = features.shape
    hbm = pl.BlockSpec(memory_space=pltpu.HBM)
    return pl.pallas_call(
        send_kernel,
        out_shape=jax.ShapeDtypeStruct((bricks, channels, rows // bricks), BF),
        in_specs=[hbm, hbm],
        out_specs=whole(1)[0],
        scratch_shapes=[
            pltpu.VMEM((channels, rows), BF),
            pltpu.VMEM((1, rows), jnp.int32),
            pltpu.VMEM((channels * rows // LOW, LOW), BF),
            pltpu.SemaphoreType.DMA,
            pltpu.SemaphoreType.DMA,
        ],
        compiler_params=pltpu.CompilerParams(vmem_limit_bytes=ALL_LIMIT),
        cost_estimate=pl.CostEstimate(flops=2 * rows * rows * channels, bytes_accessed=1 << 19, transcendentals=0),
    )(features, order)


def forward(flags, got, first, second, low, high, w, bias, cot, padded):
    offsets, voxels = low.shape
    depth, c_out = w.shape
    rows = depth // offsets * (voxels // LOW + 1)
    macs = voxels * depth * c_out * 2 + offsets * voxels * LOW * rows
    hbm = pl.BlockSpec(memory_space=pltpu.HBM)
    return pl.pallas_call(
        forward_kernel,
        out_shape=(
            jax.ShapeDtypeStruct((voxels, c_out), BF),
            jax.ShapeDtypeStruct((padded // 2, c_out), BF),
            jax.ShapeDtypeStruct((padded // 2, c_out), BF),
        ),
        in_specs=[pl.BlockSpec(memory_space=pltpu.SMEM)] + whole(5) + [hbm] + whole(1) + [hbm],
        out_specs=(hbm,) + tuple(whole(2)),
        scratch_shapes=[
            pltpu.VMEM((depth, voxels), BF),
            pltpu.VMEM((rows, LOW), BF),
            pltpu.VMEM((c_out, depth), BF),
            pltpu.VMEM((depth, c_out), BF),
            pltpu.VMEM((voxels, c_out), BF),
            pltpu.VMEM((voxels, c_out), BF),
            pltpu.VMEM((voxels, c_out), BF),
            pltpu.SemaphoreType.DMA,
            pltpu.SemaphoreType.DMA,
            pltpu.SemaphoreType.DMA,
        ],
        compiler_params=pltpu.CompilerParams(vmem_limit_bytes=FULL_LIMIT),
        cost_estimate=pl.CostEstimate(flops=2 * macs, bytes_accessed=5 << 20, transcendentals=0),
    )(flags, got, first, second, low, high, w, bias, cot)


def backward(packed, flags, out, cot, low, high, w, face):
    hbm = pl.BlockSpec(memory_space=pltpu.HBM)
    offsets, voxels = low.shape
    depth, c_out = w.shape
    channels = depth // offsets
    rows = channels * (voxels // LOW + 1)
    macs = voxels * depth * c_out + offsets * voxels * LOW * rows
    return pl.pallas_call(
        functools.partial(backward_kernel, packed),
        out_shape=(
            jax.ShapeDtypeStruct((voxels // LOW * channels, LOW), F32),
            jax.ShapeDtypeStruct((channels, face), BF),
            jax.ShapeDtypeStruct((channels, face), BF),
        ),
        in_specs=[pl.BlockSpec(memory_space=pltpu.SMEM), hbm, hbm] + whole(2) + [hbm],
        out_specs=tuple(whole(3)),
        scratch_shapes=[
            pltpu.VMEM((depth, voxels), BF),
            pltpu.VMEM((rows, LOW), F32),
            pltpu.VMEM((voxels, c_out), BF),
            pltpu.VMEM((voxels, c_out), BF),
            pltpu.VMEM((voxels, c_out), BF),
            pltpu.VMEM((depth, c_out), BF),
            pltpu.SemaphoreType.DMA,
            pltpu.SemaphoreType.DMA,
            pltpu.SemaphoreType.DMA((9,)),
        ],
        compiler_params=pltpu.CompilerParams(vmem_limit_bytes=VMEM_LIMIT),
        cost_estimate=pl.CostEstimate(flops=2 * macs, bytes_accessed=3 << 20, transcendentals=0),
    )(flags, out, cot, low, high, w)


def finish(packed, flags, here, first, second, pick):
    rows, _ = here.shape
    channels, face = first.shape
    return pl.pallas_call(
        functools.partial(finish_kernel, packed),
        out_shape=jax.ShapeDtypeStruct((rows, LOW), BF),
        in_specs=[pl.BlockSpec(memory_space=pltpu.SMEM)] + whole(4),
        out_specs=whole(1)[0],
        scratch_shapes=[pltpu.VMEM((channels, 2 * face), BF)],
        compiler_params=pltpu.CompilerParams(vmem_limit_bytes=SMALL_LIMIT),
        cost_estimate=pl.CostEstimate(flops=4 * rows * LOW * face, bytes_accessed=1 << 20, transcendentals=0),
    )(flags, here, first, second, pick)


def place(side, keep, came, order, channels):
    rows = order.shape[1]
    return pl.pallas_call(
        place_kernel,
        out_shape=jax.ShapeDtypeStruct((channels, rows), BF),
        in_specs=[pl.BlockSpec(memory_space=pltpu.SMEM)] + whole(3),
        out_specs=whole(1)[0],
        scratch_shapes=[pltpu.VMEM((channels, rows), BF)],
        compiler_params=pltpu.CompilerParams(vmem_limit_bytes=SMALL_LIMIT),
        cost_estimate=pl.CostEstimate(flops=2 * rows * rows * channels, bytes_accessed=1 << 20, transcendentals=0),
    )(side, keep, came, order)


def halve(digit, keep, got, radix):
    rows, width = keep.shape
    shapes = [jax.ShapeDtypeStruct((rows // radix, width), F32 if d == 0 else BF) for d in range(radix)]
    return pl.pallas_call(
        halve_kernel,
        out_shape=tuple(shapes),
        in_specs=[pl.BlockSpec(memory_space=pltpu.SMEM)] + whole(2),
        out_specs=tuple(whole(radix)),
        compiler_params=pltpu.CompilerParams(vmem_limit_bytes=SMALL_LIMIT),
        cost_estimate=pl.CostEstimate(flops=rows * width, bytes_accessed=7 * rows * width, transcendentals=0),
    )(digit, keep, got)


def stages(count):
    plan, stride = [], 1
    while stride < count:
        left = count // stride
        radix = 4 if stride > 1 and left % 4 == 0 else 2
        if left % radix:
            radix = left
        plan.append((stride, radix))
        stride *= radix
    return plan


def swapped(array, count, stride, radix, delta):
    def partner(i):
        digit = i // stride % radix
        other = (digit ^ delta) if radix in (2, 4) else (delta - digit) % radix
        return i + (other - digit) * stride

    return lax.ppermute(array, AXES, [(i, partner(i)) for i in range(count)])


def other_digit(digit, delta, radix):
    return (digit ^ delta) if radix in (2, 4) else (delta - digit) % radix


def reduce_stage(x, flat, count, stride, radix):
    digit = flat // stride % radix
    pieces = x.reshape((radix, x.shape[0] // radix) + x.shape[1:])
    total = None
    for delta in range(radix):
        piece = lax.dynamic_index_in_dim(pieces, other_digit(digit, delta, radix), 0, keepdims=False)
        if radix not in (2, 4) or delta:
            piece = swapped(piece, count, stride, radix, delta)
        total = piece.astype(F32) if total is None else total + piece.astype(F32)
    return total.astype(BF)


def by_digit(got, digit, radix):
    parts = []
    for place in range(radix):
        part = got[0]
        for d in range(radix):
            where = (place ^ d) if radix in (2, 4) else (place + d) % radix
            part = jnp.where(digit == d, got[where], part)
        parts.append(part)
    return parts


def joined(parts):
    return parts[0] if len(parts) == 1 else jnp.concatenate(parts, 0)


def gather_stage(parts, flat, count, stride, radix, cargo=lambda delta: None):
    digit = flat // stride % radix
    rows = sum(part.shape[0] for part in parts)
    got, brought = [], {}
    for d in range(radix):
        if radix in (2, 4) and d == 0:
            got.append(joined(parts))
            continue
        extra = cargo(d)
        piece = swapped(joined(parts if extra is None else parts + [extra]), count, stride, radix, d)
        got.append(piece[:rows])
        brought[d] = piece[rows:]
    return by_digit(got, digit, radix), brought


def meet(first, second):
    size = lax.axis_size("brick")
    got = []
    for start, array in ((0, first), (1, second)):
        pairs = []
        for i in range(start, size - 1, 2):
            pairs += [(i, i + 1), (i + 1, i)]
        got.append(lax.ppermute(array, "brick", pairs))
    return got


def on_device(features, order, face_list, face_count, kernel_map, weight, bias, cotangent):
    offsets, channels, c_out = weight.shape
    rows = features.shape[0]
    face = face_list.shape[0] // 2
    bricks = lax.axis_size("brick")
    count = bricks * lax.axis_size("group")
    per = rows // bricks
    depth = offsets * channels
    unit = 8 * count
    padded = -(-depth // unit) * unit

    w = weight.reshape(depth, c_out)
    flat = lax.axis_index("brick") * lax.axis_size("group") + lax.axis_index("group")
    send = send_blocks(features.T, order[None], bricks)
    got = lax.all_to_all(send, "brick", split_axis=0, concat_axis=0)

    slots = jnp.arange(2 * face, dtype=jnp.int32)
    live = jnp.where(slots < face, slots < face_count[0], slots - face < face_count[1])
    pick = one_hot_rows(jnp.where(live, face_list, -1), rows)
    pick, got = lax.optimization_barrier((pick, got))
    local = got.transpose(1, 0, 2).reshape(channels, rows)
    shown = dot(local, pick, 1, 1).astype(BF)
    odd = lax.axis_index("brick") % 2
    down, up = shown[:, :face], shown[:, face:]
    first, second = meet(jnp.where(odd == 1, down, up), jnp.where(odd == 1, up, down))

    flags = jnp.stack([flat % 2, odd]).astype(jnp.int32)
    low = (kernel_map & (LOW - 1)).astype(F32)
    high = lax.shift_right_logical(kernel_map, SHIFT).astype(F32)
    output, give, keep = forward(flags, got, first, second, low, high, w, bias[None], cotangent, padded)
    packed = (bricks, count) == (8, 32) and per * 2 == LOW and channels % 16 == 0
    plan = stages(count)[1:]
    taken = swapped(give, count, 1, 2, 1)
    if plan[0][1] == 4 and padded % 128 == 0:
        stride, radix = plan[0]
        pieces = halve((flat // stride % radix).astype(jnp.int32)[None], keep, taken, radix)
        total = pieces[0]
        for d in range(1, radix):
            total = total + swapped(pieces[d], count, stride, radix, d).astype(F32)
        total = total.astype(BF)
    else:
        total = (keep.astype(F32) + taken.astype(F32)).astype(BF)
        total = reduce_stage(total, flat, count, *plan[0])
    here, first, second = backward(packed, flags, output, cotangent, low, high, w, face)
    total, first, second = lax.optimization_barrier((total, first, second))
    first, second = meet(first, second)
    for stride, radix in plan[1:]:
        total = reduce_stage(total, flat, count, stride, radix)

    local_grad = finish(packed, flags, here, first, second, pick)
    if packed:
        part = channels // 2
        total, local_grad = lax.optimization_barrier((total, local_grad))
        local_grad = local_grad.reshape(bricks // 2, channels, LOW)
        z, x = flat // 8, flat // 4 % 2
        cargo = lambda d: lax.dynamic_index_in_dim(local_grad, z ^ d, 0, keepdims=False)
        parts, brought = gather_stage([total], flat, count, 8, 4, cargo)
        mine = jnp.stack(by_digit([cargo(0)] + [brought[d] for d in (1, 2, 3)], z, 4))
        mine = mine.reshape(bricks // 2, 2, part, LOW)
        give = jnp.where(x == 0, mine[:, 1], mine[:, 0]).reshape(-1, LOW)
        keep = jnp.where(x == 0, mine[:, 0], mine[:, 1]).reshape(-1, LOW)
        parts, brought = gather_stage(parts, flat, count, 2, 4, lambda d: give if d == 2 else None)
        came = brought[2]
    else:
        blocks = rows // LOW
        send = local_grad.reshape(blocks, channels, LOW // per, per).transpose(0, 2, 1, 3)
        came = lax.all_to_all(send.reshape(bricks, channels, per), "brick", split_axis=0, concat_axis=0)
        parts = [total]
        for stride, radix in reversed(plan):
            parts, _ = gather_stage(parts, flat, count, stride, radix)
    total = joined(parts)
    total, came = lax.optimization_barrier((total, came))
    if packed:
        grad_in = place(x.astype(jnp.int32)[None], keep, came, order[None], channels).T
    else:
        returned = came.transpose(1, 0, 2).reshape(channels, rows)
        grad_in = dot(returned, one_hot_rows(order, rows), 1, 0).astype(BF).T
    other = swapped(total, count, 1, 2, 1)
    low = jnp.where(flat % 2 == 0, total, other)[: depth // 2]
    high = jnp.where(flat % 2 == 0, other, total)[: depth // 2]
    scale = jnp.float32(1.0 / math.sqrt(count * rows))
    weight_grad = (jnp.concatenate([low, high], 0).astype(F32) * scale).reshape(offsets, channels, c_out)
    return output, grad_in, weight_grad


def solution(mesh):
    return jax.shard_map(
        on_device,
        mesh=mesh,
        in_specs=(
            P(AXES, None),
            P(AXES),
            P(AXES),
            P(AXES),
            P(None, AXES),
            P(),
            P(),
            P(AXES, None),
        ),
        out_specs=(P(AXES, None), P(AXES, None), P()),
        check_vma=False,
    )
```

```python
import functools
import math

import jax
import jax.numpy as jnp
from jax import lax
from jax.experimental import pallas as pl
from jax.experimental.pallas import tpu as pltpu
from jax.sharding import PartitionSpec as P

BF = jnp.bfloat16
F32 = jnp.float32
LOW = 256
SHIFT = 8
VMEM_LIMIT = 20 << 20
SMALL_LIMIT = 6 << 20
FULL_LIMIT = 50 << 20
ALL_LIMIT = 60 << 20
AXES = ("brick", "group")


def dot(a, b, a_dim, b_dim):
    dims = (((a_dim,), (b_dim,)), ((), ()))
    return lax.dot_general(a, b, dims, preferred_element_type=F32)


def one_hot_rows(index, width):
    columns = jnp.arange(width, dtype=jnp.int32)
    return (index[:, None] == columns[None, :]).astype(BF)


def one_hot_low(low, lanes):
    iota = lax.broadcasted_iota(jnp.int32, (LOW, lanes), 0).astype(BF)
    hit = iota == jnp.broadcast_to(low.astype(BF), (LOW, lanes))
    return jnp.where(hit, jnp.ones((), BF), jnp.zeros((), BF))


def send_kernel(feat_hbm, order_hbm, out_ref, feat_ref, order_ref, x_ref, feat_sem, order_sem):
    fetch_feat = pltpu.make_async_copy(feat_hbm, feat_ref, feat_sem)
    fetch_feat.start()
    fetch_order = pltpu.make_async_copy(order_hbm, order_ref, order_sem)
    fetch_order.start()
    channels, rows = feat_ref.shape
    per = out_ref.shape[2]
    fetch_feat.wait()
    fetch_order.wait()
    for a in range(rows // LOW):
        x_ref[a * channels : (a + 1) * channels, :] = feat_ref[:, a * LOW : (a + 1) * LOW]
    for n in range(rows // LOW):
        row = order_ref[:, n * LOW : (n + 1) * LOW]
        terms = dot(x_ref[...], one_hot_low((row & (LOW - 1)).astype(F32), LOW), 1, 0)
        block = jnp.broadcast_to(lax.shift_right_logical(row, SHIFT), (channels, LOW))
        picked = terms[:channels]
        for a in range(1, rows // LOW):
            picked = jnp.where(block == a, terms[a * channels : (a + 1) * channels], picked)
        picked = picked.astype(BF)
        for p in range(LOW // per):
            out_ref[n * (LOW // per) + p] = picked[:, p * per : (p + 1) * per]


def sides(odd, first_ref, second_ref):
    first, second = first_ref[...].astype(F32), second_ref[...].astype(F32)
    low = jnp.where(odd == 1, first, second)
    high = jnp.where(odd == 1, second, first)
    return low.astype(BF), high.astype(BF)


def forward_kernel(
    flag_ref, got_ref, even_ref, odd_ref, low_ref, high_ref, w_hbm, bias_ref, cot_hbm, out_hbm, send_ref, keep_ref,
    g_ref, x_ref, wt_ref, w_ref, cot_ref, out_ref, pg_ref, w_sem, cot_sem, out_sem,
):
    fetch_w = pltpu.make_async_copy(w_hbm, w_ref, w_sem)
    fetch_w.start()
    fetch_cot = pltpu.make_async_copy(cot_hbm, cot_ref, cot_sem)
    fetch_cot.start()
    offsets, voxels = low_ref.shape
    depth, c_out = w_ref.shape
    channels = depth // offsets
    here = voxels // LOW
    blocks = x_ref.shape[0] // channels
    center = offsets // 2
    per = got_ref.shape[2]
    for a in range(here):
        for p in range(LOW // per):
            x_ref[a * channels : (a + 1) * channels, p * per : (p + 1) * per] = got_ref[a * (LOW // per) + p]
    face = even_ref.shape[1]
    prev, after = sides(flag_ref[1], even_ref, odd_ref)
    x_ref[here * channels :, :face] = prev
    x_ref[here * channels :, face:] = after
    ready = offsets // 3
    for k in range(offsets):
        if k == ready:
            fetch_w.wait()
            fetch_cot.wait()
        for j in range(2 * (k - ready), min(2 * (k - ready + 1), offsets)) if k >= ready else ():
            wt_ref[:, j * channels : (j + 1) * channels] = w_ref[j * channels : (j + 1) * channels, :].T
        at = slice(k * channels, (k + 1) * channels)
        if k == center:
            for a in range(here):
                g_ref[at, a * LOW : (a + 1) * LOW] = x_ref[a * channels : (a + 1) * channels, :]
            continue
        low, high = low_ref[k : k + 1, :], high_ref[k : k + 1, :]
        for n in range(here):
            sl = slice(n * LOW, (n + 1) * LOW)
            terms = dot(x_ref[...], one_hot_low(low[:, sl], LOW), 1, 0)
            block = jnp.broadcast_to(high[:, sl], (channels, LOW))
            picked = jnp.zeros((channels, LOW), F32)
            for a in range(blocks):
                picked = jnp.where(block == a, terms[a * channels : (a + 1) * channels], picked)
            g_ref[at, sl] = picked.astype(BF)
    for n in range(here):
        sl = slice(n * LOW, (n + 1) * LOW)
        pre = dot(wt_ref[...], g_ref[:, sl], 1, 0).T + bias_ref[...]
        out_ref[sl, :] = jnp.maximum(pre, 0.0).astype(BF)
        pg_ref[sl, :] = jnp.where(pre > 0, cot_ref[sl, :].astype(F32), 0.0).astype(BF)
    store = pltpu.make_async_copy(out_ref, out_hbm, out_sem)
    store.start()
    half = flag_ref[0]
    count = depth // 2
    for ref, which in ((send_ref, 1 - half), (keep_ref, half)):
        for m in range(0, count, 288):
            step = min(288, count - m)
            at = pl.ds(pl.multiple_of(which * count + m, 16), step)
            ref[m : m + step, :] = dot(g_ref[at, :], pg_ref[...], 1, 0).astype(ref.dtype)
        ref[count:, :] = jnp.zeros((ref.shape[0] - count, c_out), ref.dtype)
    store.wait()


def backward_kernel(
    packed, flag_ref, out_ref, cot_ref, low_ref, high_ref, w_ref, here_ref, first_ref, second_ref, c_ref, acc_ref, pg_ref
):
    offsets, voxels = low_ref.shape
    depth = w_ref.shape[0]
    channels = depth // offsets
    here = voxels // LOW
    blocks = acc_ref.shape[0] // channels
    pg_ref[...] = jnp.where(out_ref[...] > 0, cot_ref[...], jnp.zeros((), BF))
    step = depth // 9
    for m in range(9):
        sl = slice(m * step, (m + 1) * step)
        c_ref[sl, :] = dot(w_ref[sl, :], pg_ref[...], 1, 1).astype(BF)
    center = offsets // 2
    for a in range(here):
        at = slice(a * channels, (a + 1) * channels)
        acc_ref[at, :] = c_ref[center * channels : (center + 1) * channels, a * LOW : (a + 1) * LOW].astype(F32)
    acc_ref[here * channels :, :] = jnp.zeros((channels * (blocks - here), LOW), F32)
    for k in range(offsets):
        if k == center:
            continue
        contrib = c_ref[k * channels : (k + 1) * channels, :]
        low, high = low_ref[k : k + 1, :], high_ref[k : k + 1, :]
        block = jnp.broadcast_to(high.astype(BF), (channels, voxels))
        parts = [jnp.where(block == jnp.array(a, BF), contrib, jnp.zeros((), BF)) for a in range(blocks)]
        acc_ref[...] += dot(jnp.concatenate(parts, 0), one_hot_low(low, voxels), 1, 1)
    if packed:
        part, per = channels // 2, LOW // 2
        for a in range(here):
            for p in range(2):
                for h in range(2):
                    at = slice(a * channels + h * part, a * channels + (h + 1) * part)
                    to = slice((2 * a + p) * part, (2 * a + p + 1) * part)
                    here_ref[to, h * per : (h + 1) * per] = acc_ref[at, p * per : (p + 1) * per]
    else:
        here_ref[...] = acc_ref[: here * channels, :]
    face = first_ref.shape[1]
    down, up = acc_ref[here * channels :, :face], acc_ref[here * channels :, face:]
    odd = flag_ref[1]
    first_ref[...] = jnp.where(odd == 1, down, up).astype(BF)
    second_ref[...] = jnp.where(odd == 1, up, down).astype(BF)


def finish_kernel(packed, flag_ref, here_ref, first_ref, second_ref, row_ref, out_ref, from_ref):
    channels, face = first_ref.shape
    blocks = here_ref.shape[0] // channels
    prev, after = sides(flag_ref[1], first_ref, second_ref)
    from_ref[:, :face] = prev
    from_ref[:, face:] = after
    part, per = channels // 2, LOW // 2
    for a in range(blocks):
        rows = lax.broadcasted_iota(jnp.int32, (LOW, 2 * face), 0) + a * LOW
        hot = jnp.where(rows == row_ref[...], 1.0, 0.0).astype(BF)
        added = dot(from_ref[...], hot, 1, 1)
        if not packed:
            at = slice(a * channels, (a + 1) * channels)
            out_ref[at, :] = (here_ref[at, :] + added).astype(BF)
            continue
        for p in range(2):
            at = slice((2 * a + p) * part, (2 * a + p + 1) * part)
            for h in range(2):
                lanes = slice(h * per, (h + 1) * per)
                term = added[h * part : (h + 1) * part, p * per : (p + 1) * per]
                out_ref[at, lanes] = (here_ref[at, lanes] + term).astype(BF)


def place_kernel(side_ref, keep_ref, came_ref, order_ref, out_ref, back_ref):
    channels, rows = out_ref.shape
    part, per = channels // 2, LOW // 2
    side = side_ref[0]
    for z in range(rows // LOW):
        at = slice(z * part, (z + 1) * part)
        for p in range(2):
            block = jnp.where(side == p, keep_ref[at, :].astype(F32), came_ref[at, :].astype(F32)).astype(BF)
            lanes = slice((2 * z + p) * per, (2 * z + p + 1) * per)
            for h in range(2):
                back_ref[h * part : (h + 1) * part, lanes] = block[:, h * per : (h + 1) * per]
    row = order_ref[...]
    block = jnp.broadcast_to(lax.shift_right_logical(row, SHIFT).astype(F32).astype(BF), (channels, rows))
    back = back_ref[...]
    parts = [jnp.where(block == jnp.array(a, BF), back, jnp.zeros((), BF)) for a in range(rows // LOW)]
    placed = dot(jnp.concatenate(parts, 0), one_hot_low((row & (LOW - 1)).astype(F32), rows), 1, 1)
    for a in range(rows // LOW):
        out_ref[:, a * LOW : (a + 1) * LOW] = placed[a * channels : (a + 1) * channels].astype(BF)


def halve_kernel(digit_ref, keep_ref, got_ref, *out_refs):
    rows = out_refs[0].shape[0]
    for d, out_ref in enumerate(out_refs):
        at = pl.ds(pl.multiple_of((digit_ref[0] ^ d) * rows, 16), rows)
        out_ref[...] = (keep_ref[at, :].astype(F32) + got_ref[at, :].astype(F32)).astype(out_ref.dtype)


def whole(count):
    return [pl.BlockSpec(memory_space=pltpu.VMEM)] * count


def send_blocks(features, order, bricks):
    channels, rows = features.shape
    hbm = pl.BlockSpec(memory_space=pltpu.HBM)
    return pl.pallas_call(
        send_kernel,
        out_shape=jax.ShapeDtypeStruct((bricks, channels, rows // bricks), BF),
        in_specs=[hbm, hbm],
        out_specs=whole(1)[0],
        scratch_shapes=[
            pltpu.VMEM((channels, rows), BF),
            pltpu.VMEM((1, rows), jnp.int32),
            pltpu.VMEM((channels * rows // LOW, LOW), BF),
            pltpu.SemaphoreType.DMA,
            pltpu.SemaphoreType.DMA,
        ],
        compiler_params=pltpu.CompilerParams(vmem_limit_bytes=ALL_LIMIT),
        cost_estimate=pl.CostEstimate(flops=2 * rows * rows * channels, bytes_accessed=1 << 19, transcendentals=0),
    )(features, order)


def forward(flags, got, first, second, low, high, w, bias, cot, padded):
    offsets, voxels = low.shape
    depth, c_out = w.shape
    rows = depth // offsets * (voxels // LOW + 1)
    macs = voxels * depth * c_out * 2 + offsets * voxels * LOW * rows
    hbm = pl.BlockSpec(memory_space=pltpu.HBM)
    return pl.pallas_call(
        forward_kernel,
        out_shape=(
            jax.ShapeDtypeStruct((voxels, c_out), BF),
            jax.ShapeDtypeStruct((padded // 2, c_out), BF),
            jax.ShapeDtypeStruct((padded // 2, c_out), BF),
        ),
        in_specs=[pl.BlockSpec(memory_space=pltpu.SMEM)] + whole(5) + [hbm] + whole(1) + [hbm],
        out_specs=(hbm,) + tuple(whole(2)),
        scratch_shapes=[
            pltpu.VMEM((depth, voxels), BF),
            pltpu.VMEM((rows, LOW), BF),
            pltpu.VMEM((c_out, depth), BF),
            pltpu.VMEM((depth, c_out), BF),
            pltpu.VMEM((voxels, c_out), BF),
            pltpu.VMEM((voxels, c_out), BF),
            pltpu.VMEM((voxels, c_out), BF),
            pltpu.SemaphoreType.DMA,
            pltpu.SemaphoreType.DMA,
            pltpu.SemaphoreType.DMA,
        ],
        compiler_params=pltpu.CompilerParams(vmem_limit_bytes=FULL_LIMIT),
        cost_estimate=pl.CostEstimate(flops=2 * macs, bytes_accessed=5 << 20, transcendentals=0),
    )(flags, got, first, second, low, high, w, bias, cot)


def backward(packed, flags, out, cot, low, high, w, face):
    offsets, voxels = low.shape
    depth, c_out = w.shape
    channels = depth // offsets
    rows = channels * (voxels // LOW + 1)
    macs = voxels * depth * c_out + offsets * voxels * LOW * rows
    return pl.pallas_call(
        functools.partial(backward_kernel, packed),
        out_shape=(
            jax.ShapeDtypeStruct((voxels // LOW * channels, LOW), F32),
            jax.ShapeDtypeStruct((channels, face), BF),
            jax.ShapeDtypeStruct((channels, face), BF),
        ),
        in_specs=[pl.BlockSpec(memory_space=pltpu.SMEM)] + whole(5),
        out_specs=tuple(whole(3)),
        scratch_shapes=[
            pltpu.VMEM((depth, voxels), BF),
            pltpu.VMEM((rows, LOW), F32),
            pltpu.VMEM((voxels, c_out), BF),
        ],
        compiler_params=pltpu.CompilerParams(vmem_limit_bytes=VMEM_LIMIT),
        cost_estimate=pl.CostEstimate(flops=2 * macs, bytes_accessed=3 << 20, transcendentals=0),
    )(flags, out, cot, low, high, w)


def finish(packed, flags, here, first, second, face_rows):
    rows, _ = here.shape
    channels, face = first.shape
    return pl.pallas_call(
        functools.partial(finish_kernel, packed),
        out_shape=jax.ShapeDtypeStruct((rows, LOW), BF),
        in_specs=[pl.BlockSpec(memory_space=pltpu.SMEM)] + whole(4),
        out_specs=whole(1)[0],
        scratch_shapes=[pltpu.VMEM((channels, 2 * face), BF)],
        compiler_params=pltpu.CompilerParams(vmem_limit_bytes=SMALL_LIMIT),
        cost_estimate=pl.CostEstimate(flops=4 * rows * LOW * face, bytes_accessed=1 << 20, transcendentals=0),
    )(flags, here, first, second, face_rows)


def place(side, keep, came, order, channels):
    rows = order.shape[1]
    return pl.pallas_call(
        place_kernel,
        out_shape=jax.ShapeDtypeStruct((channels, rows), BF),
        in_specs=[pl.BlockSpec(memory_space=pltpu.SMEM)] + whole(3),
        out_specs=whole(1)[0],
        scratch_shapes=[pltpu.VMEM((channels, rows), BF)],
        compiler_params=pltpu.CompilerParams(vmem_limit_bytes=SMALL_LIMIT),
        cost_estimate=pl.CostEstimate(flops=2 * rows * rows * channels, bytes_accessed=1 << 20, transcendentals=0),
    )(side, keep, came, order)


def halve(digit, keep, got, radix):
    rows, width = keep.shape
    shapes = [jax.ShapeDtypeStruct((rows // radix, width), F32 if d == 0 else BF) for d in range(radix)]
    return pl.pallas_call(
        halve_kernel,
        out_shape=tuple(shapes),
        in_specs=[pl.BlockSpec(memory_space=pltpu.SMEM)] + whole(2),
        out_specs=tuple(whole(radix)),
        compiler_params=pltpu.CompilerParams(vmem_limit_bytes=SMALL_LIMIT),
        cost_estimate=pl.CostEstimate(flops=rows * width, bytes_accessed=7 * rows * width, transcendentals=0),
    )(digit, keep, got)


def stages(count):
    plan, stride = [], 1
    while stride < count:
        left = count // stride
        radix = 4 if stride > 1 and left % 4 == 0 else 2
        if left % radix:
            radix = left
        plan.append((stride, radix))
        stride *= radix
    return plan


def swapped(array, count, stride, radix, delta):
    def partner(i):
        digit = i // stride % radix
        other = (digit ^ delta) if radix in (2, 4) else (delta - digit) % radix
        return i + (other - digit) * stride

    return lax.ppermute(array, AXES, [(i, partner(i)) for i in range(count)])


def other_digit(digit, delta, radix):
    return (digit ^ delta) if radix in (2, 4) else (delta - digit) % radix


def reduce_stage(x, flat, count, stride, radix):
    digit = flat // stride % radix
    pieces = x.reshape((radix, x.shape[0] // radix) + x.shape[1:])
    total = None
    for delta in range(radix):
        piece = lax.dynamic_index_in_dim(pieces, other_digit(digit, delta, radix), 0, keepdims=False)
        if radix not in (2, 4) or delta:
            piece = swapped(piece, count, stride, radix, delta)
        total = piece.astype(F32) if total is None else total + piece.astype(F32)
    return total.astype(BF)


def by_digit(got, digit, radix):
    parts = []
    for place in range(radix):
        part = got[0]
        for d in range(radix):
            where = (place ^ d) if radix in (2, 4) else (place + d) % radix
            part = jnp.where(digit == d, got[where], part)
        parts.append(part)
    return parts


def joined(parts):
    return parts[0] if len(parts) == 1 else jnp.concatenate(parts, 0)


def gather_stage(parts, flat, count, stride, radix, cargo=lambda delta: None):
    digit = flat // stride % radix
    rows = sum(part.shape[0] for part in parts)
    got, brought = [], {}
    for d in range(radix):
        if radix in (2, 4) and d == 0:
            got.append(joined(parts))
            continue
        extra = cargo(d)
        piece = swapped(joined(parts if extra is None else parts + [extra]), count, stride, radix, d)
        got.append(piece[:rows])
        brought[d] = piece[rows:]
    return by_digit(got, digit, radix), brought


def meet(first, second):
    size = lax.axis_size("brick")
    got = []
    for start, array in ((0, first), (1, second)):
        pairs = []
        for i in range(start, size - 1, 2):
            pairs += [(i, i + 1), (i + 1, i)]
        got.append(lax.ppermute(array, "brick", pairs))
    return got


def on_device(features, order, face_list, face_count, kernel_map, weight, bias, cotangent):
    offsets, channels, c_out = weight.shape
    rows = features.shape[0]
    face = face_list.shape[0] // 2
    bricks = lax.axis_size("brick")
    count = bricks * lax.axis_size("group")
    per = rows // bricks
    depth = offsets * channels
    unit = 8 * count
    padded = -(-depth // unit) * unit

    w = weight.reshape(depth, c_out)
    flat = lax.axis_index("brick") * lax.axis_size("group") + lax.axis_index("group")
    send = send_blocks(features.T, order[None], bricks)
    got = lax.all_to_all(send, "brick", split_axis=0, concat_axis=0)

    slots = jnp.arange(2 * face, dtype=jnp.int32)
    live = jnp.where(slots < face, slots < face_count[0], slots - face < face_count[1])
    face_rows = jnp.where(live, face_list, -1)
    pick = one_hot_rows(face_rows, rows)
    pick, got = lax.optimization_barrier((pick, got))
    local = got.transpose(1, 0, 2).reshape(channels, rows)
    shown = dot(local, pick, 1, 1).astype(BF)
    odd = lax.axis_index("brick") % 2
    down, up = shown[:, :face], shown[:, face:]
    first, second = meet(jnp.where(odd == 1, down, up), jnp.where(odd == 1, up, down))

    flags = jnp.stack([flat % 2, odd]).astype(jnp.int32)
    low = (kernel_map & (LOW - 1)).astype(F32)
    high = lax.shift_right_logical(kernel_map, SHIFT).astype(F32)
    output, give, keep = forward(flags, got, first, second, low, high, w, bias[None], cotangent, padded)
    packed = (bricks, count) == (8, 32) and per * 2 == LOW and channels % 16 == 0
    plan = stages(count)[1:]
    taken = swapped(give, count, 1, 2, 1)
    if plan[0][1] == 4 and padded % 128 == 0:
        stride, radix = plan[0]
        pieces = halve((flat // stride % radix).astype(jnp.int32)[None], keep, taken, radix)
        total = pieces[0]
        for d in range(1, radix):
            total = total + swapped(pieces[d], count, stride, radix, d).astype(F32)
        total = total.astype(BF)
    else:
        total = (keep.astype(F32) + taken.astype(F32)).astype(BF)
        total = reduce_stage(total, flat, count, *plan[0])
    here, first, second = backward(packed, flags, output, cotangent, low, high, w, face)
    total, first, second = lax.optimization_barrier((total, first, second))
    first, second = meet(first, second)
    for stride, radix in plan[1:]:
        total = reduce_stage(total, flat, count, stride, radix)

    local_grad = finish(packed, flags, here, first, second, face_rows[None])
    if packed:
        part = channels // 2
        total, local_grad = lax.optimization_barrier((total, local_grad))
        local_grad = local_grad.reshape(bricks // 2, channels, LOW)
        z, x = flat // 8, flat // 4 % 2
        cargo = lambda d: lax.dynamic_index_in_dim(local_grad, z ^ d, 0, keepdims=False)
        parts, brought = gather_stage([total], flat, count, 8, 4, cargo)
        mine = jnp.stack(by_digit([cargo(0)] + [brought[d] for d in (1, 2, 3)], z, 4))
        mine = mine.reshape(bricks // 2, 2, part, LOW)
        give = jnp.where(x == 0, mine[:, 1], mine[:, 0]).reshape(-1, LOW)
        keep = jnp.where(x == 0, mine[:, 0], mine[:, 1]).reshape(-1, LOW)
        parts, brought = gather_stage(parts, flat, count, 2, 4, lambda d: give if d == 2 else None)
        came = brought[2]
    else:
        blocks = rows // LOW
        send = local_grad.reshape(blocks, channels, LOW // per, per).transpose(0, 2, 1, 3)
        came = lax.all_to_all(send.reshape(bricks, channels, per), "brick", split_axis=0, concat_axis=0)
        parts = [total]
        for stride, radix in reversed(plan):
            parts, _ = gather_stage(parts, flat, count, stride, radix)
    total = joined(parts)
    total, came = lax.optimization_barrier((total, came))
    if packed:
        grad_in = place(x.astype(jnp.int32)[None], keep, came, order[None], channels).T
    else:
        returned = came.transpose(1, 0, 2).reshape(channels, rows)
        grad_in = dot(returned, one_hot_rows(order, rows), 1, 0).astype(BF).T
    other = swapped(total, count, 1, 2, 1)
    low = jnp.where(flat % 2 == 0, total, other)[: depth // 2]
    high = jnp.where(flat % 2 == 0, other, total)[: depth // 2]
    scale = jnp.float32(1.0 / math.sqrt(count * rows))
    weight_grad = (jnp.concatenate([low, high], 0).astype(F32) * scale).reshape(offsets, channels, c_out)
    return output, grad_in, weight_grad


def solution(mesh):
    return jax.shard_map(
        on_device,
        mesh=mesh,
        in_specs=(
            P(AXES, None),
            P(AXES),
            P(AXES),
            P(AXES),
            P(None, AXES),
            P(),
            P(),
            P(AXES, None),
        ),
        out_specs=(P(AXES, None), P(AXES, None), P()),
        check_vma=False,
    )
```

```python
import functools
import math

import jax
import jax.numpy as jnp
from jax import lax
from jax.experimental import pallas as pl
from jax.experimental.pallas import tpu as pltpu
from jax.sharding import PartitionSpec as P

BF = jnp.bfloat16
F32 = jnp.float32
LOW = 256
SHIFT = 8
VMEM_LIMIT = 52 << 20
SMALL_LIMIT = 6 << 20
FULL_LIMIT = 51 << 20
ALL_LIMIT = 60 << 20
AXES = ("brick", "group")


def dot(a, b, a_dim, b_dim):
    dims = (((a_dim,), (b_dim,)), ((), ()))
    return lax.dot_general(a, b, dims, preferred_element_type=F32)


def one_hot_rows(index, width):
    columns = jnp.arange(width, dtype=jnp.int32)
    return (index[:, None] == columns[None, :]).astype(BF)


def one_hot_low(low, lanes):
    iota = lax.broadcasted_iota(jnp.int32, (LOW, lanes), 0).astype(BF)
    hit = iota == jnp.broadcast_to(low.astype(BF), (LOW, lanes))
    return jnp.where(hit, jnp.ones((), BF), jnp.zeros((), BF))


def send_kernel(feat_hbm, order_hbm, out_ref, feat_ref, order_ref, x_ref, feat_sem, order_sem):
    fetch_feat = pltpu.make_async_copy(feat_hbm, feat_ref, feat_sem)
    fetch_feat.start()
    fetch_order = pltpu.make_async_copy(order_hbm, order_ref, order_sem)
    fetch_order.start()
    channels, rows = feat_ref.shape
    per = out_ref.shape[2]
    fetch_feat.wait()
    fetch_order.wait()
    for a in range(rows // LOW):
        x_ref[a * channels : (a + 1) * channels, :] = feat_ref[:, a * LOW : (a + 1) * LOW]
    for n in range(rows // LOW):
        row = order_ref[:, n * LOW : (n + 1) * LOW]
        terms = dot(x_ref[...], one_hot_low((row & (LOW - 1)).astype(F32), LOW), 1, 0)
        block = jnp.broadcast_to(lax.shift_right_logical(row, SHIFT), (channels, LOW))
        picked = terms[:channels]
        for a in range(1, rows // LOW):
            picked = jnp.where(block == a, terms[a * channels : (a + 1) * channels], picked)
        picked = picked.astype(BF)
        for p in range(LOW // per):
            out_ref[n * (LOW // per) + p] = picked[:, p * per : (p + 1) * per]


def sides(odd, first_ref, second_ref):
    first, second = first_ref[...].astype(F32), second_ref[...].astype(F32)
    low = jnp.where(odd == 1, first, second)
    high = jnp.where(odd == 1, second, first)
    return low.astype(BF), high.astype(BF)


def forward_kernel(
    flag_ref, got_ref, even_ref, odd_ref, low_ref, high_ref, w_hbm, bias_ref, cot_hbm, out_hbm, send_ref, keep_ref,
    g_ref, x_ref, wt_ref, w_ref, cot_ref, out_ref, pg_ref, w_sem, cot_sem, out_sem,
):
    fetch_w = pltpu.make_async_copy(w_hbm, w_ref, w_sem)
    fetch_w.start()
    fetch_cot = pltpu.make_async_copy(cot_hbm, cot_ref, cot_sem)
    fetch_cot.start()
    offsets, voxels = low_ref.shape
    depth, c_out = w_ref.shape
    channels = depth // offsets
    here = voxels // LOW
    blocks = x_ref.shape[0] // channels
    center = offsets // 2
    per = got_ref.shape[2]
    for a in range(here):
        for p in range(LOW // per):
            x_ref[a * channels : (a + 1) * channels, p * per : (p + 1) * per] = got_ref[a * (LOW // per) + p]
    face = even_ref.shape[1]
    prev, after = sides(flag_ref[1], even_ref, odd_ref)
    x_ref[here * channels :, :face] = prev
    x_ref[here * channels :, face:] = after
    ready = offsets // 3
    for k in range(offsets):
        if k == ready:
            fetch_w.wait()
            fetch_cot.wait()
        for j in range(2 * (k - ready), min(2 * (k - ready + 1), offsets)) if k >= ready else ():
            wt_ref[:, j * channels : (j + 1) * channels] = w_ref[j * channels : (j + 1) * channels, :].T
        at = slice(k * channels, (k + 1) * channels)
        if k == center:
            for a in range(here):
                g_ref[at, a * LOW : (a + 1) * LOW] = x_ref[a * channels : (a + 1) * channels, :]
            continue
        low, high = low_ref[k : k + 1, :], high_ref[k : k + 1, :]
        for n in range(here):
            sl = slice(n * LOW, (n + 1) * LOW)
            terms = dot(x_ref[...], one_hot_low(low[:, sl], LOW), 1, 0)
            block = jnp.broadcast_to(high[:, sl], (channels, LOW))
            picked = jnp.zeros((channels, LOW), F32)
            for a in range(blocks):
                picked = jnp.where(block == a, terms[a * channels : (a + 1) * channels], picked)
            g_ref[at, sl] = picked.astype(BF)
    for n in range(here):
        sl = slice(n * LOW, (n + 1) * LOW)
        pre = dot(wt_ref[...], g_ref[:, sl], 1, 0).T + bias_ref[...]
        out_ref[sl, :] = jnp.maximum(pre, 0.0).astype(BF)
        pg_ref[sl, :] = jnp.where(pre > 0, cot_ref[sl, :].astype(F32), 0.0).astype(BF)
    store = pltpu.make_async_copy(out_ref, out_hbm, out_sem)
    store.start()
    half = flag_ref[0]
    count = depth // 2
    for ref, which in ((send_ref, 1 - half), (keep_ref, half)):
        for m in range(0, count, 288):
            step = min(288, count - m)
            at = pl.ds(pl.multiple_of(which * count + m, 16), step)
            ref[m : m + step, :] = dot(g_ref[at, :], pg_ref[...], 1, 0).astype(ref.dtype)
        ref[count:, :] = jnp.zeros((ref.shape[0] - count, c_out), ref.dtype)
    store.wait()


def backward_kernel(
    packed, flag_ref, out_ref, cot_ref, low_ref, high_ref, w_ref, here_ref, first_ref, second_ref, c_ref, acc_ref, pg_ref
):
    offsets, voxels = low_ref.shape
    depth = w_ref.shape[0]
    channels = depth // offsets
    here = voxels // LOW
    blocks = acc_ref.shape[0] // channels
    pg_ref[...] = jnp.where(out_ref[...] > 0, cot_ref[...], jnp.zeros((), BF))
    step = depth // 9
    for m in range(9):
        sl = slice(m * step, (m + 1) * step)
        c_ref[sl, :] = dot(w_ref[sl, :], pg_ref[...], 1, 1).astype(BF)
    center = offsets // 2
    for a in range(here):
        at = slice(a * channels, (a + 1) * channels)
        acc_ref[at, :] = c_ref[center * channels : (center + 1) * channels, a * LOW : (a + 1) * LOW].astype(F32)
    acc_ref[here * channels :, :] = jnp.zeros((channels * (blocks - here), LOW), F32)
    for k in range(offsets):
        if k == center:
            continue
        contrib = c_ref[k * channels : (k + 1) * channels, :]
        low, high = low_ref[k : k + 1, :], high_ref[k : k + 1, :]
        block = jnp.broadcast_to(high.astype(BF), (channels, voxels))
        parts = [jnp.where(block == jnp.array(a, BF), contrib, jnp.zeros((), BF)) for a in range(blocks)]
        acc_ref[...] += dot(jnp.concatenate(parts, 0), one_hot_low(low, voxels), 1, 1)
    if packed:
        part, per = channels // 2, LOW // 2
        for a in range(here):
            for p in range(2):
                for h in range(2):
                    at = slice(a * channels + h * part, a * channels + (h + 1) * part)
                    to = slice((2 * a + p) * part, (2 * a + p + 1) * part)
                    here_ref[to, h * per : (h + 1) * per] = acc_ref[at, p * per : (p + 1) * per]
    else:
        here_ref[...] = acc_ref[: here * channels, :]
    face = first_ref.shape[1]
    down, up = acc_ref[here * channels :, :face], acc_ref[here * channels :, face:]
    odd = flag_ref[1]
    first_ref[...] = jnp.where(odd == 1, down, up).astype(BF)
    second_ref[...] = jnp.where(odd == 1, up, down).astype(BF)


def finish_kernel(packed, flag_ref, here_ref, first_ref, second_ref, row_ref, out_ref, from_ref):
    channels, face = first_ref.shape
    blocks = here_ref.shape[0] // channels
    prev, after = sides(flag_ref[1], first_ref, second_ref)
    from_ref[:, :face] = prev
    from_ref[:, face:] = after
    part, per = channels // 2, LOW // 2
    for a in range(blocks):
        rows = lax.broadcasted_iota(jnp.int32, (LOW, 2 * face), 0) + a * LOW
        hot = jnp.where(rows == row_ref[...], 1.0, 0.0).astype(BF)
        added = dot(from_ref[...], hot, 1, 1)
        if not packed:
            at = slice(a * channels, (a + 1) * channels)
            out_ref[at, :] = (here_ref[at, :] + added).astype(BF)
            continue
        for p in range(2):
            at = slice((2 * a + p) * part, (2 * a + p + 1) * part)
            for h in range(2):
                lanes = slice(h * per, (h + 1) * per)
                term = added[h * part : (h + 1) * part, p * per : (p + 1) * per]
                out_ref[at, lanes] = (here_ref[at, lanes] + term).astype(BF)


def place_kernel(side_ref, keep_ref, came_ref, order_ref, out_ref, back_ref):
    channels, rows = out_ref.shape
    part, per = channels // 2, LOW // 2
    side = side_ref[0]
    for z in range(rows // LOW):
        at = slice(z * part, (z + 1) * part)
        for p in range(2):
            block = jnp.where(side == p, keep_ref[at, :].astype(F32), came_ref[at, :].astype(F32)).astype(BF)
            lanes = slice((2 * z + p) * per, (2 * z + p + 1) * per)
            for h in range(2):
                back_ref[h * part : (h + 1) * part, lanes] = block[:, h * per : (h + 1) * per]
    row = order_ref[...]
    block = jnp.broadcast_to(lax.shift_right_logical(row, SHIFT).astype(F32).astype(BF), (channels, rows))
    back = back_ref[...]
    parts = [jnp.where(block == jnp.array(a, BF), back, jnp.zeros((), BF)) for a in range(rows // LOW)]
    placed = dot(jnp.concatenate(parts, 0), one_hot_low((row & (LOW - 1)).astype(F32), rows), 1, 1)
    for a in range(rows // LOW):
        out_ref[:, a * LOW : (a + 1) * LOW] = placed[a * channels : (a + 1) * channels].astype(BF)


def halve_kernel(digit_ref, keep_ref, got_ref, *out_refs):
    rows = out_refs[0].shape[0]
    for d, out_ref in enumerate(out_refs):
        at = pl.ds(pl.multiple_of((digit_ref[0] ^ d) * rows, 16), rows)
        out_ref[...] = (keep_ref[at, :].astype(F32) + got_ref[at, :].astype(F32)).astype(out_ref.dtype)


def whole(count):
    return [pl.BlockSpec(memory_space=pltpu.VMEM)] * count


def send_blocks(features, order, bricks):
    channels, rows = features.shape
    hbm = pl.BlockSpec(memory_space=pltpu.HBM)
    return pl.pallas_call(
        send_kernel,
        out_shape=jax.ShapeDtypeStruct((bricks, channels, rows // bricks), BF),
        in_specs=[hbm, hbm],
        out_specs=whole(1)[0],
        scratch_shapes=[
            pltpu.VMEM((channels, rows), BF),
            pltpu.VMEM((1, rows), jnp.int32),
            pltpu.VMEM((channels * rows // LOW, LOW), BF),
            pltpu.SemaphoreType.DMA,
            pltpu.SemaphoreType.DMA,
        ],
        compiler_params=pltpu.CompilerParams(vmem_limit_bytes=ALL_LIMIT),
        cost_estimate=pl.CostEstimate(flops=2 * rows * rows * channels, bytes_accessed=1 << 19, transcendentals=0),
    )(features, order)


def forward(flags, got, first, second, low, high, w, bias, cot, padded):
    offsets, voxels = low.shape
    depth, c_out = w.shape
    rows = depth // offsets * (voxels // LOW + 1)
    macs = voxels * depth * c_out * 2 + offsets * voxels * LOW * rows
    hbm = pl.BlockSpec(memory_space=pltpu.HBM)
    return pl.pallas_call(
        forward_kernel,
        out_shape=(
            jax.ShapeDtypeStruct((voxels, c_out), BF),
            jax.ShapeDtypeStruct((padded // 2, c_out), BF),
            jax.ShapeDtypeStruct((padded // 2, c_out), BF),
        ),
        in_specs=[pl.BlockSpec(memory_space=pltpu.SMEM)] + whole(5) + [hbm] + whole(1) + [hbm],
        out_specs=(hbm,) + tuple(whole(2)),
        scratch_shapes=[
            pltpu.VMEM((depth, voxels), BF),
            pltpu.VMEM((rows, LOW), BF),
            pltpu.VMEM((c_out, depth), BF),
            pltpu.VMEM((depth, c_out), BF),
            pltpu.VMEM((voxels, c_out), BF),
            pltpu.VMEM((voxels, c_out), BF),
            pltpu.VMEM((voxels, c_out), BF),
            pltpu.SemaphoreType.DMA,
            pltpu.SemaphoreType.DMA,
            pltpu.SemaphoreType.DMA,
        ],
        compiler_params=pltpu.CompilerParams(vmem_limit_bytes=FULL_LIMIT),
        cost_estimate=pl.CostEstimate(flops=2 * macs, bytes_accessed=5 << 20, transcendentals=0),
    )(flags, got, first, second, low, high, w, bias, cot)


def backward(packed, flags, out, cot, low, high, w, face):
    offsets, voxels = low.shape
    depth, c_out = w.shape
    channels = depth // offsets
    rows = channels * (voxels // LOW + 1)
    macs = voxels * depth * c_out + offsets * voxels * LOW * rows
    return pl.pallas_call(
        functools.partial(backward_kernel, packed),
        out_shape=(
            jax.ShapeDtypeStruct((voxels // LOW * channels, LOW), F32),
            jax.ShapeDtypeStruct((channels, face), BF),
            jax.ShapeDtypeStruct((channels, face), BF),
        ),
        in_specs=[pl.BlockSpec(memory_space=pltpu.SMEM)] + whole(5),
        out_specs=tuple(whole(3)),
        scratch_shapes=[
            pltpu.VMEM((depth, voxels), BF),
            pltpu.VMEM((rows, LOW), F32),
            pltpu.VMEM((voxels, c_out), BF),
        ],
        compiler_params=pltpu.CompilerParams(vmem_limit_bytes=VMEM_LIMIT),
        cost_estimate=pl.CostEstimate(flops=2 * macs, bytes_accessed=3 << 20, transcendentals=0),
    )(flags, out, cot, low, high, w)


def finish(packed, flags, here, first, second, face_rows):
    rows, _ = here.shape
    channels, face = first.shape
    return pl.pallas_call(
        functools.partial(finish_kernel, packed),
        out_shape=jax.ShapeDtypeStruct((rows, LOW), BF),
        in_specs=[pl.BlockSpec(memory_space=pltpu.SMEM)] + whole(4),
        out_specs=whole(1)[0],
        scratch_shapes=[pltpu.VMEM((channels, 2 * face), BF)],
        compiler_params=pltpu.CompilerParams(vmem_limit_bytes=SMALL_LIMIT),
        cost_estimate=pl.CostEstimate(flops=4 * rows * LOW * face, bytes_accessed=1 << 20, transcendentals=0),
    )(flags, here, first, second, face_rows)


def place(side, keep, came, order, channels):
    rows = order.shape[1]
    return pl.pallas_call(
        place_kernel,
        out_shape=jax.ShapeDtypeStruct((channels, rows), BF),
        in_specs=[pl.BlockSpec(memory_space=pltpu.SMEM)] + whole(3),
        out_specs=whole(1)[0],
        scratch_shapes=[pltpu.VMEM((channels, rows), BF)],
        compiler_params=pltpu.CompilerParams(vmem_limit_bytes=SMALL_LIMIT),
        cost_estimate=pl.CostEstimate(flops=2 * rows * rows * channels, bytes_accessed=1 << 20, transcendentals=0),
    )(side, keep, came, order)


def halve(digit, keep, got, radix):
    rows, width = keep.shape
    shapes = [jax.ShapeDtypeStruct((rows // radix, width), F32 if d == 0 else BF) for d in range(radix)]
    return pl.pallas_call(
        halve_kernel,
        out_shape=tuple(shapes),
        in_specs=[pl.BlockSpec(memory_space=pltpu.SMEM)] + whole(2),
        out_specs=tuple(whole(radix)),
        compiler_params=pltpu.CompilerParams(vmem_limit_bytes=SMALL_LIMIT),
        cost_estimate=pl.CostEstimate(flops=rows * width, bytes_accessed=7 * rows * width, transcendentals=0),
    )(digit, keep, got)


def stages(count):
    plan, stride = [], 1
    while stride < count:
        left = count // stride
        radix = 4 if stride > 1 and left % 4 == 0 else 2
        if left % radix:
            radix = left
        plan.append((stride, radix))
        stride *= radix
    return plan


def swapped(array, count, stride, radix, delta):
    def partner(i):
        digit = i // stride % radix
        other = (digit ^ delta) if radix in (2, 4) else (delta - digit) % radix
        return i + (other - digit) * stride

    return lax.ppermute(array, AXES, [(i, partner(i)) for i in range(count)])


def other_digit(digit, delta, radix):
    return (digit ^ delta) if radix in (2, 4) else (delta - digit) % radix


def reduce_stage(x, flat, count, stride, radix):
    digit = flat // stride % radix
    pieces = x.reshape((radix, x.shape[0] // radix) + x.shape[1:])
    total = None
    for delta in range(radix):
        piece = lax.dynamic_index_in_dim(pieces, other_digit(digit, delta, radix), 0, keepdims=False)
        if radix not in (2, 4) or delta:
            piece = swapped(piece, count, stride, radix, delta)
        total = piece.astype(F32) if total is None else total + piece.astype(F32)
    return total.astype(BF)


def by_digit(got, digit, radix):
    parts = []
    for place in range(radix):
        part = got[0]
        for d in range(radix):
            where = (place ^ d) if radix in (2, 4) else (place + d) % radix
            part = jnp.where(digit == d, got[where], part)
        parts.append(part)
    return parts


def joined(parts):
    return parts[0] if len(parts) == 1 else jnp.concatenate(parts, 0)


def gather_stage(parts, flat, count, stride, radix, cargo=lambda delta: None):
    digit = flat // stride % radix
    rows = sum(part.shape[0] for part in parts)
    got, brought = [], {}
    for d in range(radix):
        if radix in (2, 4) and d == 0:
            got.append(joined(parts))
            continue
        extra = cargo(d)
        piece = swapped(joined(parts if extra is None else parts + [extra]), count, stride, radix, d)
        got.append(piece[:rows])
        brought[d] = piece[rows:]
    return by_digit(got, digit, radix), brought


def meet(first, second):
    size = lax.axis_size("brick")
    got = []
    for start, array in ((0, first), (1, second)):
        pairs = []
        for i in range(start, size - 1, 2):
            pairs += [(i, i + 1), (i + 1, i)]
        got.append(lax.ppermute(array, "brick", pairs))
    return got


def on_device(features, order, face_list, face_count, kernel_map, weight, bias, cotangent):
    offsets, channels, c_out = weight.shape
    rows = features.shape[0]
    face = face_list.shape[0] // 2
    bricks = lax.axis_size("brick")
    count = bricks * lax.axis_size("group")
    per = rows // bricks
    depth = offsets * channels
    unit = 8 * count
    padded = -(-depth // unit) * unit

    w = weight.reshape(depth, c_out)
    flat = lax.axis_index("brick") * lax.axis_size("group") + lax.axis_index("group")
    send = send_blocks(features.T, order[None], bricks)
    got = lax.all_to_all(send, "brick", split_axis=0, concat_axis=0)

    slots = jnp.arange(2 * face, dtype=jnp.int32)
    live = jnp.where(slots < face, slots < face_count[0], slots - face < face_count[1])
    face_rows = jnp.where(live, face_list, -1)
    pick = one_hot_rows(face_rows, rows)
    pick, got = lax.optimization_barrier((pick, got))
    local = got.transpose(1, 0, 2).reshape(channels, rows)
    shown = dot(local, pick, 1, 1).astype(BF)
    odd = lax.axis_index("brick") % 2
    down, up = shown[:, :face], shown[:, face:]
    first, second = meet(jnp.where(odd == 1, down, up), jnp.where(odd == 1, up, down))

    flags = jnp.stack([flat % 2, odd]).astype(jnp.int32)
    low = (kernel_map & (LOW - 1)).astype(F32)
    high = lax.shift_right_logical(kernel_map, SHIFT).astype(F32)
    output, give, keep = forward(flags, got, first, second, low, high, w, bias[None], cotangent, padded)
    packed = (bricks, count) == (8, 32) and per * 2 == LOW and channels % 16 == 0
    plan = stages(count)[1:]
    taken = swapped(give, count, 1, 2, 1)
    if plan[0][1] == 4 and padded % 128 == 0:
        stride, radix = plan[0]
        pieces = halve((flat // stride % radix).astype(jnp.int32)[None], keep, taken, radix)
        total = pieces[0]
        for d in range(1, radix):
            total = total + swapped(pieces[d], count, stride, radix, d).astype(F32)
        total = total.astype(BF)
    else:
        total = (keep.astype(F32) + taken.astype(F32)).astype(BF)
        total = reduce_stage(total, flat, count, *plan[0])
    here, first, second = backward(packed, flags, output, cotangent, low, high, w, face)
    total, first, second = lax.optimization_barrier((total, first, second))
    first, second = meet(first, second)
    for stride, radix in plan[1:]:
        total = reduce_stage(total, flat, count, stride, radix)

    local_grad = finish(packed, flags, here, first, second, face_rows[None])
    if packed:
        part = channels // 2
        total, local_grad = lax.optimization_barrier((total, local_grad))
        local_grad = local_grad.reshape(bricks // 2, channels, LOW)
        z, x = flat // 8, flat // 4 % 2
        cargo = lambda d: lax.dynamic_index_in_dim(local_grad, z ^ d, 0, keepdims=False)
        parts, brought = gather_stage([total], flat, count, 8, 4, cargo)
        mine = jnp.stack(by_digit([cargo(0)] + [brought[d] for d in (1, 2, 3)], z, 4))
        mine = mine.reshape(bricks // 2, 2, part, LOW)
        give = jnp.where(x == 0, mine[:, 1], mine[:, 0]).reshape(-1, LOW)
        keep = jnp.where(x == 0, mine[:, 0], mine[:, 1]).reshape(-1, LOW)
        parts, brought = gather_stage(parts, flat, count, 2, 4, lambda d: give if d == 2 else None)
        came = brought[2]
    else:
        blocks = rows // LOW
        send = local_grad.reshape(blocks, channels, LOW // per, per).transpose(0, 2, 1, 3)
        came = lax.all_to_all(send.reshape(bricks, channels, per), "brick", split_axis=0, concat_axis=0)
        parts = [total]
        for stride, radix in reversed(plan):
            parts, _ = gather_stage(parts, flat, count, stride, radix)
    total = joined(parts)
    total, came = lax.optimization_barrier((total, came))
    if packed:
        grad_in = place(x.astype(jnp.int32)[None], keep, came, order[None], channels).T
    else:
        returned = came.transpose(1, 0, 2).reshape(channels, rows)
        grad_in = dot(returned, one_hot_rows(order, rows), 1, 0).astype(BF).T
    other = swapped(total, count, 1, 2, 1)
    low = jnp.where(flat % 2 == 0, total, other)[: depth // 2]
    high = jnp.where(flat % 2 == 0, other, total)[: depth // 2]
    scale = jnp.float32(1.0 / math.sqrt(count * rows))
    weight_grad = (jnp.concatenate([low, high], 0).astype(F32) * scale).reshape(offsets, channels, c_out)
    return output, grad_in, weight_grad


def solution(mesh):
    return jax.shard_map(
        on_device,
        mesh=mesh,
        in_specs=(
            P(AXES, None),
            P(AXES),
            P(AXES),
            P(AXES),
            P(None, AXES),
            P(),
            P(),
            P(AXES, None),
        ),
        out_specs=(P(AXES, None), P(AXES, None), P()),
        check_vma=False,
    )
```
